512 devices in a mesh: src: 32 (over z, core), tgt: 16 (over y, x).
Axes of the slice: x: 4, y: 4, z: 16, core: 2. Of those that a mesh axis runs over, the one named last changes fastest.
Arguments:
- source: bfloat16 [65536, 1024], P(('src', 'tgt')), may hold values from -16 to 16
- target: bfloat16 [65536, 1024], P(('src', 'tgt')), may hold values from -16 to 16
- src_bucket: int32 [65536], P(('src', 'tgt')), may hold values from 0 to 4095, as said below
- tgt_bucket: int32 [65536], P(('src', 'tgt')), may hold values from 0 to 4095, as said below
- band: int32 [65536], P(('src', 'tgt')), may hold values from 1 to 8, as said below
- route: int32 [65536], P(('src', 'tgt')), may hold values from 0 to 65535, as said below
Outputs:
- src_read: float32 [65536, 1024], P(('src', 'tgt'))
- tgt_read: float32 [65536, 1024], P(('src', 'tgt'))
The draws below stay inside these ranges and needn't reach their ends.
Inputs may be any that keep to these rules, and one draw needn't show every extreme that they name: `route`: A permutation. Each device's 128 sources go to positions in blocks of devices with the same index along tgt, exactly 4 to each index along src; those from src index s land at offsets s * 4 to (s + 1) * 4 - 1 of the receiving block. `src_bucket`: A source placed by route in the block of device (g, t) has a bucket from g * 128 + t * 8 to g * 128 + (t + 1) * 8 - 1, and each of these 8 buckets occurs among the sources placed in that block. `tgt_bucket`: A target in the block of device (g, t) has a bucket from g * 128 + t * 8 to g * 128 + (t + 1) * 8 - 1, and each of these 8 buckets occurs among that block's targets. Every block of bucket-ordered sources holds a source with band 8.
All inputs are finite; a program needn't handle non-finite values.
Results may differ from the reference program's by a relative error of at most 0.0014.
Values may be sent and summed in bfloat16 or wider, within the bound.
A program may use at most 64 MiB of HBM per device.

```python
import math
import jax
import jax.numpy as jnp
from jax import lax

D = 1024
ROWS = 128
BPD = 8
BANDMAX = 8
BPG = 128
SPAN = 4
GROUP_ROWS = 2048
SENTENCES = 65536


def block_layout():
    blocks = SENTENCES // ROWS
    tgt_count = GROUP_ROWS // ROWS
    block_ids = jnp.arange(blocks, dtype=jnp.int32)
    return (blocks, tgt_count, block_ids)


def route_table(key):
    blocks, tgt_count, block_ids = block_layout()
    subkeys = jax.random.split(jax.random.fold_in(key, 11), blocks)
    slot_ids = jax.vmap(lambda single: jax.random.permutation(single, ROWS))(subkeys).astype(jnp.int32)
    dest_index = slot_ids // SPAN
    within = slot_ids % SPAN
    src_index = (block_ids // tgt_count)[:, None]
    tgt_index = (block_ids % tgt_count)[:, None]
    table = (dest_index * tgt_count + tgt_index) * ROWS + src_index * SPAN + within
    return table.reshape(SENTENCES).astype(jnp.int32)


def bucket_offsets(key):
    blocks, tgt_count, block_ids = block_layout()
    positions = jnp.arange(ROWS, dtype=jnp.int32)[None, :]
    cover = positions >= ROWS - BPD
    filler = positions - (ROWS - BPD)
    source_off = jax.random.randint(jax.random.fold_in(key, 12), (blocks, ROWS), 0, BPD, dtype=jnp.int32)
    source_off = jnp.where(cover, filler, source_off)
    source_off = source_off.at[:, 1].set(source_off[:, 0])
    target_off = jax.random.randint(jax.random.fold_in(key, 13), (blocks, ROWS), 0, BPD, dtype=jnp.int32)
    target_off = jnp.where(cover, filler, target_off)
    target_off = target_off.at[:, 0].set(source_off[:, 0])
    target_off = target_off.at[:, 1].set(source_off[:, 0])
    base_bucket = (block_ids // tgt_count * BPG + block_ids % tgt_count * BPD)[:, None]
    return ((base_bucket + source_off).reshape(SENTENCES), (base_bucket + target_off).reshape(SENTENCES))


def row_scales(key, lower, upper):
    return jnp.exp(jax.random.uniform(key, (SENTENCES, 1), jnp.float32, math.log(lower), math.log(upper)))


def draw_source(key, part):
    values = jnp.clip(jax.random.normal(jax.random.fold_in(key, 21), (SENTENCES, D), jnp.float32), -6.0, 6.0)
    values = values * row_scales(jax.random.fold_in(key, 22), 0.25, 2.5)
    return values[route_table(key)].astype(jnp.bfloat16)


def draw_target(key, part):
    values = jnp.clip(jax.random.normal(jax.random.fold_in(key, 23), (SENTENCES, D), jnp.float32), -6.0, 6.0)
    values = values * row_scales(jax.random.fold_in(key, 24), 0.25, 2.5)
    return values.astype(jnp.bfloat16)


def draw_src_bucket(key, part):
    ordered_bucket, target_bucket = bucket_offsets(key)
    return ordered_bucket[route_table(key)]


def draw_tgt_bucket(key, part):
    ordered_bucket, target_bucket = bucket_offsets(key)
    return target_bucket


def draw_band(key, part):
    blocks, tgt_count, block_ids = block_layout()
    widths = jax.random.randint(jax.random.fold_in(key, 14), (blocks, ROWS), 1, BANDMAX + 1, dtype=jnp.int32)
    widths = widths.at[:, ROWS - 1].set(BANDMAX)
    return widths.reshape(SENTENCES)[route_table(key)]


def draw_route(key, part):
    return route_table(key)


def setup_inputs(seed: int = 0) -> dict:
    key_of = jax.random.split(jax.random.key(seed), 7)
    source = draw_source(jax.random.fold_in(key_of[6], 71), 0)
    target = draw_target(jax.random.fold_in(key_of[6], 71), 0)
    src_bucket = draw_src_bucket(jax.random.fold_in(key_of[6], 71), 0)
    tgt_bucket = draw_tgt_bucket(jax.random.fold_in(key_of[6], 71), 0)
    band = draw_band(jax.random.fold_in(key_of[6], 71), 0)
    route = draw_route(jax.random.fold_in(key_of[6], 71), 0)
    return {"source": source, "target": target, "src_bucket": src_bucket, "tgt_bucket": tgt_bucket, "band": band, "route": route}


lowest = -1e+30

def one_group(pieces):
    x_group, y_group, bucket_x, bucket_y, band_x = pieces
    scores = jnp.dot(x_group, y_group.T, preferred_element_type=jnp.float32) * (2.0 / math.sqrt(D))
    allowed = (jnp.abs(bucket_x[:, None] - bucket_y[None, :]) <= band_x[:, None]) & (bucket_x[:, None] // BPG == bucket_y[None, :] // BPG)
    masked = jnp.where(allowed, scores, lowest)
    row_top = lax.optimization_barrier(jnp.max(masked, axis=1, keepdims=True))
    row_weights = jnp.where(allowed, jnp.exp(masked - row_top), 0.0)
    src_out = jnp.dot(row_weights.astype(jnp.bfloat16), y_group, preferred_element_type=jnp.float32)
    src_out = src_out / lax.optimization_barrier(jnp.sum(row_weights, axis=1, keepdims=True))
    col_top = lax.optimization_barrier(jnp.max(masked, axis=0, keepdims=True))
    col_weights = jnp.where(allowed, jnp.exp(masked - col_top), 0.0)
    tgt_out = jnp.dot(col_weights.T.astype(jnp.bfloat16), x_group, preferred_element_type=jnp.float32)
    tgt_out = tgt_out / lax.optimization_barrier(jnp.sum(col_weights, axis=0))[:, None]
    return (src_out, tgt_out)

def reference(source, target, src_bucket, tgt_bucket, band, route):
    ordered = jnp.zeros_like(source).at[route].set(source)
    ordered_bucket = jnp.zeros_like(src_bucket).at[route].set(src_bucket)
    ordered_band = jnp.zeros_like(band).at[route].set(band)
    groups = SENTENCES // GROUP_ROWS
    pieces = (ordered.reshape(groups, GROUP_ROWS, D), target.reshape(groups, GROUP_ROWS, D), ordered_bucket.reshape(groups, GROUP_ROWS), tgt_bucket.reshape(groups, GROUP_ROWS), ordered_band.reshape(groups, GROUP_ROWS))
    src_read, tgt_read = lax.map(one_group, pieces)
    return (src_read.reshape(SENTENCES, D), tgt_read.reshape(SENTENCES, D))
```

```python
import math

import jax
import jax.numpy as jnp
from jax import lax
from jax.sharding import PartitionSpec as P

lowest = -1e30


def shifted(value, axis, steps):
    count = lax.axis_size(axis)
    pairs = [(source, (source + steps) % count) for source in range(count)]
    return lax.ppermute(value, axis, pairs)


def allowed_mask(x_bucket, x_band, y_bucket, groups):
    near = jnp.abs(x_bucket[:, None] - y_bucket[None, :]) <= x_band[:, None]
    same = x_bucket[:, None] // groups == y_bucket[None, :] // groups
    return near & same


def on_device(source, target, src_bucket, tgt_bucket, band, route, bucket_group):
    row_count, feature_count = source.shape
    src_count = lax.axis_size("src")
    tgt_count = lax.axis_size("tgt")
    per_peer = row_count // src_count
    scaling = 2.0 / math.sqrt(feature_count)

    t_left = shifted((target, tgt_bucket), "tgt", 1)
    t_right = shifted((target, tgt_bucket), "tgt", -1)

    dest_slot = route // (row_count * tgt_count) * per_peer + route % per_peer
    placed = jnp.zeros_like(source).at[dest_slot].set(source)
    labels = jnp.stack([src_bucket, band], axis=1)
    placed_labels = jnp.zeros_like(labels).at[dest_slot].set(labels)
    sources = lax.all_to_all(placed, "src", split_axis=0, concat_axis=0, tiled=True)
    got_labels = lax.all_to_all(placed_labels, "src", split_axis=0, concat_axis=0, tiled=True)
    x_bucket, x_band = got_labels[:, 0], got_labels[:, 1]

    x_left = shifted((sources, x_bucket, x_band), "tgt", 1)
    x_right = shifted((sources, x_bucket, x_band), "tgt", -1)

    y_all = jnp.concatenate([t_left[0], target, t_right[0]], axis=0)
    y_bucket = jnp.concatenate([t_left[1], tgt_bucket, t_right[1]], axis=0)
    scores = lax.dot_general(
        sources, y_all, (((1,), (1,)), ((), ())), preferred_element_type=jnp.float32
    ) * scaling
    allowed = allowed_mask(x_bucket, x_band, y_bucket, bucket_group)
    masked = jnp.where(allowed, scores, lowest)
    row_top = jnp.max(masked, axis=1, keepdims=True)
    row_weights = jnp.where(allowed, jnp.exp(masked - row_top), 0.0)
    src_read = jnp.dot(
        row_weights.astype(jnp.bfloat16), y_all, preferred_element_type=jnp.float32
    ) / jnp.sum(row_weights, axis=1, keepdims=True)

    xs_all = jnp.concatenate([x_left[0], sources, x_right[0]], axis=0)
    xs_bucket = jnp.concatenate([x_left[1], x_bucket, x_right[1]], axis=0)
    xs_band = jnp.concatenate([x_left[2], x_band, x_right[2]], axis=0)
    col_scores = lax.dot_general(
        xs_all, target, (((1,), (1,)), ((), ())), preferred_element_type=jnp.float32
    ) * scaling
    col_allowed = allowed_mask(xs_bucket, xs_band, tgt_bucket, bucket_group)
    col_masked = jnp.where(col_allowed, col_scores, lowest)
    col_top = jnp.max(col_masked, axis=0, keepdims=True)
    col_weights = jnp.where(col_allowed, jnp.exp(col_masked - col_top), 0.0)
    tgt_read = lax.dot_general(
        col_weights.astype(jnp.bfloat16),
        xs_all,
        (((0,), (0,)), ((), ())),
        preferred_element_type=jnp.float32,
    ) / jnp.sum(col_weights, axis=0)[:, None]
    return (src_read, tgt_read)


def solution(mesh):
    placed = (
        P(("src", "tgt"), None),
        P(("src", "tgt"), None),
        P(("src", "tgt")),
        P(("src", "tgt")),
        P(("src", "tgt")),
        P(("src", "tgt")),
    )
    bucket_group = 128

    def body(*args):
        return on_device(*args, bucket_group)

    return jax.shard_map(
        body,
        mesh=mesh,
        in_specs=placed,
        out_specs=(P(("src", "tgt"), None), P(("src", "tgt"), None)),
        check_vma=False,
    )
```

```python
import functools
import math

import jax
import jax.numpy as jnp
from jax import lax
from jax.experimental import pallas as pl
from jax.experimental.pallas import tpu as pltpu
from jax.sharding import PartitionSpec as P

lowest = -1e30
MESH = pl.DeviceIdType.MESH
LABEL_LANES = 128
DIGIT = 64


def labelled(rows, columns):
    pad = jnp.zeros((rows.shape[0], LABEL_LANES - len(columns)), rows.dtype)
    labels = [c.astype(jnp.float32).astype(rows.dtype)[:, None] for c in columns]
    return jnp.concatenate([rows] + labels + [pad], axis=1)


def block_labels(block, features):
    slab = block[:, features:].astype(jnp.float32)
    as_cols = slab.astype(jnp.int32)
    as_rows = slab.T.astype(jnp.int32)
    return as_cols, as_rows


def kernel(groups, features, scaling, placed, target, src_out, tgt_out,
           xs, xl, xr, tl, tr, a2a_send, a2a_recv, nb_send, nb_recv, local_sem):
    g = lax.axis_index("src")
    t = lax.axis_index("tgt")
    n_src = lax.axis_size("src")
    n_tgt = lax.axis_size("tgt")
    span = placed.shape[0] // n_src
    left = lax.rem(t + n_tgt - 1, n_tgt)
    right = lax.rem(t + 1, n_tgt)

    barrier = pltpu.get_barrier_semaphore()

    def greet(d, carry):
        peer = lax.rem(g + d, n_src)
        pl.semaphore_signal(barrier, inc=1, device_id=(peer, t), device_id_type=MESH)
        return carry

    lax.fori_loop(1, n_src, greet, 0)
    pl.semaphore_signal(barrier, inc=1, device_id=(g, left), device_id_type=MESH)
    pl.semaphore_signal(barrier, inc=1, device_id=(g, right), device_id_type=MESH)
    pl.semaphore_wait(barrier, n_src + 1)

    t_to_right = pltpu.make_async_remote_copy(
        target, tl, nb_send.at[0], nb_recv.at[0], device_id=(g, right), device_id_type=MESH)
    t_to_left = pltpu.make_async_remote_copy(
        target, tr, nb_send.at[1], nb_recv.at[1], device_id=(g, left), device_id_type=MESH)
    t_to_right.start()
    t_to_left.start()

    def a2a_copy(peer):
        return pltpu.make_async_remote_copy(
            placed.at[pl.ds(peer * span, span)],
            xs.at[pl.ds(g * span, span)],
            a2a_send.at[peer],
            a2a_recv.at[g],
            device_id=(peer, t),
            device_id_type=MESH,
        )

    def a2a_start(d, carry):
        a2a_copy(lax.rem(g + d, n_src)).start()
        return carry

    lax.fori_loop(1, n_src, a2a_start, 0)
    own = pltpu.make_async_copy(
        placed.at[pl.ds(g * span, span)], xs.at[pl.ds(g * span, span)], local_sem.at[0])
    own.start()

    def a2a_wait(d, carry):
        peer = lax.rem(g + d, n_src)
        a2a_copy(peer).wait_send()
        sender = lax.rem(g + n_src - d, n_src)
        pltpu.make_async_remote_copy(
            placed.at[pl.ds(sender * span, span)],
            xs.at[pl.ds(sender * span, span)],
            a2a_send.at[sender],
            a2a_recv.at[sender],
            device_id=(sender, t),
            device_id_type=MESH,
        ).wait_recv()
        return carry

    lax.fori_loop(1, n_src, a2a_wait, 0)
    own.wait()

    x_to_right = pltpu.make_async_remote_copy(
        xs, xl, nb_send.at[2], nb_recv.at[2], device_id=(g, right), device_id_type=MESH)
    x_to_left = pltpu.make_async_remote_copy(
        xs, xr, nb_send.at[3], nb_recv.at[3], device_id=(g, left), device_id_type=MESH)
    x_to_right.start()
    x_to_left.start()

    t_to_right.wait()
    t_to_left.wait()

    x_main = xs[:, :features]
    x_cols, _ = block_labels(xs[...], features)
    x_bucket = x_cols[:, 0:1] * DIGIT + x_cols[:, 1:2]
    x_band = x_cols[:, 2:3]
    row_scores, row_masks = [], []
    for blk in (tl, target, tr):
        _, y_rows = block_labels(blk[...], features)
        y_bucket = y_rows[0:1, :] * DIGIT + y_rows[1:2, :]
        s = lax.dot_general(
            x_main, blk[:, :features], (((1,), (1,)), ((), ())),
            preferred_element_type=jnp.float32) * scaling
        ok = (jnp.abs(x_bucket - y_bucket) <= x_band) & (
            (x_bucket >> 7) == (y_bucket >> 7))
        row_scores.append(jnp.where(ok, s, lowest))
        row_masks.append(ok)
    top = functools.reduce(jnp.maximum, [jnp.max(s, axis=1, keepdims=True) for s in row_scores])
    total = jnp.zeros_like(top)
    read = jnp.zeros((x_main.shape[0], features), jnp.float32)
    for s, ok, blk in zip(row_scores, row_masks, (tl, target, tr)):
        w = jnp.where(ok, jnp.exp(s - top), 0.0)
        total = total + jnp.sum(w, axis=1, keepdims=True)
        read = read + jnp.dot(w.astype(jnp.bfloat16), blk[:, :features],
                              preferred_element_type=jnp.float32)
    src_out[...] = read / total

    x_to_right.wait()
    x_to_left.wait()

    y_main = target[:, :features]
    y_cols, _ = block_labels(target[...], features)
    y_bucket = y_cols[:, 0:1] * DIGIT + y_cols[:, 1:2]
    col_scores, col_masks = [], []
    for blk in (xl, xs, xr):
        _, s_rows = block_labels(blk[...], features)
        s_bucket = s_rows[0:1, :] * DIGIT + s_rows[1:2, :]
        s_band = s_rows[2:3, :]
        s = lax.dot_general(
            y_main, blk[:, :features], (((1,), (1,)), ((), ())),
            preferred_element_type=jnp.float32) * scaling
        ok = (jnp.abs(s_bucket - y_bucket) <= s_band) & (
            (s_bucket >> 7) == (y_bucket >> 7))
        col_scores.append(jnp.where(ok, s, lowest))
        col_masks.append(ok)
    top = functools.reduce(jnp.maximum, [jnp.max(s, axis=1, keepdims=True) for s in col_scores])
    total = jnp.zeros_like(top)
    read = jnp.zeros((y_main.shape[0], features), jnp.float32)
    for s, ok, blk in zip(col_scores, col_masks, (xl, xs, xr)):
        w = jnp.where(ok, jnp.exp(s - top), 0.0)
        total = total + jnp.sum(w, axis=1, keepdims=True)
        read = read + jnp.dot(w.astype(jnp.bfloat16), blk[:, :features],
                              preferred_element_type=jnp.float32)
    tgt_out[...] = read / total


def on_device(source, target, src_bucket, tgt_bucket, band, route):
    row_count, feature_count = source.shape
    src_count = lax.axis_size("src")
    tgt_count = lax.axis_size("tgt")
    per_peer = row_count // src_count
    scaling = 2.0 / math.sqrt(feature_count)
    groups = 128

    dest_slot = route // (row_count * tgt_count) * per_peer + route % per_peer
    src_lab = labelled(source, [src_bucket // DIGIT, src_bucket % DIGIT, band])
    placed = jnp.zeros_like(src_lab).at[dest_slot].set(src_lab)
    tgt_lab = labelled(target, [tgt_bucket // DIGIT, tgt_bucket % DIGIT])
    width = placed.shape[1]

    block = jax.ShapeDtypeStruct((row_count, feature_count), jnp.float32)
    vmem = pl.BlockSpec(memory_space=pltpu.VMEM)
    return pl.pallas_call(
        functools.partial(kernel, groups, feature_count, scaling),
        out_shape=(block, block),
        in_specs=[vmem, vmem],
        out_specs=(vmem, vmem),
        scratch_shapes=[pltpu.VMEM((row_count, width), jnp.bfloat16)] * 5
        + [
            pltpu.SemaphoreType.DMA((src_count,)),
            pltpu.SemaphoreType.DMA((src_count,)),
            pltpu.SemaphoreType.DMA((4,)),
            pltpu.SemaphoreType.DMA((4,)),
            pltpu.SemaphoreType.DMA((1,)),
        ],
        compiler_params=pltpu.CompilerParams(collective_id=0, has_side_effects=True),
    )(placed, tgt_lab)


def solution(mesh):
    placed = (
        P(("src", "tgt"), None),
        P(("src", "tgt"), None),
        P(("src", "tgt")),
        P(("src", "tgt")),
        P(("src", "tgt")),
        P(("src", "tgt")),
    )
    return jax.shard_map(
        on_device,
        mesh=mesh,
        in_specs=placed,
        out_specs=(P(("src", "tgt"), None), P(("src", "tgt"), None)),
        check_vma=False,
    )
```

```python
import functools
import math

import jax
import jax.numpy as jnp
from jax import lax
from jax.experimental import pallas as pl
from jax.experimental.pallas import tpu as pltpu
from jax.sharding import PartitionSpec as P

lowest = -1e30
MESH = pl.DeviceIdType.MESH
LABEL_LANES = 128
DIGIT = 64
SRC_HI, SRC_LO, SRC_BAND, DEST, TGT_HI, TGT_LO = range(6)


def softmax_read(main, main_bucket, band_col, others, features, scaling, band_of_rows):
    scores, masks = [], []
    for blk, bucket_row, band_row in others:
        s = lax.dot_general(
            main, blk[:, :features], (((1,), (1,)), ((), ())),
            preferred_element_type=jnp.float32) * scaling
        band = band_col if band_of_rows else band_row
        ok = (jnp.abs(main_bucket - bucket_row) <= band) & (
            (main_bucket >> 7) == (bucket_row >> 7))
        scores.append(jnp.where(ok, s, lowest))
        masks.append(ok)
    top = functools.reduce(jnp.maximum, [jnp.max(s, axis=1, keepdims=True) for s in scores])
    total = jnp.zeros_like(top)
    read = jnp.zeros((main.shape[0], features), jnp.float32)
    for s, ok, (blk, _, _) in zip(scores, masks, others):
        w = jnp.where(ok, jnp.exp(s - top), 0.0)
        total = total + jnp.sum(w, axis=1, keepdims=True)
        read = read + jnp.dot(w.astype(jnp.bfloat16), blk[:, :features],
                              preferred_element_type=jnp.float32)
    return read / total


def label_rows(blk, features, hi, lo, band=None):
    slab = blk[:, features:].astype(jnp.float32).T.astype(jnp.int32)
    bucket = slab[hi:hi + 1, :] * DIGIT + slab[lo:lo + 1, :]
    return bucket, (slab[band:band + 1, :] if band is not None else None)


def kernel(features, scaling, source, target, lab, src_out, tgt_out,
           xsend, tsend, xs, xl, xr, tl, tr,
           a2a_send, a2a_recv, fw_send, fw_recv, nb_send, nb_recv, local_sem):
    g = lax.axis_index("src")
    t = lax.axis_index("tgt")
    n_src = lax.axis_size("src")
    n_tgt = lax.axis_size("tgt")
    rows = source.shape[0]
    span = rows // n_src
    n_z = n_src // 2
    z = g // 2
    core = g % 2
    partner = z * 2 + 1 - core
    left = lax.rem(t + n_tgt - 1, n_tgt)
    right = lax.rem(t + 1, n_tgt)

    def far_peer(j):
        kz = j // 2 + 1
        offset = ((kz + 1) // 2) * (2 * (kz % 2) - 1)
        return ((z + offset + n_z) % n_z) * 2 + j % 2

    barrier = pltpu.get_barrier_semaphore()
    pl.semaphore_signal(barrier, inc=1, device_id=(partner, t), device_id_type=MESH)

    def greet(j, carry):
        pl.semaphore_signal(barrier, inc=1, device_id=(far_peer(j), t), device_id_type=MESH)
        return carry

    lax.fori_loop(0, n_src - 2, greet, 0)
    pl.semaphore_signal(barrier, inc=1, device_id=(g, left), device_id_type=MESH)
    pl.semaphore_signal(barrier, inc=1, device_id=(g, right), device_id_type=MESH)

    table = lab[...]
    labels = table.T.astype(jnp.bfloat16)
    dest = table[DEST:DEST + 1, :].astype(jnp.int32)
    onehot = (lax.broadcasted_iota(jnp.int32, (rows, rows), 0) == dest).astype(jnp.bfloat16)
    xsend[:, :features] = jnp.dot(
        onehot, source[...], preferred_element_type=jnp.float32).astype(jnp.bfloat16)
    xsend[:, features:] = jnp.dot(
        onehot, labels, preferred_element_type=jnp.float32).astype(jnp.bfloat16)
    tsend[:, :features] = target[...]
    tsend[:, features:] = labels

    pl.semaphore_wait(barrier, n_src + 1)

    t_to_right = pltpu.make_async_remote_copy(
        tsend, tl, nb_send.at[0], nb_recv.at[0], device_id=(g, right), device_id_type=MESH)
    t_to_left = pltpu.make_async_remote_copy(
        tsend, tr, nb_send.at[1], nb_recv.at[1], device_id=(g, left), device_id_type=MESH)
    t_to_right.start()
    t_to_left.start()

    def a2a_copy(peer, sender):
        return pltpu.make_async_remote_copy(
            xsend.at[pl.ds(peer * span, span)],
            xs.at[pl.ds(sender * span, span)],
            a2a_send.at[peer],
            a2a_recv.at[sender],
            device_id=(peer, t),
            device_id_type=MESH,
        )

    own = pltpu.make_async_copy(
        xsend.at[pl.ds(g * span, span)], xs.at[pl.ds(g * span, span)], local_sem.at[0])
    own.start()
    a2a_copy(partner, g).start()

    def a2a_start(j, carry):
        a2a_copy(far_peer(j), g).start()
        return carry

    lax.fori_loop(0, n_src - 2, a2a_start, 0)

    def forward(sender):
        rows_of = pl.ds(sender * span, span)
        return (
            pltpu.make_async_remote_copy(
                xs.at[rows_of], xl.at[rows_of], fw_send.at[sender], fw_recv.at[sender],
                device_id=(g, right), device_id_type=MESH),
            pltpu.make_async_remote_copy(
                xs.at[rows_of], xr.at[rows_of], fw_send.at[n_src + sender],
                fw_recv.at[n_src + sender], device_id=(g, left), device_id_type=MESH),
        )

    def arrive_and_forward(sender):
        rows_of = pl.ds(sender * span, span)
        pltpu.make_async_remote_copy(
            xsend.at[rows_of], xs.at[rows_of], a2a_send.at[sender], a2a_recv.at[sender],
            device_id=(sender, t), device_id_type=MESH).wait_recv()
        for c in forward(sender):
            c.start()

    own.wait()
    for c in forward(g):
        c.start()
    arrive_and_forward(partner)

    def a2a_arrive(j, carry):
        arrive_and_forward(far_peer(j))
        return carry

    lax.fori_loop(0, n_src - 2, a2a_arrive, 0)

    t_to_right.wait()
    t_to_left.wait()

    x_cols = xs[:, features:].astype(jnp.float32).astype(jnp.int32)
    x_bucket = x_cols[:, SRC_HI:SRC_HI + 1] * DIGIT + x_cols[:, SRC_LO:SRC_LO + 1]
    x_band = x_cols[:, SRC_BAND:SRC_BAND + 1]
    tgt_blocks = []
    for blk in (tl, tsend, tr):
        bucket_row, _ = label_rows(blk[...], features, TGT_HI, TGT_LO)
        tgt_blocks.append((blk, bucket_row, None))
    src_out[...] = softmax_read(
        xs[:, :features], x_bucket, x_band, tgt_blocks, features, scaling, True)

    a2a_copy(partner, g).wait_send()

    def a2a_sent(j, carry):
        a2a_copy(far_peer(j), g).wait_send()
        return carry

    lax.fori_loop(0, n_src - 2, a2a_sent, 0)

    def fw_done(s, carry):
        for c in forward(s):
            c.wait_send()
            c.wait_recv()
        return carry

    lax.fori_loop(0, n_src, fw_done, 0)

    y_cols = tsend[:, features:].astype(jnp.float32).astype(jnp.int32)
    y_bucket = y_cols[:, TGT_HI:TGT_HI + 1] * DIGIT + y_cols[:, TGT_LO:TGT_LO + 1]
    src_blocks = []
    for blk in (xl, xs, xr):
        bucket_row, band_row = label_rows(blk[...], features, SRC_HI, SRC_LO, SRC_BAND)
        src_blocks.append((blk, bucket_row, band_row))
    tgt_out[...] = softmax_read(
        tsend[:, :features], y_bucket, None, src_blocks, features, scaling, False)


def on_device(source, target, src_bucket, tgt_bucket, band, route):
    row_count, feature_count = source.shape
    src_count = lax.axis_size("src")
    tgt_count = lax.axis_size("tgt")
    per_peer = row_count // src_count
    scaling = 2.0 / math.sqrt(feature_count)

    dest_slot = route // (row_count * tgt_count) * per_peer + route % per_peer
    table = jnp.stack(
        [src_bucket // DIGIT, src_bucket % DIGIT, band, dest_slot,
         tgt_bucket // DIGIT, tgt_bucket % DIGIT]).astype(jnp.float32)
    table = jnp.pad(table, ((0, LABEL_LANES - table.shape[0]), (0, 0)))
    width = feature_count + LABEL_LANES

    block = jax.ShapeDtypeStruct((row_count, feature_count), jnp.float32)
    vmem = pl.BlockSpec(memory_space=pltpu.VMEM)
    return pl.pallas_call(
        functools.partial(kernel, feature_count, scaling),
        out_shape=(block, block),
        in_specs=[vmem, vmem, vmem],
        out_specs=(vmem, vmem),
        scratch_shapes=[pltpu.VMEM((row_count, width), jnp.bfloat16)] * 7
        + [
            pltpu.SemaphoreType.DMA((src_count,)),
            pltpu.SemaphoreType.DMA((src_count,)),
            pltpu.SemaphoreType.DMA((2 * src_count,)),
            pltpu.SemaphoreType.DMA((2 * src_count,)),
            pltpu.SemaphoreType.DMA((2,)),
            pltpu.SemaphoreType.DMA((2,)),
            pltpu.SemaphoreType.DMA((1,)),
        ],
        compiler_params=pltpu.CompilerParams(collective_id=0, has_side_effects=True),
    )(source, target, table)


def solution(mesh):
    placed = (
        P(("src", "tgt"), None),
        P(("src", "tgt"), None),
        P(("src", "tgt")),
        P(("src", "tgt")),
        P(("src", "tgt")),
        P(("src", "tgt")),
    )
    return jax.shard_map(
        on_device,
        mesh=mesh,
        in_specs=placed,
        out_specs=(P(("src", "tgt"), None), P(("src", "tgt"), None)),
        check_vma=False,
    )
```

```python
import functools
import math

import jax
import jax.numpy as jnp
from jax import lax
from jax.experimental import pallas as pl
from jax.experimental.pallas import tpu as pltpu
from jax.sharding import PartitionSpec as P

lowest = -1e30
MESH = pl.DeviceIdType.MESH
LABEL_LANES = 128
DIGIT = 64
SRC_HI, SRC_LO, SRC_BAND, DEST, TGT_HI, TGT_LO = range(6)


def softmax_read(main, main_bucket, band_col, others, features, scaling, band_of_rows):
    scores, masks = [], []
    for blk, bucket_row, band_row in others:
        s = lax.dot_general(
            main, blk[:, :features], (((1,), (1,)), ((), ())),
            preferred_element_type=jnp.float32) * scaling
        band = band_col if band_of_rows else band_row
        ok = (jnp.abs(main_bucket - bucket_row) <= band) & (
            (main_bucket >> 7) == (bucket_row >> 7))
        scores.append(jnp.where(ok, s, lowest))
        masks.append(ok)
    top = functools.reduce(jnp.maximum, [jnp.max(s, axis=1, keepdims=True) for s in scores])
    total = jnp.zeros_like(top)
    read = jnp.zeros((main.shape[0], features), jnp.float32)
    for s, ok, (blk, _, _) in zip(scores, masks, others):
        w = jnp.where(ok, jnp.exp(s - top), 0.0)
        total = total + jnp.sum(w, axis=1, keepdims=True)
        read = read + jnp.dot(w.astype(jnp.bfloat16), blk[:, :features],
                              preferred_element_type=jnp.float32)
    return read, total


def label_rows(blk, features, hi, lo, band=None):
    slab = blk[:, features:].astype(jnp.float32).T.astype(jnp.int32)
    bucket = slab[hi:hi + 1, :] * DIGIT + slab[lo:lo + 1, :]
    return bucket, (slab[band:band + 1, :] if band is not None else None)


def kernel(features, scaling, source_hbm, target_hbm, lab_hbm, src_out, tgt_out, src_total, tgt_total,
           source, target, lab, xsend, tsend, xs, xl, xr, tl, tr,
           a2a_send, a2a_recv, fw_send, fw_recv, nb_send, nb_recv, local_sem):
    g = lax.axis_index("src")
    t = lax.axis_index("tgt")
    n_src = lax.axis_size("src")
    n_tgt = lax.axis_size("tgt")
    rows = source.shape[0]
    span = rows // n_src
    n_z = n_src // 2
    z = g // 2
    core = g % 2
    partner = z * 2 + 1 - core
    left = lax.rem(t + n_tgt - 1, n_tgt)
    right = lax.rem(t + 1, n_tgt)

    def far_peer(j):
        kz = j // 2 + 1
        offset = ((kz + 1) // 2) * (2 * (kz % 2) - 1)
        return ((z + offset + n_z) % n_z) * 2 + j % 2

    loads = [
        pltpu.make_async_copy(hbm, vmem, local_sem.at[1 + i])
        for i, (hbm, vmem) in enumerate(((source_hbm, source), (target_hbm, target), (lab_hbm, lab)))
    ]
    for c in loads:
        c.start()

    barrier = pltpu.get_barrier_semaphore()
    pl.semaphore_signal(barrier, inc=1, device_id=(partner, t), device_id_type=MESH)

    def greet(j, carry):
        pl.semaphore_signal(barrier, inc=1, device_id=(far_peer(j), t), device_id_type=MESH)
        return carry

    lax.fori_loop(0, n_src - 2, greet, 0)
    pl.semaphore_signal(barrier, inc=1, device_id=(g, left), device_id_type=MESH)
    pl.semaphore_signal(barrier, inc=1, device_id=(g, right), device_id_type=MESH)

    for c in loads:
        c.wait()

    table = lab[...]
    slot = lax.broadcasted_iota(jnp.int32, (rows, rows), 0)
    lane = lax.broadcasted_iota(jnp.int32, (rows, LABEL_LANES), 1)
    onehot = (slot == table[DEST:DEST + 1, :].astype(jnp.int32)).astype(jnp.float32)
    ident = (slot == lax.broadcasted_iota(jnp.int32, (rows, rows), 1)).astype(jnp.float32)

    def label_slab(select, kinds):
        slab = jnp.zeros((rows, LABEL_LANES), jnp.float32)
        for k in kinds:
            column = jnp.sum(select * table[k:k + 1, :], axis=1, keepdims=True)
            slab = jnp.where(lane == k, column, slab)
        return slab.astype(jnp.bfloat16)

    xsend[:, :features] = jnp.dot(
        onehot.astype(jnp.bfloat16), source[...],
        preferred_element_type=jnp.float32).astype(jnp.bfloat16)
    xsend[:, features:] = label_slab(onehot, (SRC_HI, SRC_LO, SRC_BAND))
    tsend[:, :features] = target[...]
    tsend[:, features:] = label_slab(ident, (TGT_HI, TGT_LO))

    pl.semaphore_wait(barrier, n_src + 1)

    t_to_right = pltpu.make_async_remote_copy(
        tsend, tl, nb_send.at[0], nb_recv.at[0], device_id=(g, right), device_id_type=MESH)
    t_to_left = pltpu.make_async_remote_copy(
        tsend, tr, nb_send.at[1], nb_recv.at[1], device_id=(g, left), device_id_type=MESH)
    t_to_right.start()
    t_to_left.start()

    def a2a_copy(peer, sender):
        return pltpu.make_async_remote_copy(
            xsend.at[pl.ds(peer * span, span)],
            xs.at[pl.ds(sender * span, span)],
            a2a_send.at[peer],
            a2a_recv.at[sender],
            device_id=(peer, t),
            device_id_type=MESH,
        )

    own = pltpu.make_async_copy(
        xsend.at[pl.ds(g * span, span)], xs.at[pl.ds(g * span, span)], local_sem.at[0])
    own.start()
    a2a_copy(partner, g).start()

    def a2a_start(j, carry):
        a2a_copy(far_peer(j), g).start()
        return carry

    lax.fori_loop(0, n_src - 2, a2a_start, 0)

    def forward(sender):
        rows_of = pl.ds(sender * span, span)
        return (
            pltpu.make_async_remote_copy(
                xs.at[rows_of], xl.at[rows_of], fw_send.at[sender], fw_recv.at[sender],
                device_id=(g, right), device_id_type=MESH),
            pltpu.make_async_remote_copy(
                xs.at[rows_of], xr.at[rows_of], fw_send.at[n_src + sender],
                fw_recv.at[n_src + sender], device_id=(g, left), device_id_type=MESH),
        )

    def arrive_and_forward(sender):
        rows_of = pl.ds(sender * span, span)
        pltpu.make_async_remote_copy(
            xsend.at[rows_of], xs.at[rows_of], a2a_send.at[sender], a2a_recv.at[sender],
            device_id=(sender, t), device_id_type=MESH).wait_recv()
        for c in forward(sender):
            c.start()

    own.wait()
    for c in forward(g):
        c.start()
    arrive_and_forward(partner)

    def a2a_arrive(j, carry):
        arrive_and_forward(far_peer(j))
        return carry

    lax.fori_loop(0, n_src - 2, a2a_arrive, 0)

    t_to_right.wait()
    t_to_left.wait()

    x_cols = xs[:, features:].astype(jnp.float32).astype(jnp.int32)
    x_bucket = x_cols[:, SRC_HI:SRC_HI + 1] * DIGIT + x_cols[:, SRC_LO:SRC_LO + 1]
    x_band = x_cols[:, SRC_BAND:SRC_BAND + 1]
    tgt_blocks = []
    for blk in (tl, tsend, tr):
        bucket_row, _ = label_rows(blk[...], features, TGT_HI, TGT_LO)
        tgt_blocks.append((blk, bucket_row, None))
    src_out[...], src_total[...] = softmax_read(
        xs[:, :features], x_bucket, x_band, tgt_blocks, features, scaling, True)

    a2a_copy(partner, g).wait_send()

    def a2a_sent(j, carry):
        a2a_copy(far_peer(j), g).wait_send()
        return carry

    lax.fori_loop(0, n_src - 2, a2a_sent, 0)

    def fw_done(s, carry):
        for c in forward(s):
            c.wait_send()
            c.wait_recv()
        return carry

    lax.fori_loop(0, n_src, fw_done, 0)

    y_cols = tsend[:, features:].astype(jnp.float32).astype(jnp.int32)
    y_bucket = y_cols[:, TGT_HI:TGT_HI + 1] * DIGIT + y_cols[:, TGT_LO:TGT_LO + 1]
    src_blocks = []
    for blk in (xl, xs, xr):
        bucket_row, band_row = label_rows(blk[...], features, SRC_HI, SRC_LO, SRC_BAND)
        src_blocks.append((blk, bucket_row, band_row))
    tgt_out[...], tgt_total[...] = softmax_read(
        tsend[:, :features], y_bucket, None, src_blocks, features, scaling, False)


def on_device(source, target, src_bucket, tgt_bucket, band, route):
    row_count, feature_count = source.shape
    src_count = lax.axis_size("src")
    tgt_count = lax.axis_size("tgt")
    per_peer = row_count // src_count
    scaling = 2.0 / math.sqrt(feature_count)

    dest_slot = route // (row_count * tgt_count) * per_peer + route % per_peer
    table = jnp.stack(
        [src_bucket // DIGIT, src_bucket % DIGIT, band, dest_slot,
         tgt_bucket // DIGIT, tgt_bucket % DIGIT]).astype(jnp.float32)
    table = jnp.pad(table, ((0, 8 - table.shape[0]), (0, 0)))
    width = feature_count + LABEL_LANES

    block = jax.ShapeDtypeStruct((row_count, feature_count), jnp.float32)
    totals = jax.ShapeDtypeStruct((row_count, 1), jnp.float32)
    vmem = pl.BlockSpec(memory_space=pltpu.VMEM)
    hbm = pl.BlockSpec(memory_space=pl.ANY)
    src_read, tgt_read, src_total, tgt_total = pl.pallas_call(
        functools.partial(kernel, feature_count, scaling),
        out_shape=(block, block, totals, totals),
        in_specs=[hbm, hbm, hbm],
        out_specs=(vmem, vmem, vmem, vmem),
        scratch_shapes=[
            pltpu.VMEM((row_count, feature_count), jnp.bfloat16),
            pltpu.VMEM((row_count, feature_count), jnp.bfloat16),
            pltpu.VMEM(table.shape, jnp.float32),
        ]
        + [pltpu.VMEM((row_count, width), jnp.bfloat16)] * 7
        + [
            pltpu.SemaphoreType.DMA((src_count,)),
            pltpu.SemaphoreType.DMA((src_count,)),
            pltpu.SemaphoreType.DMA((2 * src_count,)),
            pltpu.SemaphoreType.DMA((2 * src_count,)),
            pltpu.SemaphoreType.DMA((2,)),
            pltpu.SemaphoreType.DMA((2,)),
            pltpu.SemaphoreType.DMA((4,)),
        ],
        compiler_params=pltpu.CompilerParams(collective_id=0, has_side_effects=True),
    )(source, target, table)
    return (src_read / src_total, tgt_read / tgt_total)


def solution(mesh):
    placed = (
        P(("src", "tgt"), None),
        P(("src", "tgt"), None),
        P(("src", "tgt")),
        P(("src", "tgt")),
        P(("src", "tgt")),
        P(("src", "tgt")),
    )
    return jax.shard_map(
        on_device,
        mesh=mesh,
        in_specs=placed,
        out_specs=(P(("src", "tgt"), None), P(("src", "tgt"), None)),
        check_vma=False,
    )
```

```python
import functools
import math

import jax
import jax.numpy as jnp
from jax import lax
from jax.experimental import pallas as pl
from jax.experimental.pallas import tpu as pltpu
from jax.sharding import PartitionSpec as P

lowest = -1e30
MESH = pl.DeviceIdType.MESH
LABEL_LANES = 128
DIGIT = 64
SRC_HI, SRC_LO, SRC_BAND, TGT_HI, TGT_LO = 0, 1, 2, 4, 5


def softmax_read(main, main_bucket, band_col, others, features, scaling, band_of_rows):
    scores, masks = [], []
    for blk, bucket_row, band_row in others:
        s = lax.dot_general(
            main, blk[:, :features], (((1,), (1,)), ((), ())),
            preferred_element_type=jnp.float32) * scaling
        band = band_col if band_of_rows else band_row
        ok = (jnp.abs(main_bucket - bucket_row) <= band) & (
            (main_bucket >> 7) == (bucket_row >> 7))
        scores.append(jnp.where(ok, s, lowest))
        masks.append(ok)
    top = functools.reduce(jnp.maximum, [jnp.max(s, axis=1, keepdims=True) for s in scores])
    total = jnp.zeros_like(top)
    read = jnp.zeros((main.shape[0], features), jnp.float32)
    for s, ok, (blk, _, _) in zip(scores, masks, others):
        w = jnp.where(ok, jnp.exp(s - top), 0.0)
        total = total + jnp.sum(w, axis=1, keepdims=True)
        read = read + jnp.dot(w.astype(jnp.bfloat16), blk[:, :features],
                              preferred_element_type=jnp.float32)
    return read / total


def label_rows(blk, features, hi, lo, band=None):
    slab = blk[:, features:].astype(jnp.float32).T.astype(jnp.int32)
    bucket = slab[hi:hi + 1, :] * DIGIT + slab[lo:lo + 1, :]
    return bucket, (slab[band:band + 1, :] if band is not None else None)


def shift_of(divisor):
    assert divisor & (divisor - 1) == 0
    return divisor.bit_length() - 1


def kernel(features, scaling, source_hbm, target_hbm, src_bucket_hbm, band_hbm, route_hbm,
           tgt_bucket_hbm, src_out, tgt_out,
           source, target, src_bucket, band, route, tgt_bucket, xsend, tsend, xs, xl, xr, tl, tr,
           a2a_send, a2a_recv, fw_send, fw_recv, nb_send, nb_recv, local_sem):
    g = lax.axis_index("src")
    t = lax.axis_index("tgt")
    n_src = lax.axis_size("src")
    n_tgt = lax.axis_size("tgt")
    rows = source.shape[0]
    span = rows // n_src
    n_z = n_src // 2
    z = g // 2
    core = g % 2
    partner = z * 2 + 1 - core
    left = lax.rem(t + n_tgt - 1, n_tgt)
    right = lax.rem(t + 1, n_tgt)

    def far_peer(j):
        kz = j // 2 + 1
        offset = ((kz + 1) // 2) * (2 * (kz % 2) - 1)
        return ((z + offset + n_z) % n_z) * 2 + j % 2

    pairs = ((source_hbm, source), (target_hbm, target), (src_bucket_hbm, src_bucket),
             (band_hbm, band), (route_hbm, route), (tgt_bucket_hbm, tgt_bucket))
    loads = [pltpu.make_async_copy(h, v, local_sem.at[1 + i]) for i, (h, v) in enumerate(pairs)]
    for c in loads:
        c.start()

    barrier = pltpu.get_barrier_semaphore()
    pl.semaphore_signal(barrier, inc=1, device_id=(partner, t), device_id_type=MESH)

    def greet(j, carry):
        pl.semaphore_signal(barrier, inc=1, device_id=(far_peer(j), t), device_id_type=MESH)
        return carry

    lax.fori_loop(0, n_src - 2, greet, 0)
    pl.semaphore_signal(barrier, inc=1, device_id=(g, left), device_id_type=MESH)
    pl.semaphore_signal(barrier, inc=1, device_id=(g, right), device_id_type=MESH)

    for c in loads:
        c.wait()

    where_to = route[...]
    dest = (where_to >> shift_of(rows * n_tgt)) * span + (where_to & ((1 << shift_of(span)) - 1))
    sb = src_bucket[...]
    tb = tgt_bucket[...]
    label_rows_of = {
        SRC_HI: sb >> shift_of(DIGIT), SRC_LO: sb & (DIGIT - 1), SRC_BAND: band[...],
        TGT_HI: tb >> shift_of(DIGIT), TGT_LO: tb & (DIGIT - 1),
    }
    slot = lax.broadcasted_iota(jnp.int32, (rows, rows), 0)
    lane = lax.broadcasted_iota(jnp.int32, (rows, LABEL_LANES), 1)
    onehot = (slot == dest).astype(jnp.float32)
    ident = (slot == lax.broadcasted_iota(jnp.int32, (rows, rows), 1)).astype(jnp.float32)

    def label_slab(select, kinds):
        slab = jnp.zeros((rows, LABEL_LANES), jnp.float32)
        for k in kinds:
            row = label_rows_of[k].astype(jnp.float32)
            column = jnp.sum(select * row, axis=1, keepdims=True)
            slab = jnp.where(lane == k, column, slab)
        return slab.astype(jnp.bfloat16)

    xsend[:, :features] = jnp.dot(
        onehot.astype(jnp.bfloat16), source[...],
        preferred_element_type=jnp.float32).astype(jnp.bfloat16)
    xsend[:, features:] = label_slab(onehot, (SRC_HI, SRC_LO, SRC_BAND))
    tsend[:, :features] = target[...]
    tsend[:, features:] = label_slab(ident, (TGT_HI, TGT_LO))

    pl.semaphore_wait(barrier, n_src + 1)

    t_to_right = pltpu.make_async_remote_copy(
        tsend, tl, nb_send.at[0], nb_recv.at[0], device_id=(g, right), device_id_type=MESH)
    t_to_left = pltpu.make_async_remote_copy(
        tsend, tr, nb_send.at[1], nb_recv.at[1], device_id=(g, left), device_id_type=MESH)
    t_to_right.start()
    t_to_left.start()

    def a2a_copy(peer, sender):
        return pltpu.make_async_remote_copy(
            xsend.at[pl.ds(peer * span, span)],
            xs.at[pl.ds(sender * span, span)],
            a2a_send.at[peer],
            a2a_recv.at[sender],
            device_id=(peer, t),
            device_id_type=MESH,
        )

    own = pltpu.make_async_copy(
        xsend.at[pl.ds(g * span, span)], xs.at[pl.ds(g * span, span)], local_sem.at[0])
    def a2a_start(j, carry):
        a2a_copy(far_peer(n_src - 3 - j), g).start()
        return carry

    lax.fori_loop(0, n_src - 2, a2a_start, 0)
    a2a_copy(partner, g).start()
    own.start()

    def forward(sender):
        rows_of = pl.ds(sender * span, span)
        return (
            pltpu.make_async_remote_copy(
                xs.at[rows_of], xl.at[rows_of], fw_send.at[sender], fw_recv.at[sender],
                device_id=(g, right), device_id_type=MESH),
            pltpu.make_async_remote_copy(
                xs.at[rows_of], xr.at[rows_of], fw_send.at[n_src + sender],
                fw_recv.at[n_src + sender], device_id=(g, left), device_id_type=MESH),
        )

    def arrive_and_forward(sender):
        rows_of = pl.ds(sender * span, span)
        pltpu.make_async_remote_copy(
            xsend.at[rows_of], xs.at[rows_of], a2a_send.at[sender], a2a_recv.at[sender],
            device_id=(sender, t), device_id_type=MESH).wait_recv()
        for c in forward(sender):
            c.start()

    own.wait()
    for c in forward(g):
        c.start()
    arrive_and_forward(partner)

    def a2a_arrive(j, carry):
        arrive_and_forward(far_peer(j))
        return carry

    lax.fori_loop(0, n_src - 2, a2a_arrive, 0)

    t_to_right.wait()
    t_to_left.wait()

    x_cols = xs[:, features:].astype(jnp.float32).astype(jnp.int32)
    x_bucket = x_cols[:, SRC_HI:SRC_HI + 1] * DIGIT + x_cols[:, SRC_LO:SRC_LO + 1]
    x_band = x_cols[:, SRC_BAND:SRC_BAND + 1]
    tgt_blocks = []
    for blk in (tl, tsend, tr):
        bucket_row, _ = label_rows(blk[...], features, TGT_HI, TGT_LO)
        tgt_blocks.append((blk, bucket_row, None))
    src_out[...] = softmax_read(
        xs[:, :features], x_bucket, x_band, tgt_blocks, features, scaling, True)

    a2a_copy(partner, g).wait_send()

    def a2a_sent(j, carry):
        a2a_copy(far_peer(j), g).wait_send()
        return carry

    lax.fori_loop(0, n_src - 2, a2a_sent, 0)

    def fw_done(s, carry):
        for c in forward(s):
            c.wait_send()
            c.wait_recv()
        return carry

    lax.fori_loop(0, n_src, fw_done, 0)

    y_cols = tsend[:, features:].astype(jnp.float32).astype(jnp.int32)
    y_bucket = y_cols[:, TGT_HI:TGT_HI + 1] * DIGIT + y_cols[:, TGT_LO:TGT_LO + 1]
    src_blocks = []
    for blk in (xl, xs, xr):
        bucket_row, band_row = label_rows(blk[...], features, SRC_HI, SRC_LO, SRC_BAND)
        src_blocks.append((blk, bucket_row, band_row))
    tgt_out[...] = softmax_read(
        tsend[:, :features], y_bucket, None, src_blocks, features, scaling, False)


def on_device(source, target, src_bucket, tgt_bucket, band, route):
    row_count, feature_count = source.shape
    src_count = lax.axis_size("src")
    tgt_count = lax.axis_size("tgt")
    per_peer = row_count // src_count
    scaling = 2.0 / math.sqrt(feature_count)

    width = feature_count + LABEL_LANES
    ints = [v.reshape(1, row_count) for v in (src_bucket, band, route, tgt_bucket)]

    block = jax.ShapeDtypeStruct((row_count, feature_count), jnp.float32)
    vmem = pl.BlockSpec(memory_space=pltpu.VMEM)
    return pl.pallas_call(
        functools.partial(kernel, feature_count, scaling),
        out_shape=(block, block),
        in_specs=[pl.BlockSpec(memory_space=pl.ANY)] * 6,
        out_specs=(vmem, vmem),
        scratch_shapes=[pltpu.VMEM((row_count, feature_count), jnp.bfloat16)] * 2
        + [pltpu.VMEM((1, row_count), jnp.int32)] * 4
        + [pltpu.VMEM((row_count, width), jnp.bfloat16)] * 7
        + [
            pltpu.SemaphoreType.DMA((src_count,)),
            pltpu.SemaphoreType.DMA((src_count,)),
            pltpu.SemaphoreType.DMA((2 * src_count,)),
            pltpu.SemaphoreType.DMA((2 * src_count,)),
            pltpu.SemaphoreType.DMA((2,)),
            pltpu.SemaphoreType.DMA((2,)),
            pltpu.SemaphoreType.DMA((7,)),
        ],
        compiler_params=pltpu.CompilerParams(collective_id=0, has_side_effects=True),
    )(source, target, *ints)


def solution(mesh):
    placed = (
        P(("src", "tgt"), None),
        P(("src", "tgt"), None),
        P(("src", "tgt")),
        P(("src", "tgt")),
        P(("src", "tgt")),
        P(("src", "tgt")),
    )
    return jax.shard_map(
        on_device,
        mesh=mesh,
        in_specs=placed,
        out_specs=(P(("src", "tgt"), None), P(("src", "tgt"), None)),
        check_vma=False,
    )
```

```python
import functools
import math

import jax
import jax.numpy as jnp
from jax import lax
from jax.experimental import pallas as pl
from jax.experimental.pallas import tpu as pltpu
from jax.sharding import PartitionSpec as P

lowest = -1e30
MESH = pl.DeviceIdType.MESH
LABEL_LANES = 128
DIGIT = 64
SRC_HI, SRC_LO, SRC_BAND, TGT_HI, TGT_LO = 0, 1, 2, 4, 5


def softmax_read(main, main_bucket, band_col, others, features, scaling, band_of_rows):
    scores, masks = [], []
    for blk, bucket_row, band_row in others:
        s = lax.dot_general(
            main, blk[:, :features], (((1,), (1,)), ((), ())),
            preferred_element_type=jnp.float32) * scaling
        band = band_col if band_of_rows else band_row
        ok = (jnp.abs(main_bucket - bucket_row) <= band) & (
            (main_bucket >> 7) == (bucket_row >> 7))
        scores.append(jnp.where(ok, s, lowest))
        masks.append(ok)
    top = functools.reduce(jnp.maximum, [jnp.max(s, axis=1, keepdims=True) for s in scores])
    total = jnp.zeros_like(top)
    read = jnp.zeros((main.shape[0], features), jnp.float32)
    for s, ok, (blk, _, _) in zip(scores, masks, others):
        w = jnp.where(ok, jnp.exp(s - top), 0.0)
        total = total + jnp.sum(w, axis=1, keepdims=True)
        read = read + jnp.dot(w.astype(jnp.bfloat16), blk[:, :features],
                              preferred_element_type=jnp.float32)
    return read / total


def label_rows(blk, features, hi, lo, band=None):
    slab = blk[:, features:].astype(jnp.float32).T.astype(jnp.int32)
    bucket = slab[hi:hi + 1, :] * DIGIT + slab[lo:lo + 1, :]
    return bucket, (slab[band:band + 1, :] if band is not None else None)


def shift_of(divisor):
    assert divisor & (divisor - 1) == 0
    return divisor.bit_length() - 1


def kernel(features, scaling, source_hbm, target_hbm, src_bucket_hbm, band_hbm, route_hbm,
           tgt_bucket_hbm, src_out, tgt_out,
           source, target, src_bucket, band, route, tgt_bucket, xsend, tsend, xs, xp, xl, xr, tl, tr,
           wsend, wrecv, fw_send, fw_recv, rsend, prelay, nb_send, nb_recv, local_sem):
    g = lax.axis_index("src")
    t = lax.axis_index("tgt")
    n_src = lax.axis_size("src")
    n_tgt = lax.axis_size("tgt")
    rows = source.shape[0]
    span = rows // n_src
    n_z = n_src // 2
    z = g // 2
    core = g % 2
    partner = z * 2 + 1 - core
    left = lax.rem(t + n_tgt - 1, n_tgt)
    right = lax.rem(t + 1, n_tgt)

    pairs = ((source_hbm, source), (target_hbm, target), (src_bucket_hbm, src_bucket),
             (band_hbm, band), (route_hbm, route), (tgt_bucket_hbm, tgt_bucket))
    loads = [pltpu.make_async_copy(h, v, local_sem.at[1 + i]) for i, (h, v) in enumerate(pairs)]
    for c in loads:
        c.start()

    barrier = pltpu.get_barrier_semaphore()
    pl.semaphore_signal(barrier, inc=1, device_id=(partner, t), device_id_type=MESH)

    def z_far(j):
        kz = j + 1
        offset = ((kz + 1) // 2) * (2 * (kz % 2) - 1)
        return (z + offset + n_z) % n_z

    def greet(j, carry):
        pl.semaphore_signal(barrier, inc=1, device_id=(z_far(j) * 2 + core, t), device_id_type=MESH)
        return carry

    lax.fori_loop(0, n_z - 1, greet, 0)
    pl.semaphore_signal(barrier, inc=1, device_id=(g, left), device_id_type=MESH)
    pl.semaphore_signal(barrier, inc=1, device_id=(g, right), device_id_type=MESH)

    for c in loads:
        c.wait()

    where_to = route[...]
    dest = (where_to >> shift_of(rows * n_tgt)) * span + (where_to & ((1 << shift_of(span)) - 1))
    sb = src_bucket[...]
    tb = tgt_bucket[...]
    label_rows_of = {
        SRC_HI: sb >> shift_of(DIGIT), SRC_LO: sb & (DIGIT - 1), SRC_BAND: band[...],
        TGT_HI: tb >> shift_of(DIGIT), TGT_LO: tb & (DIGIT - 1),
    }
    slot = lax.broadcasted_iota(jnp.int32, (rows, rows), 0)
    lane = lax.broadcasted_iota(jnp.int32, (rows, LABEL_LANES), 1)
    onehot = (slot == dest).astype(jnp.float32)
    ident = (slot == lax.broadcasted_iota(jnp.int32, (rows, rows), 1)).astype(jnp.float32)

    def label_slab(select, kinds):
        slab = jnp.zeros((rows, LABEL_LANES), jnp.float32)
        for k in kinds:
            row = label_rows_of[k].astype(jnp.float32)
            column = jnp.sum(select * row, axis=1, keepdims=True)
            slab = jnp.where(lane == k, column, slab)
        return slab.astype(jnp.bfloat16)

    xsend[:, :features] = jnp.dot(
        onehot.astype(jnp.bfloat16), source[...],
        preferred_element_type=jnp.float32).astype(jnp.bfloat16)
    xsend[:, features:] = label_slab(onehot, (SRC_HI, SRC_LO, SRC_BAND))
    tsend[:, :features] = target[...]
    tsend[:, features:] = label_slab(ident, (TGT_HI, TGT_LO))

    pl.semaphore_wait(barrier, n_z + 2)

    t_to_right = pltpu.make_async_remote_copy(
        tsend, tl, nb_send.at[0], nb_recv.at[0], device_id=(g, right), device_id_type=MESH)
    t_to_left = pltpu.make_async_remote_copy(
        tsend, tr, nb_send.at[1], nb_recv.at[1], device_id=(g, left), device_id_type=MESH)
    t_to_right.start()
    t_to_left.start()

    wide = 2 * span
    mine = core * span
    theirs = (1 - core) * span

    def wide_copy(zd, zs):
        return pltpu.make_async_remote_copy(
            xsend.at[pl.ds(zd * wide, wide)], xs.at[pl.ds(zs * wide, wide)],
            wsend.at[zd], wrecv.at[zs], device_id=(zd * 2 + core, t), device_id_type=MESH)

    def relay_copy(zs):
        return pltpu.make_async_remote_copy(
            xs.at[pl.ds(zs * wide + theirs, span)], xp.at[pl.ds(zs * wide + mine, span)],
            rsend.at[zs], prelay.at[zs], device_id=(partner, t), device_id_type=MESH)

    def relay_arrival(zs):
        return pltpu.make_async_remote_copy(
            xs.at[pl.ds(zs * wide + mine, span)], xp.at[pl.ds(zs * wide + theirs, span)],
            rsend.at[zs], prelay.at[zs], device_id=(partner, t), device_id_type=MESH)

    def w_start(j, carry):
        zd = z_far(n_z - 2 - j)
        wide_copy(zd, z).start()
        return carry

    lax.fori_loop(0, n_z - 1, w_start, 0)
    direct = pltpu.make_async_remote_copy(
        xsend.at[pl.ds(z * wide + theirs, span)], xp.at[pl.ds(z * wide + mine, span)],
        rsend.at[z], prelay.at[z], device_id=(partner, t), device_id_type=MESH)
    direct.start()
    own = pltpu.make_async_copy(
        xsend.at[pl.ds(z * wide + mine, span)], xs.at[pl.ds(z * wide + mine, span)], local_sem.at[0])
    own.start()

    def forward(sender, buf):
        rows_of = pl.ds(sender * span, span)
        return (
            pltpu.make_async_remote_copy(
                buf.at[rows_of], xl.at[rows_of], fw_send.at[sender], fw_recv.at[sender],
                device_id=(g, right), device_id_type=MESH),
            pltpu.make_async_remote_copy(
                buf.at[rows_of], xr.at[rows_of], fw_send.at[n_src + sender],
                fw_recv.at[n_src + sender], device_id=(g, left), device_id_type=MESH),
        )

    def wide_arrived(zs):
        wide_copy(zs, zs).wait_recv()
        relay_copy(zs).start()
        for c in forward(zs * 2 + core, xs):
            c.start()

    def relay_arrived(zs):
        relay_arrival(zs).wait_recv()
        for c in forward(zs * 2 + 1 - core, xp):
            c.start()

    own.wait()
    for c in forward(g, xs):
        c.start()
    wide_arrived(z_far(0))

    def w_arrive(j, carry):
        wide_arrived(z_far(j))
        relay_arrived(z_far(j - 1))
        return carry

    lax.fori_loop(1, n_z - 1, w_arrive, 0)
    relay_arrived(z_far(n_z - 2))
    relay_arrived(z)

    t_to_right.wait()
    t_to_left.wait()

    sender_core = (lax.broadcasted_iota(jnp.int32, (rows, 1), 0) // span) % 2
    merged = jnp.where(sender_core == core, xs[...], xp[...])

    x_cols = merged[:, features:].astype(jnp.float32).astype(jnp.int32)
    x_bucket = x_cols[:, SRC_HI:SRC_HI + 1] * DIGIT + x_cols[:, SRC_LO:SRC_LO + 1]
    x_band = x_cols[:, SRC_BAND:SRC_BAND + 1]
    tgt_blocks = []
    for blk in (tl, tsend, tr):
        bucket_row, _ = label_rows(blk[...], features, TGT_HI, TGT_LO)
        tgt_blocks.append((blk, bucket_row, None))
    src_out[...] = softmax_read(
        merged[:, :features], x_bucket, x_band, tgt_blocks, features, scaling, True)

    def w_sent(j, carry):
        wide_copy(z_far(j), z).wait_send()
        relay_copy(z_far(j)).wait_send()
        return carry

    lax.fori_loop(0, n_z - 1, w_sent, 0)
    direct.wait_send()

    def fw_done(s, carry):
        for c in forward(s, xs):
            c.wait_send()
            c.wait_recv()
        return carry

    lax.fori_loop(0, n_src, fw_done, 0)

    y_cols = tsend[:, features:].astype(jnp.float32).astype(jnp.int32)
    y_bucket = y_cols[:, TGT_HI:TGT_HI + 1] * DIGIT + y_cols[:, TGT_LO:TGT_LO + 1]
    src_blocks = []
    for blk in (xl, merged, xr):
        bucket_row, band_row = label_rows(blk[...], features, SRC_HI, SRC_LO, SRC_BAND)
        src_blocks.append((blk, bucket_row, band_row))
    tgt_out[...] = softmax_read(
        tsend[:, :features], y_bucket, None, src_blocks, features, scaling, False)


def on_device(source, target, src_bucket, tgt_bucket, band, route):
    row_count, feature_count = source.shape
    src_count = lax.axis_size("src")
    tgt_count = lax.axis_size("tgt")
    per_peer = row_count // src_count
    scaling = 2.0 / math.sqrt(feature_count)

    width = feature_count + LABEL_LANES
    ints = [v.reshape(1, row_count) for v in (src_bucket, band, route, tgt_bucket)]

    block = jax.ShapeDtypeStruct((row_count, feature_count), jnp.float32)
    vmem = pl.BlockSpec(memory_space=pltpu.VMEM)
    return pl.pallas_call(
        functools.partial(kernel, feature_count, scaling),
        out_shape=(block, block),
        in_specs=[pl.BlockSpec(memory_space=pl.ANY)] * 6,
        out_specs=(vmem, vmem),
        scratch_shapes=[pltpu.VMEM((row_count, feature_count), jnp.bfloat16)] * 2
        + [pltpu.VMEM((1, row_count), jnp.int32)] * 4
        + [pltpu.VMEM((row_count, width), jnp.bfloat16)] * 8
        + [
            pltpu.SemaphoreType.DMA((src_count // 2,)),
            pltpu.SemaphoreType.DMA((src_count // 2,)),
            pltpu.SemaphoreType.DMA((2 * src_count,)),
            pltpu.SemaphoreType.DMA((2 * src_count,)),
            pltpu.SemaphoreType.DMA((src_count // 2,)),
            pltpu.SemaphoreType.DMA((src_count // 2,)),
            pltpu.SemaphoreType.DMA((2,)),
            pltpu.SemaphoreType.DMA((2,)),
            pltpu.SemaphoreType.DMA((7,)),
        ],
        compiler_params=pltpu.CompilerParams(collective_id=0, has_side_effects=True),
    )(source, target, *ints)


def solution(mesh):
    placed = (
        P(("src", "tgt"), None),
        P(("src", "tgt"), None),
        P(("src", "tgt")),
        P(("src", "tgt")),
        P(("src", "tgt")),
        P(("src", "tgt")),
    )
    return jax.shard_map(
        on_device,
        mesh=mesh,
        in_specs=placed,
        out_specs=(P(("src", "tgt"), None), P(("src", "tgt"), None)),
        check_vma=False,
    )
```

```python
import functools
import math

import jax
import jax.numpy as jnp
from jax import lax
from jax.experimental import pallas as pl
from jax.experimental.pallas import tpu as pltpu
from jax.sharding import PartitionSpec as P

lowest = -1e30
MESH = pl.DeviceIdType.MESH
LABEL_LANES = 128
DIGIT = 64
SRC_HI, SRC_LO, SRC_BAND, TGT_HI, TGT_LO = 0, 1, 2, 4, 5


def softmax_read(main, main_bucket, band_col, others, features, scaling, band_of_rows):
    scores, masks = [], []
    for blk, bucket_row, band_row in others:
        s = lax.dot_general(
            main, blk[:, :features], (((1,), (1,)), ((), ())),
            preferred_element_type=jnp.float32) * scaling
        band = band_col if band_of_rows else band_row
        ok = (jnp.abs(main_bucket - bucket_row) <= band) & (
            (main_bucket >> 7) == (bucket_row >> 7))
        scores.append(jnp.where(ok, s, lowest))
        masks.append(ok)
    top = functools.reduce(jnp.maximum, [jnp.max(s, axis=1, keepdims=True) for s in scores])
    total = jnp.zeros_like(top)
    read = jnp.zeros((main.shape[0], features), jnp.float32)
    for s, ok, (blk, _, _) in zip(scores, masks, others):
        w = jnp.where(ok, jnp.exp(s - top), 0.0)
        total = total + jnp.sum(w, axis=1, keepdims=True)
        read = read + jnp.dot(w.astype(jnp.bfloat16), blk[:, :features],
                              preferred_element_type=jnp.float32)
    return read / total


def label_rows(blk, features, hi, lo, band=None):
    slab = blk[:, features:].astype(jnp.float32).T.astype(jnp.int32)
    bucket = slab[hi:hi + 1, :] * DIGIT + slab[lo:lo + 1, :]
    return bucket, (slab[band:band + 1, :] if band is not None else None)


def shift_of(divisor):
    assert divisor & (divisor - 1) == 0
    return divisor.bit_length() - 1


def kernel(features, scaling, source_hbm, target_hbm, src_bucket_hbm, band_hbm, route_hbm,
           tgt_bucket_hbm, src_out, tgt_out,
           source, target, src_bucket, band, route, tgt_bucket, xsend, tsend, xs, xl, xr, tl, tr,
           a2a_send, a2a_recv, fw_send, fw_recv, nb_send, nb_recv, local_sem):
    g = lax.axis_index("src")
    t = lax.axis_index("tgt")
    n_src = lax.axis_size("src")
    n_tgt = lax.axis_size("tgt")
    rows = source.shape[0]
    span = rows // n_src
    n_z = n_src // 2
    z = g // 2
    core = g % 2
    partner = z * 2 + 1 - core
    left = lax.rem(t + n_tgt - 1, n_tgt)
    right = lax.rem(t + 1, n_tgt)

    def far_peer(j):
        kz = j // 2 + 1
        offset = ((kz + 1) // 2) * (2 * (kz % 2) - 1)
        return ((z + offset + n_z) % n_z) * 2 + j % 2

    pairs = ((source_hbm, source), (target_hbm, target), (src_bucket_hbm, src_bucket),
             (band_hbm, band), (route_hbm, route), (tgt_bucket_hbm, tgt_bucket))
    loads = [pltpu.make_async_copy(h, v, local_sem.at[1 + i]) for i, (h, v) in enumerate(pairs)]
    for c in loads:
        c.start()

    barrier = pltpu.get_barrier_semaphore()
    pl.semaphore_signal(barrier, inc=1, device_id=(partner, t), device_id_type=MESH)

    def greet(j, carry):
        pl.semaphore_signal(barrier, inc=1, device_id=(far_peer(j), t), device_id_type=MESH)
        return carry

    lax.fori_loop(0, n_src - 2, greet, 0)
    pl.semaphore_signal(barrier, inc=1, device_id=(g, left), device_id_type=MESH)
    pl.semaphore_signal(barrier, inc=1, device_id=(g, right), device_id_type=MESH)

    for c in loads:
        c.wait()

    where_to = route[...]
    dest = (where_to >> shift_of(rows * n_tgt)) * span + (where_to & ((1 << shift_of(span)) - 1))
    sb = src_bucket[...]
    tb = tgt_bucket[...]
    label_rows_of = {
        SRC_HI: sb >> shift_of(DIGIT), SRC_LO: sb & (DIGIT - 1), SRC_BAND: band[...],
        TGT_HI: tb >> shift_of(DIGIT), TGT_LO: tb & (DIGIT - 1),
    }
    slot = lax.broadcasted_iota(jnp.int32, (rows, rows), 0)
    lane = lax.broadcasted_iota(jnp.int32, (rows, LABEL_LANES), 1)
    onehot = (slot == dest).astype(jnp.float32)
    ident = (slot == lax.broadcasted_iota(jnp.int32, (rows, rows), 1)).astype(jnp.float32)

    def label_slab(select, kinds):
        slab = jnp.zeros((rows, LABEL_LANES), jnp.float32)
        for k in kinds:
            row = label_rows_of[k].astype(jnp.float32)
            column = jnp.sum(select * row, axis=1, keepdims=True)
            slab = jnp.where(lane == k, column, slab)
        return slab.astype(jnp.bfloat16)

    xsend[:, :features] = jnp.dot(
        onehot.astype(jnp.bfloat16), source[...],
        preferred_element_type=jnp.float32).astype(jnp.bfloat16)
    xsend[:, features:] = label_slab(onehot, (SRC_HI, SRC_LO, SRC_BAND))
    tsend[:, :features] = target[...]
    tsend[:, features:] = label_slab(ident, (TGT_HI, TGT_LO))

    pl.semaphore_wait(barrier, n_src + 1)

    t_to_right = pltpu.make_async_remote_copy(
        tsend, tl, nb_send.at[0], nb_recv.at[0], device_id=(g, right), device_id_type=MESH)
    t_to_left = pltpu.make_async_remote_copy(
        tsend, tr, nb_send.at[1], nb_recv.at[1], device_id=(g, left), device_id_type=MESH)
    t_to_right.start()
    t_to_left.start()

    def a2a_copy(peer, sender):
        return pltpu.make_async_remote_copy(
            xsend.at[pl.ds(peer * span, span)],
            xs.at[pl.ds(sender * span, span)],
            a2a_send.at[peer],
            a2a_recv.at[sender],
            device_id=(peer, t),
            device_id_type=MESH,
        )

    own = pltpu.make_async_copy(
        xsend.at[pl.ds(g * span, span)], xs.at[pl.ds(g * span, span)], local_sem.at[0])
    own.start()
    a2a_copy(partner, g).start()

    def a2a_start(j, carry):
        a2a_copy(far_peer(j), g).start()
        return carry

    lax.fori_loop(0, n_src - 2, a2a_start, 0)

    def forward(sender):
        rows_of = pl.ds(sender * span, span)
        return (
            pltpu.make_async_remote_copy(
                xs.at[rows_of], xl.at[rows_of], fw_send.at[sender], fw_recv.at[sender],
                device_id=(g, right), device_id_type=MESH),
            pltpu.make_async_remote_copy(
                xs.at[rows_of], xr.at[rows_of], fw_send.at[n_src + sender],
                fw_recv.at[n_src + sender], device_id=(g, left), device_id_type=MESH),
        )

    def arrive_and_forward(sender):
        rows_of = pl.ds(sender * span, span)
        pltpu.make_async_remote_copy(
            xsend.at[rows_of], xs.at[rows_of], a2a_send.at[sender], a2a_recv.at[sender],
            device_id=(sender, t), device_id_type=MESH).wait_recv()
        for c in forward(sender):
            c.start()

    own.wait()
    for c in forward(g):
        c.start()
    arrive_and_forward(partner)

    def a2a_arrive(j, carry):
        arrive_and_forward(far_peer(j))
        return carry

    lax.fori_loop(0, n_src - 2, a2a_arrive, 0)

    t_to_right.wait()
    t_to_left.wait()

    x_cols = xs[:, features:].astype(jnp.float32).astype(jnp.int32)
    x_bucket = x_cols[:, SRC_HI:SRC_HI + 1] * DIGIT + x_cols[:, SRC_LO:SRC_LO + 1]
    x_band = x_cols[:, SRC_BAND:SRC_BAND + 1]
    tgt_blocks = []
    for blk in (tl, tsend, tr):
        bucket_row, _ = label_rows(blk[...], features, TGT_HI, TGT_LO)
        tgt_blocks.append((blk, bucket_row, None))
    src_out[...] = softmax_read(
        xs[:, :features], x_bucket, x_band, tgt_blocks, features, scaling, True)

    a2a_copy(partner, g).wait_send()

    def a2a_sent(j, carry):
        a2a_copy(far_peer(j), g).wait_send()
        return carry

    lax.fori_loop(0, n_src - 2, a2a_sent, 0)

    def fw_done(s, carry):
        for c in forward(s):
            c.wait_send()
            c.wait_recv()
        return carry

    lax.fori_loop(0, n_src, fw_done, 0)

    y_cols = tsend[:, features:].astype(jnp.float32).astype(jnp.int32)
    y_bucket = y_cols[:, TGT_HI:TGT_HI + 1] * DIGIT + y_cols[:, TGT_LO:TGT_LO + 1]
    src_blocks = []
    for blk in (xl, xs, xr):
        bucket_row, band_row = label_rows(blk[...], features, SRC_HI, SRC_LO, SRC_BAND)
        src_blocks.append((blk, bucket_row, band_row))
    tgt_out[...] = softmax_read(
        tsend[:, :features], y_bucket, None, src_blocks, features, scaling, False)


def on_device(source, target, src_bucket, tgt_bucket, band, route):
    row_count, feature_count = source.shape
    src_count = lax.axis_size("src")
    tgt_count = lax.axis_size("tgt")
    per_peer = row_count // src_count
    scaling = 2.0 / math.sqrt(feature_count)

    width = feature_count + LABEL_LANES
    ints = [v.reshape(1, row_count) for v in (src_bucket, band, route, tgt_bucket)]

    block = jax.ShapeDtypeStruct((row_count, feature_count), jnp.float32)
    vmem = pl.BlockSpec(memory_space=pltpu.VMEM)
    return pl.pallas_call(
        functools.partial(kernel, feature_count, scaling),
        out_shape=(block, block),
        in_specs=[pl.BlockSpec(memory_space=pl.ANY)] * 6,
        out_specs=(vmem, vmem),
        scratch_shapes=[pltpu.VMEM((row_count, feature_count), jnp.bfloat16)] * 2
        + [pltpu.VMEM((1, row_count), jnp.int32)] * 4
        + [pltpu.VMEM((row_count, width), jnp.bfloat16)] * 7
        + [
            pltpu.SemaphoreType.DMA((src_count,)),
            pltpu.SemaphoreType.DMA((src_count,)),
            pltpu.SemaphoreType.DMA((2 * src_count,)),
            pltpu.SemaphoreType.DMA((2 * src_count,)),
            pltpu.SemaphoreType.DMA((2,)),
            pltpu.SemaphoreType.DMA((2,)),
            pltpu.SemaphoreType.DMA((7,)),
        ],
        compiler_params=pltpu.CompilerParams(collective_id=0, has_side_effects=True),
    )(source, target, *ints)


def solution(mesh):
    placed = (
        P(("src", "tgt"), None),
        P(("src", "tgt"), None),
        P(("src", "tgt")),
        P(("src", "tgt")),
        P(("src", "tgt")),
        P(("src", "tgt")),
    )
    return jax.shard_map(
        on_device,
        mesh=mesh,
        in_specs=placed,
        out_specs=(P(("src", "tgt"), None), P(("src", "tgt"), None)),
        check_vma=False,
    )
```

```python
import functools
import math

import jax
import jax.numpy as jnp
from jax import lax
from jax.experimental import pallas as pl
from jax.experimental.pallas import tpu as pltpu
from jax.sharding import PartitionSpec as P

lowest = -1e30
MESH = pl.DeviceIdType.MESH
LABEL_LANES = 128
DIGIT = 64
SRC_HI, SRC_LO, SRC_BAND, TGT_HI, TGT_LO = 0, 1, 2, 4, 5


def softmax_read(main, main_bucket, band_col, others, features, scaling, band_of_rows):
    scores, masks = [], []
    for blk, bucket_row, band_row in others:
        s = lax.dot_general(
            main, blk[:, :features], (((1,), (1,)), ((), ())),
            preferred_element_type=jnp.float32) * scaling
        band = band_col if band_of_rows else band_row
        ok = (jnp.abs(main_bucket - bucket_row) <= band) & (
            (main_bucket >> 7) == (bucket_row >> 7))
        scores.append(jnp.where(ok, s, lowest))
        masks.append(ok)
    top = functools.reduce(jnp.maximum, [jnp.max(s, axis=1, keepdims=True) for s in scores])
    total = jnp.zeros_like(top)
    read = jnp.zeros((main.shape[0], features), jnp.float32)
    for s, ok, (blk, _, _) in zip(scores, masks, others):
        w = jnp.where(ok, jnp.exp(s - top), 0.0)
        total = total + jnp.sum(w, axis=1, keepdims=True)
        read = read + jnp.dot(w.astype(jnp.bfloat16), blk[:, :features],
                              preferred_element_type=jnp.float32)
    return read / total


def label_rows(blk, features, hi, lo, band=None):
    slab = blk[:, features:].astype(jnp.float32).T.astype(jnp.int32)
    bucket = slab[hi:hi + 1, :] * DIGIT + slab[lo:lo + 1, :]
    return bucket, (slab[band:band + 1, :] if band is not None else None)


def shift_of(divisor):
    assert divisor & (divisor - 1) == 0
    return divisor.bit_length() - 1


def kernel(features, scaling, source_hbm, target_hbm, src_bucket_hbm, band_hbm, route_hbm,
           tgt_bucket_hbm, src_out, tgt_out,
           source, target, src_bucket, band, route, tgt_bucket, xsend, tsend, xs, xl, xr, tl, tr,
           a2a_send, a2a_recv, fw_send, fw_recv, nb_send, nb_recv, local_sem):
    g = lax.axis_index("src")
    t = lax.axis_index("tgt")
    n_src = lax.axis_size("src")
    n_tgt = lax.axis_size("tgt")
    rows = source.shape[0]
    span = rows // n_src
    n_z = n_src // 2
    z = g // 2
    core = g % 2
    partner = z * 2 + 1 - core
    left = lax.rem(t + n_tgt - 1, n_tgt)
    right = lax.rem(t + 1, n_tgt)

    def far_peer(j):
        kz = j // 2 + 1
        offset = ((kz + 1) // 2) * (2 * (kz % 2) - 1)
        return ((z + offset + n_z) % n_z) * 2 + j % 2

    pairs = ((source_hbm, source), (target_hbm, target), (src_bucket_hbm, src_bucket),
             (band_hbm, band), (route_hbm, route), (tgt_bucket_hbm, tgt_bucket))
    loads = [pltpu.make_async_copy(h, v, local_sem.at[1 + i]) for i, (h, v) in enumerate(pairs)]
    for c in loads:
        c.start()

    barrier = pltpu.get_barrier_semaphore()
    pl.semaphore_signal(barrier, inc=1, device_id=(partner, t), device_id_type=MESH)

    def greet(j, carry):
        pl.semaphore_signal(barrier, inc=1, device_id=(far_peer(j), t), device_id_type=MESH)
        return carry

    lax.fori_loop(0, n_src - 2, greet, 0)
    pl.semaphore_signal(barrier, inc=1, device_id=(g, left), device_id_type=MESH)
    pl.semaphore_signal(barrier, inc=1, device_id=(g, right), device_id_type=MESH)

    for c in loads:
        c.wait()

    where_to = route[...]
    dest = (where_to >> shift_of(rows * n_tgt)) * span + (where_to & ((1 << shift_of(span)) - 1))
    sb = src_bucket[...]
    tb = tgt_bucket[...]
    label_rows_of = {
        SRC_HI: sb >> shift_of(DIGIT), SRC_LO: sb & (DIGIT - 1), SRC_BAND: band[...],
        TGT_HI: tb >> shift_of(DIGIT), TGT_LO: tb & (DIGIT - 1),
    }
    slot = lax.broadcasted_iota(jnp.int32, (rows, rows), 0)
    lane = lax.broadcasted_iota(jnp.int32, (rows, LABEL_LANES), 1)
    onehot = (slot == dest).astype(jnp.float32)
    ident = (slot == lax.broadcasted_iota(jnp.int32, (rows, rows), 1)).astype(jnp.float32)

    def label_slab(select, kinds):
        slab = jnp.zeros((rows, LABEL_LANES), jnp.float32)
        for k in kinds:
            row = label_rows_of[k].astype(jnp.float32)
            column = jnp.sum(select * row, axis=1, keepdims=True)
            slab = jnp.where(lane == k, column, slab)
        return slab.astype(jnp.bfloat16)

    xsend[:, :features] = jnp.dot(
        onehot.astype(jnp.bfloat16), source[...],
        preferred_element_type=jnp.float32).astype(jnp.bfloat16)
    xsend[:, features:] = label_slab(onehot, (SRC_HI, SRC_LO, SRC_BAND))
    tsend[:, :features] = target[...]
    tsend[:, features:] = label_slab(ident, (TGT_HI, TGT_LO))

    pl.semaphore_wait(barrier, n_src + 1)

    t_to_right = pltpu.make_async_remote_copy(
        tsend, tl, nb_send.at[0], nb_recv.at[0], device_id=(g, right), device_id_type=MESH)
    t_to_left = pltpu.make_async_remote_copy(
        tsend, tr, nb_send.at[1], nb_recv.at[1], device_id=(g, left), device_id_type=MESH)

    def a2a_copy(peer, sender):
        return pltpu.make_async_remote_copy(
            xsend.at[pl.ds(peer * span, span)],
            xs.at[pl.ds(sender * span, span)],
            a2a_send.at[peer],
            a2a_recv.at[sender],
            device_id=(peer, t),
            device_id_type=MESH,
        )

    own = pltpu.make_async_copy(
        xsend.at[pl.ds(g * span, span)], xs.at[pl.ds(g * span, span)], local_sem.at[0])
    own.start()
    a2a_copy(partner, g).start()

    def a2a_start(j, carry):
        a2a_copy(far_peer(j), g).start()
        return carry

    lax.fori_loop(0, n_src - 2, a2a_start, 0)
    t_to_right.start()
    t_to_left.start()

    def forward(sender):
        rows_of = pl.ds(sender * span, span)
        return (
            pltpu.make_async_remote_copy(
                xs.at[rows_of], xl.at[rows_of], fw_send.at[sender], fw_recv.at[sender],
                device_id=(g, right), device_id_type=MESH),
            pltpu.make_async_remote_copy(
                xs.at[rows_of], xr.at[rows_of], fw_send.at[n_src + sender],
                fw_recv.at[n_src + sender], device_id=(g, left), device_id_type=MESH),
        )

    def arrive_and_forward(sender):
        rows_of = pl.ds(sender * span, span)
        pltpu.make_async_remote_copy(
            xsend.at[rows_of], xs.at[rows_of], a2a_send.at[sender], a2a_recv.at[sender],
            device_id=(sender, t), device_id_type=MESH).wait_recv()
        for c in forward(sender):
            c.start()

    own.wait()
    for c in forward(g):
        c.start()
    arrive_and_forward(partner)

    def a2a_arrive(j, carry):
        arrive_and_forward(far_peer(j))
        return carry

    lax.fori_loop(0, n_src - 2, a2a_arrive, 0)

    t_to_right.wait()
    t_to_left.wait()

    x_cols = xs[:, features:].astype(jnp.float32).astype(jnp.int32)
    x_bucket = x_cols[:, SRC_HI:SRC_HI + 1] * DIGIT + x_cols[:, SRC_LO:SRC_LO + 1]
    x_band = x_cols[:, SRC_BAND:SRC_BAND + 1]
    tgt_blocks = []
    for blk in (tl, tsend, tr):
        bucket_row, _ = label_rows(blk[...], features, TGT_HI, TGT_LO)
        tgt_blocks.append((blk, bucket_row, None))
    src_out[...] = softmax_read(
        xs[:, :features], x_bucket, x_band, tgt_blocks, features, scaling, True)

    a2a_copy(partner, g).wait_send()

    def a2a_sent(j, carry):
        a2a_copy(far_peer(j), g).wait_send()
        return carry

    lax.fori_loop(0, n_src - 2, a2a_sent, 0)

    def fw_done(s, carry):
        for c in forward(s):
            c.wait_send()
            c.wait_recv()
        return carry

    lax.fori_loop(0, n_src, fw_done, 0)

    y_cols = tsend[:, features:].astype(jnp.float32).astype(jnp.int32)
    y_bucket = y_cols[:, TGT_HI:TGT_HI + 1] * DIGIT + y_cols[:, TGT_LO:TGT_LO + 1]
    src_blocks = []
    for blk in (xl, xs, xr):
        bucket_row, band_row = label_rows(blk[...], features, SRC_HI, SRC_LO, SRC_BAND)
        src_blocks.append((blk, bucket_row, band_row))
    tgt_out[...] = softmax_read(
        tsend[:, :features], y_bucket, None, src_blocks, features, scaling, False)


def on_device(source, target, src_bucket, tgt_bucket, band, route):
    row_count, feature_count = source.shape
    src_count = lax.axis_size("src")
    tgt_count = lax.axis_size("tgt")
    per_peer = row_count // src_count
    scaling = 2.0 / math.sqrt(feature_count)

    width = feature_count + LABEL_LANES
    ints = [v.reshape(1, row_count) for v in (src_bucket, band, route, tgt_bucket)]

    block = jax.ShapeDtypeStruct((row_count, feature_count), jnp.float32)
    vmem = pl.BlockSpec(memory_space=pltpu.VMEM)
    return pl.pallas_call(
        functools.partial(kernel, feature_count, scaling),
        out_shape=(block, block),
        in_specs=[pl.BlockSpec(memory_space=pl.ANY)] * 6,
        out_specs=(vmem, vmem),
        scratch_shapes=[pltpu.VMEM((row_count, feature_count), jnp.bfloat16)] * 2
        + [pltpu.VMEM((1, row_count), jnp.int32)] * 4
        + [pltpu.VMEM((row_count, width), jnp.bfloat16)] * 7
        + [
            pltpu.SemaphoreType.DMA((src_count,)),
            pltpu.SemaphoreType.DMA((src_count,)),
            pltpu.SemaphoreType.DMA((2 * src_count,)),
            pltpu.SemaphoreType.DMA((2 * src_count,)),
            pltpu.SemaphoreType.DMA((2,)),
            pltpu.SemaphoreType.DMA((2,)),
            pltpu.SemaphoreType.DMA((7,)),
        ],
        compiler_params=pltpu.CompilerParams(collective_id=0, has_side_effects=True),
    )(source, target, *ints)


def solution(mesh):
    placed = (
        P(("src", "tgt"), None),
        P(("src", "tgt"), None),
        P(("src", "tgt")),
        P(("src", "tgt")),
        P(("src", "tgt")),
        P(("src", "tgt")),
    )
    return jax.shard_map(
        on_device,
        mesh=mesh,
        in_specs=placed,
        out_specs=(P(("src", "tgt"), None), P(("src", "tgt"), None)),
        check_vma=False,
    )
```

```python
import functools
import math

import jax
import jax.numpy as jnp
from jax import lax
from jax.experimental import pallas as pl
from jax.experimental.pallas import tpu as pltpu
from jax.sharding import PartitionSpec as P

lowest = -1e30
MESH = pl.DeviceIdType.MESH
LABEL_LANES = 128
DIGIT = 64
SRC_HI, SRC_LO, SRC_BAND, TGT_HI, TGT_LO = 0, 1, 2, 4, 5


def softmax_read(main, main_bucket, band_col, others, features, scaling, band_of_rows):
    scores, masks = [], []
    for blk, bucket_row, band_row in others:
        s = lax.dot_general(
            main, blk[:, :features], (((1,), (1,)), ((), ())),
            preferred_element_type=jnp.float32) * scaling
        band = band_col if band_of_rows else band_row
        ok = (jnp.abs(main_bucket - bucket_row) <= band) & (
            (main_bucket >> 7) == (bucket_row >> 7))
        scores.append(jnp.where(ok, s, lowest))
        masks.append(ok)
    top = functools.reduce(jnp.maximum, [jnp.max(s, axis=1, keepdims=True) for s in scores])
    total = jnp.zeros_like(top)
    read = jnp.zeros((main.shape[0], features), jnp.float32)
    for s, ok, (blk, _, _) in zip(scores, masks, others):
        w = jnp.where(ok, jnp.exp(s - top), 0.0)
        total = total + jnp.sum(w, axis=1, keepdims=True)
        read = read + jnp.dot(w.astype(jnp.bfloat16), blk[:, :features],
                              preferred_element_type=jnp.float32)
    return read / total


def label_rows(blk, features, hi, lo, band=None):
    slab = blk[:, features:].astype(jnp.float32).T.astype(jnp.int32)
    bucket = slab[hi:hi + 1, :] * DIGIT + slab[lo:lo + 1, :]
    return bucket, (slab[band:band + 1, :] if band is not None else None)


def shift_of(divisor):
    assert divisor & (divisor - 1) == 0
    return divisor.bit_length() - 1


def kernel(features, scaling, source_hbm, target_hbm, src_bucket_hbm, band_hbm, route_hbm,
           tgt_bucket_hbm, src_out, tgt_out,
           source, target, src_bucket, band, route, tgt_bucket, xsend, tsend, xs, xl, xr, tl, tr,
           a2a_send, a2a_recv, fw_send, fw_recv, nb_send, nb_recv, local_sem):
    g = lax.axis_index("src")
    t = lax.axis_index("tgt")
    n_src = lax.axis_size("src")
    n_tgt = lax.axis_size("tgt")
    rows = source.shape[0]
    span = rows // n_src
    n_z = n_src // 2
    z = g // 2
    core = g % 2
    partner = z * 2 + 1 - core
    left = lax.rem(t + n_tgt - 1, n_tgt)
    right = lax.rem(t + 1, n_tgt)

    def far_peer(j):
        kz = j // 2 + 1
        offset = ((kz + 1) // 2) * (2 * (kz % 2) - 1)
        return ((z + offset + n_z) % n_z) * 2 + j % 2

    pairs = ((source_hbm, source), (target_hbm, target), (src_bucket_hbm, src_bucket),
             (band_hbm, band), (route_hbm, route), (tgt_bucket_hbm, tgt_bucket))
    loads = [pltpu.make_async_copy(h, v, local_sem.at[1 + i]) for i, (h, v) in enumerate(pairs)]
    for c in loads:
        c.start()

    barrier = pltpu.get_barrier_semaphore()

    def greet(j, carry):
        pl.semaphore_signal(
            barrier, inc=1, device_id=(far_peer(n_src - 3 - j), t), device_id_type=MESH)
        return carry

    lax.fori_loop(0, n_src - 2, greet, 0)
    pl.semaphore_signal(barrier, inc=1, device_id=(g, left), device_id_type=MESH)
    pl.semaphore_signal(barrier, inc=1, device_id=(g, right), device_id_type=MESH)
    pl.semaphore_signal(barrier, inc=1, device_id=(partner, t), device_id_type=MESH)

    for c in loads:
        c.wait()

    where_to = route[...]
    dest = (where_to >> shift_of(rows * n_tgt)) * span + (where_to & ((1 << shift_of(span)) - 1))
    sb = src_bucket[...]
    tb = tgt_bucket[...]
    label_rows_of = {
        SRC_HI: sb >> shift_of(DIGIT), SRC_LO: sb & (DIGIT - 1), SRC_BAND: band[...],
        TGT_HI: tb >> shift_of(DIGIT), TGT_LO: tb & (DIGIT - 1),
    }
    slot = lax.broadcasted_iota(jnp.int32, (rows, rows), 0)
    lane = lax.broadcasted_iota(jnp.int32, (rows, LABEL_LANES), 1)
    onehot = (slot == dest).astype(jnp.float32)
    ident = (slot == lax.broadcasted_iota(jnp.int32, (rows, rows), 1)).astype(jnp.float32)

    def label_slab(select, kinds):
        slab = jnp.zeros((rows, LABEL_LANES), jnp.float32)
        for k in kinds:
            row = label_rows_of[k].astype(jnp.float32)
            column = jnp.sum(select * row, axis=1, keepdims=True)
            slab = jnp.where(lane == k, column, slab)
        return slab.astype(jnp.bfloat16)

    xsend[:, :features] = jnp.dot(
        onehot.astype(jnp.bfloat16), source[...],
        preferred_element_type=jnp.float32).astype(jnp.bfloat16)
    xsend[:, features:] = label_slab(onehot, (SRC_HI, SRC_LO, SRC_BAND))
    tsend[:, :features] = target[...]
    tsend[:, features:] = label_slab(ident, (TGT_HI, TGT_LO))

    pl.semaphore_wait(barrier, n_src + 1)

    t_to_right = pltpu.make_async_remote_copy(
        tsend, tl, nb_send.at[0], nb_recv.at[0], device_id=(g, right), device_id_type=MESH)
    t_to_left = pltpu.make_async_remote_copy(
        tsend, tr, nb_send.at[1], nb_recv.at[1], device_id=(g, left), device_id_type=MESH)

    def a2a_copy(peer, sender):
        return pltpu.make_async_remote_copy(
            xsend.at[pl.ds(peer * span, span)],
            xs.at[pl.ds(sender * span, span)],
            a2a_send.at[peer],
            a2a_recv.at[sender],
            device_id=(peer, t),
            device_id_type=MESH,
        )

    own = pltpu.make_async_copy(
        xsend.at[pl.ds(g * span, span)], xs.at[pl.ds(g * span, span)], local_sem.at[0])
    own.start()
    a2a_copy(partner, g).start()

    def a2a_start(j, carry):
        a2a_copy(far_peer(j), g).start()
        return carry

    lax.fori_loop(0, n_src - 2, a2a_start, 0)
    t_to_right.start()
    t_to_left.start()

    def forward(sender):
        rows_of = pl.ds(sender * span, span)
        return (
            pltpu.make_async_remote_copy(
                xs.at[rows_of], xl.at[rows_of], fw_send.at[sender], fw_recv.at[sender],
                device_id=(g, right), device_id_type=MESH),
            pltpu.make_async_remote_copy(
                xs.at[rows_of], xr.at[rows_of], fw_send.at[n_src + sender],
                fw_recv.at[n_src + sender], device_id=(g, left), device_id_type=MESH),
        )

    def arrive_and_forward(sender):
        rows_of = pl.ds(sender * span, span)
        pltpu.make_async_remote_copy(
            xsend.at[rows_of], xs.at[rows_of], a2a_send.at[sender], a2a_recv.at[sender],
            device_id=(sender, t), device_id_type=MESH).wait_recv()
        for c in forward(sender):
            c.start()

    own.wait()
    for c in forward(g):
        c.start()
    arrive_and_forward(partner)

    def a2a_arrive(j, carry):
        arrive_and_forward(far_peer(j))
        return carry

    lax.fori_loop(0, n_src - 2, a2a_arrive, 0)

    t_to_right.wait()
    t_to_left.wait()

    x_cols = xs[:, features:].astype(jnp.float32).astype(jnp.int32)
    x_bucket = x_cols[:, SRC_HI:SRC_HI + 1] * DIGIT + x_cols[:, SRC_LO:SRC_LO + 1]
    x_band = x_cols[:, SRC_BAND:SRC_BAND + 1]
    tgt_blocks = []
    for blk in (tl, tsend, tr):
        bucket_row, _ = label_rows(blk[...], features, TGT_HI, TGT_LO)
        tgt_blocks.append((blk, bucket_row, None))
    src_out[...] = softmax_read(
        xs[:, :features], x_bucket, x_band, tgt_blocks, features, scaling, True)

    a2a_copy(partner, g).wait_send()

    def a2a_sent(j, carry):
        a2a_copy(far_peer(j), g).wait_send()
        return carry

    lax.fori_loop(0, n_src - 2, a2a_sent, 0)

    def fw_done(s, carry):
        for c in forward(s):
            c.wait_send()
            c.wait_recv()
        return carry

    lax.fori_loop(0, n_src, fw_done, 0)

    y_cols = tsend[:, features:].astype(jnp.float32).astype(jnp.int32)
    y_bucket = y_cols[:, TGT_HI:TGT_HI + 1] * DIGIT + y_cols[:, TGT_LO:TGT_LO + 1]
    src_blocks = []
    for blk in (xl, xs, xr):
        bucket_row, band_row = label_rows(blk[...], features, SRC_HI, SRC_LO, SRC_BAND)
        src_blocks.append((blk, bucket_row, band_row))
    tgt_out[...] = softmax_read(
        tsend[:, :features], y_bucket, None, src_blocks, features, scaling, False)


def on_device(source, target, src_bucket, tgt_bucket, band, route):
    row_count, feature_count = source.shape
    src_count = lax.axis_size("src")
    tgt_count = lax.axis_size("tgt")
    per_peer = row_count // src_count
    scaling = 2.0 / math.sqrt(feature_count)

    width = feature_count + LABEL_LANES
    ints = [v.reshape(1, row_count) for v in (src_bucket, band, route, tgt_bucket)]

    block = jax.ShapeDtypeStruct((row_count, feature_count), jnp.float32)
    vmem = pl.BlockSpec(memory_space=pltpu.VMEM)
    return pl.pallas_call(
        functools.partial(kernel, feature_count, scaling),
        out_shape=(block, block),
        in_specs=[pl.BlockSpec(memory_space=pl.ANY)] * 6,
        out_specs=(vmem, vmem),
        scratch_shapes=[pltpu.VMEM((row_count, feature_count), jnp.bfloat16)] * 2
        + [pltpu.VMEM((1, row_count), jnp.int32)] * 4
        + [pltpu.VMEM((row_count, width), jnp.bfloat16)] * 7
        + [
            pltpu.SemaphoreType.DMA((src_count,)),
            pltpu.SemaphoreType.DMA((src_count,)),
            pltpu.SemaphoreType.DMA((2 * src_count,)),
            pltpu.SemaphoreType.DMA((2 * src_count,)),
            pltpu.SemaphoreType.DMA((2,)),
            pltpu.SemaphoreType.DMA((2,)),
            pltpu.SemaphoreType.DMA((7,)),
        ],
        compiler_params=pltpu.CompilerParams(collective_id=0, has_side_effects=True),
    )(source, target, *ints)


def solution(mesh):
    placed = (
        P(("src", "tgt"), None),
        P(("src", "tgt"), None),
        P(("src", "tgt")),
        P(("src", "tgt")),
        P(("src", "tgt")),
        P(("src", "tgt")),
    )
    return jax.shard_map(
        on_device,
        mesh=mesh,
        in_specs=placed,
        out_specs=(P(("src", "tgt"), None), P(("src", "tgt"), None)),
        check_vma=False,
    )
```

```python
import functools
import math

import jax
import jax.numpy as jnp
from jax import lax
from jax.experimental import pallas as pl
from jax.experimental.pallas import tpu as pltpu
from jax.sharding import PartitionSpec as P

lowest = -1e30
MESH = pl.DeviceIdType.MESH
LABEL_LANES = 128
DIGIT = 64
SRC_HI, SRC_LO, SRC_BAND, TGT_HI, TGT_LO = 0, 1, 2, 4, 5


def softmax_read(main, main_bucket, band_col, others, features, scaling, band_of_rows):
    scores, masks = [], []
    for blk, bucket_row, band_row in others:
        s = lax.dot_general(
            main, blk[:, :features], (((1,), (1,)), ((), ())),
            preferred_element_type=jnp.float32) * scaling
        band = band_col if band_of_rows else band_row
        ok = (jnp.abs(main_bucket - bucket_row) <= band) & (
            (main_bucket >> 7) == (bucket_row >> 7))
        scores.append(jnp.where(ok, s, lowest))
        masks.append(ok)
    top = functools.reduce(jnp.maximum, [jnp.max(s, axis=1, keepdims=True) for s in scores])
    total = jnp.zeros_like(top)
    read = jnp.zeros((main.shape[0], features), jnp.float32)
    for s, ok, (blk, _, _) in zip(scores, masks, others):
        w = jnp.where(ok, jnp.exp(s - top), 0.0)
        total = total + jnp.sum(w, axis=1, keepdims=True)
        read = read + jnp.dot(w.astype(jnp.bfloat16), blk[:, :features],
                              preferred_element_type=jnp.float32)
    return read / total


def label_rows(blk, features, hi, lo, band=None):
    slab = blk[:, features:].astype(jnp.float32).T.astype(jnp.int32)
    bucket = slab[hi:hi + 1, :] * DIGIT + slab[lo:lo + 1, :]
    return bucket, (slab[band:band + 1, :] if band is not None else None)


def shift_of(divisor):
    assert divisor & (divisor - 1) == 0
    return divisor.bit_length() - 1


def kernel(features, scaling, source_hbm, target_hbm, src_bucket_hbm, band_hbm, route_hbm,
           tgt_bucket_hbm, src_out, tgt_out,
           source, target, src_bucket, band, route, tgt_bucket, xsend, tsend, xs, xl, xr, tl, tr,
           a2a_send, a2a_recv, fw_send, fw_recv, nb_send, nb_recv, local_sem):
    g = lax.axis_index("src")
    t = lax.axis_index("tgt")
    n_src = lax.axis_size("src")
    n_tgt = lax.axis_size("tgt")
    rows = source.shape[0]
    span = rows // n_src
    n_z = n_src // 2
    z = g // 2
    core = g % 2
    partner = z * 2 + 1 - core
    left = lax.rem(t + n_tgt - 1, n_tgt)
    right = lax.rem(t + 1, n_tgt)

    def far_peer(j):
        kz = j // 2 + 1
        offset = ((kz + 1) // 2) * (2 * (kz % 2) - 1)
        return ((z + offset + n_z) % n_z) * 2 + j % 2

    pairs = ((source_hbm, source), (target_hbm, target), (src_bucket_hbm, src_bucket),
             (band_hbm, band), (route_hbm, route), (tgt_bucket_hbm, tgt_bucket))
    loads = [pltpu.make_async_copy(h, v, local_sem.at[1 + i]) for i, (h, v) in enumerate(pairs)]
    for c in loads:
        c.start()

    barrier = pltpu.get_barrier_semaphore()

    def greet(j, carry):
        pl.semaphore_signal(
            barrier, inc=1, device_id=(far_peer(n_src - 3 - j), t), device_id_type=MESH)
        return carry

    lax.fori_loop(0, n_src - 2, greet, 0)
    pl.semaphore_signal(barrier, inc=1, device_id=(g, left), device_id_type=MESH)
    pl.semaphore_signal(barrier, inc=1, device_id=(g, right), device_id_type=MESH)
    pl.semaphore_signal(barrier, inc=1, device_id=(partner, t), device_id_type=MESH)

    for c in loads:
        c.wait()

    where_to = route[...]
    dest = (where_to >> shift_of(rows * n_tgt)) * span + (where_to & ((1 << shift_of(span)) - 1))
    sb = src_bucket[...]
    tb = tgt_bucket[...]
    label_rows_of = {
        SRC_HI: sb >> shift_of(DIGIT), SRC_LO: sb & (DIGIT - 1), SRC_BAND: band[...],
        TGT_HI: tb >> shift_of(DIGIT), TGT_LO: tb & (DIGIT - 1),
    }
    slot = lax.broadcasted_iota(jnp.int32, (rows, rows), 0)
    lane = lax.broadcasted_iota(jnp.int32, (rows, LABEL_LANES), 1)
    onehot = (slot == dest).astype(jnp.float32)
    ident = (slot == lax.broadcasted_iota(jnp.int32, (rows, rows), 1)).astype(jnp.float32)

    def label_slab(select, kinds):
        slab = jnp.zeros((rows, LABEL_LANES), jnp.float32)
        for k in kinds:
            row = label_rows_of[k].astype(jnp.float32)
            column = jnp.sum(select * row, axis=1, keepdims=True)
            slab = jnp.where(lane == k, column, slab)
        return slab.astype(jnp.bfloat16)

    xsend[:, :features] = jnp.dot(
        onehot.astype(jnp.bfloat16), source[...],
        preferred_element_type=jnp.float32).astype(jnp.bfloat16)
    xsend[:, features:] = label_slab(onehot, (SRC_HI, SRC_LO, SRC_BAND))
    tsend[:, :features] = target[...]
    tsend[:, features:] = label_slab(ident, (TGT_HI, TGT_LO))

    pl.semaphore_wait(barrier, n_src + 1)

    t_to_right = pltpu.make_async_remote_copy(
        tsend, tl, nb_send.at[0], nb_recv.at[0], device_id=(g, right), device_id_type=MESH)
    t_to_left = pltpu.make_async_remote_copy(
        tsend, tr, nb_send.at[1], nb_recv.at[1], device_id=(g, left), device_id_type=MESH)

    def a2a_copy(peer, sender):
        return pltpu.make_async_remote_copy(
            xsend.at[pl.ds(peer * span, span)],
            xs.at[pl.ds(sender * span, span)],
            a2a_send.at[peer],
            a2a_recv.at[sender],
            device_id=(peer, t),
            device_id_type=MESH,
        )

    own = pltpu.make_async_copy(
        xsend.at[pl.ds(g * span, span)], xs.at[pl.ds(g * span, span)], local_sem.at[0])
    own.start()
    a2a_copy(partner, g).start()

    def a2a_start(j, carry):
        a2a_copy(far_peer(j), g).start()
        return carry

    lax.fori_loop(0, n_src - 2, a2a_start, 0)
    t_to_right.start()
    t_to_left.start()

    def forward(sender):
        rows_of = pl.ds(sender * span, span)
        return (
            pltpu.make_async_remote_copy(
                xs.at[rows_of], xl.at[rows_of], fw_send.at[sender], fw_recv.at[sender],
                device_id=(g, right), device_id_type=MESH),
            pltpu.make_async_remote_copy(
                xs.at[rows_of], xr.at[rows_of], fw_send.at[n_src + sender],
                fw_recv.at[n_src + sender], device_id=(g, left), device_id_type=MESH),
        )

    def arrive_and_forward(sender):
        rows_of = pl.ds(sender * span, span)
        pltpu.make_async_remote_copy(
            xsend.at[rows_of], xs.at[rows_of], a2a_send.at[sender], a2a_recv.at[sender],
            device_id=(sender, t), device_id_type=MESH).wait_recv()
        for c in forward(sender):
            c.start()

    own.wait()
    for c in forward(g):
        c.start()
    arrive_and_forward(partner)

    def a2a_arrive(j, carry):
        arrive_and_forward(far_peer(j))
        return carry

    lax.fori_loop(0, n_src - 2, a2a_arrive, 0)

    t_to_right.wait()
    t_to_left.wait()

    x_cols = xs[:, features:].astype(jnp.float32).astype(jnp.int32)
    x_bucket = x_cols[:, SRC_HI:SRC_HI + 1] * DIGIT + x_cols[:, SRC_LO:SRC_LO + 1]
    x_band = x_cols[:, SRC_BAND:SRC_BAND + 1]
    tgt_blocks = []
    for blk in (tl, tsend, tr):
        bucket_row, _ = label_rows(blk[...], features, TGT_HI, TGT_LO)
        tgt_blocks.append((blk, bucket_row, None))
    src_out[...] = softmax_read(
        xs[:, :features], x_bucket, x_band, tgt_blocks, features, scaling, True)

    a2a_copy(partner, g).wait_send()

    def a2a_sent(j, carry):
        a2a_copy(far_peer(j), g).wait_send()
        return carry

    lax.fori_loop(0, n_src - 2, a2a_sent, 0)

    def fw_done(s, carry):
        for c in forward(s):
            c.wait_send()
            c.wait_recv()
        return carry

    lax.fori_loop(0, n_src, fw_done, 0)

    y_cols = tsend[:, features:].astype(jnp.float32).astype(jnp.int32)
    y_bucket = y_cols[:, TGT_HI:TGT_HI + 1] * DIGIT + y_cols[:, TGT_LO:TGT_LO + 1]
    src_blocks = []
    for blk in (xl, xs, xr):
        bucket_row, band_row = label_rows(blk[...], features, SRC_HI, SRC_LO, SRC_BAND)
        src_blocks.append((blk, bucket_row, band_row))
    tgt_out[...] = softmax_read(
        tsend[:, :features], y_bucket, None, src_blocks, features, scaling, False)


def write_kernel(src_in, tgt_in, src_res, tgt_res, sems):
    copies = [pltpu.make_async_copy(src_in, src_res, sems.at[0]),
              pltpu.make_async_copy(tgt_in, tgt_res, sems.at[1])]
    for c in copies:
        c.start()
    for c in copies:
        c.wait()


def write_out(src_read, tgt_read):
    return pl.pallas_call(
        write_kernel,
        out_shape=(jax.ShapeDtypeStruct(src_read.shape, src_read.dtype),
                   jax.ShapeDtypeStruct(tgt_read.shape, tgt_read.dtype)),
        in_specs=[pl.BlockSpec(memory_space=pltpu.VMEM)] * 2,
        out_specs=(pl.BlockSpec(memory_space=pl.ANY),) * 2,
        scratch_shapes=[pltpu.SemaphoreType.DMA((2,))],
    )(src_read, tgt_read)


def on_device(source, target, src_bucket, tgt_bucket, band, route):
    row_count, feature_count = source.shape
    src_count = lax.axis_size("src")
    tgt_count = lax.axis_size("tgt")
    per_peer = row_count // src_count
    scaling = 2.0 / math.sqrt(feature_count)

    width = feature_count + LABEL_LANES
    ints = [v.reshape(1, row_count) for v in (src_bucket, band, route, tgt_bucket)]

    block = jax.ShapeDtypeStruct((row_count, feature_count), jnp.float32)
    vmem = pl.BlockSpec(memory_space=pltpu.VMEM)
    reads = pl.pallas_call(
        functools.partial(kernel, feature_count, scaling),
        out_shape=(block, block),
        in_specs=[pl.BlockSpec(memory_space=pl.ANY)] * 6,
        out_specs=(vmem, vmem),
        scratch_shapes=[pltpu.VMEM((row_count, feature_count), jnp.bfloat16)] * 2
        + [pltpu.VMEM((1, row_count), jnp.int32)] * 4
        + [pltpu.VMEM((row_count, width), jnp.bfloat16)] * 7
        + [
            pltpu.SemaphoreType.DMA((src_count,)),
            pltpu.SemaphoreType.DMA((src_count,)),
            pltpu.SemaphoreType.DMA((2 * src_count,)),
            pltpu.SemaphoreType.DMA((2 * src_count,)),
            pltpu.SemaphoreType.DMA((2,)),
            pltpu.SemaphoreType.DMA((2,)),
            pltpu.SemaphoreType.DMA((7,)),
        ],
        compiler_params=pltpu.CompilerParams(collective_id=0, has_side_effects=True),
    )(source, target, *ints)
    return write_out(*reads)


def solution(mesh):
    placed = (
        P(("src", "tgt"), None),
        P(("src", "tgt"), None),
        P(("src", "tgt")),
        P(("src", "tgt")),
        P(("src", "tgt")),
        P(("src", "tgt")),
    )
    return jax.shard_map(
        on_device,
        mesh=mesh,
        in_specs=placed,
        out_specs=(P(("src", "tgt"), None), P(("src", "tgt"), None)),
        check_vma=False,
    )
```

```python
import functools
import math

import jax
import jax.numpy as jnp
from jax import lax
from jax.experimental import pallas as pl
from jax.experimental.pallas import tpu as pltpu
from jax.sharding import PartitionSpec as P

lowest = -1e30
MESH = pl.DeviceIdType.MESH
LABEL_LANES = 128
DIGIT = 64
SRC_HI, SRC_LO, SRC_BAND, TGT_HI, TGT_LO = 0, 1, 2, 4, 5


def softmax_read(main, main_bucket, band_col, others, features, scaling, band_of_rows):
    scores, masks = [], []
    for blk, bucket_row, band_row in others:
        s = lax.dot_general(
            main, blk[:, :features], (((1,), (1,)), ((), ())),
            preferred_element_type=jnp.float32) * scaling
        band = band_col if band_of_rows else band_row
        ok = (jnp.abs(main_bucket - bucket_row) <= band) & (
            (main_bucket >> 7) == (bucket_row >> 7))
        scores.append(jnp.where(ok, s, lowest))
        masks.append(ok)
    top = functools.reduce(jnp.maximum, [jnp.max(s, axis=1, keepdims=True) for s in scores])
    total = jnp.zeros_like(top)
    read = jnp.zeros((main.shape[0], features), jnp.float32)
    for s, ok, (blk, _, _) in zip(scores, masks, others):
        w = jnp.where(ok, jnp.exp(s - top), 0.0)
        total = total + jnp.sum(w, axis=1, keepdims=True)
        read = read + jnp.dot(w.astype(jnp.bfloat16), blk[:, :features],
                              preferred_element_type=jnp.float32)
    return read / total


def label_rows(blk, features, hi, lo, band=None):
    slab = blk[:, features:].astype(jnp.float32).T.astype(jnp.int32)
    bucket = slab[hi:hi + 1, :] * DIGIT + slab[lo:lo + 1, :]
    return bucket, (slab[band:band + 1, :] if band is not None else None)


def shift_of(divisor):
    assert divisor & (divisor - 1) == 0
    return divisor.bit_length() - 1


def kernel(features, scaling, source_hbm, target_hbm, src_bucket_hbm, band_hbm, route_hbm,
           tgt_bucket_hbm, src_out, tgt_out,
           source, target, src_bucket, band, route, tgt_bucket, xsend, tsend, xs, xl, xr, tl, tr,
           a2a_send, a2a_recv, fw_send, fw_recv, nb_send, nb_recv, local_sem):
    g = lax.axis_index("src")
    t = lax.axis_index("tgt")
    n_src = lax.axis_size("src")
    n_tgt = lax.axis_size("tgt")
    rows = source.shape[0]
    span = rows // n_src
    n_z = n_src // 2
    z = g // 2
    core = g % 2
    partner = z * 2 + 1 - core
    left = lax.rem(t + n_tgt - 1, n_tgt)
    right = lax.rem(t + 1, n_tgt)

    def far_peer(j):
        kz = j // 2 + 1
        offset = ((kz + 1) // 2) * (2 * (kz % 2) - 1)
        return ((z + offset + n_z) % n_z) * 2 + j % 2

    pairs = ((source_hbm, source), (target_hbm, target), (src_bucket_hbm, src_bucket),
             (band_hbm, band), (route_hbm, route), (tgt_bucket_hbm, tgt_bucket))
    loads = [pltpu.make_async_copy(h, v, local_sem.at[1 + i]) for i, (h, v) in enumerate(pairs)]
    for c in loads:
        c.start()

    barrier = pltpu.get_barrier_semaphore()

    def greet(j, carry):
        pl.semaphore_signal(
            barrier, inc=1, device_id=(far_peer(n_src - 3 - j), t), device_id_type=MESH)
        return carry

    lax.fori_loop(0, n_src - 2, greet, 0)
    pl.semaphore_signal(barrier, inc=1, device_id=(g, left), device_id_type=MESH)
    pl.semaphore_signal(barrier, inc=1, device_id=(g, right), device_id_type=MESH)
    pl.semaphore_signal(barrier, inc=1, device_id=(partner, t), device_id_type=MESH)

    for c in loads:
        c.wait()

    where_to = route[...]
    dest = (where_to >> shift_of(rows * n_tgt)) * span + (where_to & ((1 << shift_of(span)) - 1))
    sb = src_bucket[...]
    tb = tgt_bucket[...]
    label_rows_of = {
        SRC_HI: sb >> shift_of(DIGIT), SRC_LO: sb & (DIGIT - 1), SRC_BAND: band[...],
        TGT_HI: tb >> shift_of(DIGIT), TGT_LO: tb & (DIGIT - 1),
    }
    slot = lax.broadcasted_iota(jnp.int32, (rows, rows), 0)
    lane = lax.broadcasted_iota(jnp.int32, (rows, LABEL_LANES), 1)
    onehot = (slot == dest).astype(jnp.float32)
    ident = (slot == lax.broadcasted_iota(jnp.int32, (rows, rows), 1)).astype(jnp.float32)

    def label_slab(select, kinds):
        slab = jnp.zeros((rows, LABEL_LANES), jnp.float32)
        for k in kinds:
            row = label_rows_of[k].astype(jnp.float32)
            column = jnp.sum(select * row, axis=1, keepdims=True)
            slab = jnp.where(lane == k, column, slab)
        return slab.astype(jnp.bfloat16)

    xsend[:, :features] = jnp.dot(
        onehot.astype(jnp.bfloat16), source[...],
        preferred_element_type=jnp.float32).astype(jnp.bfloat16)
    xsend[:, features:] = label_slab(onehot, (SRC_HI, SRC_LO, SRC_BAND))
    tsend[:, :features] = target[...]
    tsend[:, features:] = label_slab(ident, (TGT_HI, TGT_LO))

    pl.semaphore_wait(barrier, n_src + 1)

    t_to_right = pltpu.make_async_remote_copy(
        tsend, tl, nb_send.at[0], nb_recv.at[0], device_id=(g, right), device_id_type=MESH)
    t_to_left = pltpu.make_async_remote_copy(
        tsend, tr, nb_send.at[1], nb_recv.at[1], device_id=(g, left), device_id_type=MESH)

    def a2a_copy(peer, sender):
        return pltpu.make_async_remote_copy(
            xsend.at[pl.ds(peer * span, span)],
            xs.at[pl.ds(sender * span, span)],
            a2a_send.at[peer],
            a2a_recv.at[sender],
            device_id=(peer, t),
            device_id_type=MESH,
        )

    own = pltpu.make_async_copy(
        xsend.at[pl.ds(g * span, span)], xs.at[pl.ds(g * span, span)], local_sem.at[0])
    own.start()
    a2a_copy(partner, g).start()

    def a2a_start(j, carry):
        a2a_copy(far_peer(j), g).start()
        return carry

    lax.fori_loop(0, n_src - 2, a2a_start, 0)
    t_to_right.start()
    t_to_left.start()

    def forward(sender):
        rows_of = pl.ds(sender * span, span)
        return (
            pltpu.make_async_remote_copy(
                xs.at[rows_of], xl.at[rows_of], fw_send.at[sender], fw_recv.at[sender],
                device_id=(g, right), device_id_type=MESH),
            pltpu.make_async_remote_copy(
                xs.at[rows_of], xr.at[rows_of], fw_send.at[n_src + sender],
                fw_recv.at[n_src + sender], device_id=(g, left), device_id_type=MESH),
        )

    def arrive_and_forward(sender):
        rows_of = pl.ds(sender * span, span)
        pltpu.make_async_remote_copy(
            xsend.at[rows_of], xs.at[rows_of], a2a_send.at[sender], a2a_recv.at[sender],
            device_id=(sender, t), device_id_type=MESH).wait_recv()
        for c in forward(sender):
            c.start()

    own.wait()
    for c in forward(g):
        c.start()
    arrive_and_forward(partner)

    def a2a_arrive(j, carry):
        arrive_and_forward(far_peer(j))
        return carry

    lax.fori_loop(0, n_src - 2, a2a_arrive, 0)

    t_to_right.wait()
    t_to_left.wait()

    x_cols = xs[:, features:].astype(jnp.float32).astype(jnp.int32)
    x_bucket = x_cols[:, SRC_HI:SRC_HI + 1] * DIGIT + x_cols[:, SRC_LO:SRC_LO + 1]
    x_band = x_cols[:, SRC_BAND:SRC_BAND + 1]
    tgt_blocks = []
    for blk in (tl, tsend, tr):
        bucket_row, _ = label_rows(blk[...], features, TGT_HI, TGT_LO)
        tgt_blocks.append((blk, bucket_row, None))
    src_out[...] = softmax_read(
        xs[:, :features], x_bucket, x_band, tgt_blocks, features, scaling, True)

    a2a_copy(partner, g).wait_send()

    def a2a_sent(j, carry):
        a2a_copy(far_peer(j), g).wait_send()
        return carry

    lax.fori_loop(0, n_src - 2, a2a_sent, 0)

    def fw_arrived(s, carry):
        for c in forward(s):
            c.wait_recv()
        return carry

    lax.fori_loop(0, n_src, fw_arrived, 0)

    y_cols = tsend[:, features:].astype(jnp.float32).astype(jnp.int32)
    y_bucket = y_cols[:, TGT_HI:TGT_HI + 1] * DIGIT + y_cols[:, TGT_LO:TGT_LO + 1]
    src_blocks = []
    for blk in (xl, xs, xr):
        bucket_row, band_row = label_rows(blk[...], features, SRC_HI, SRC_LO, SRC_BAND)
        src_blocks.append((blk, bucket_row, band_row))
    tgt_out[...] = softmax_read(
        tsend[:, :features], y_bucket, None, src_blocks, features, scaling, False)

    def fw_sent(s, carry):
        for c in forward(s):
            c.wait_send()
        return carry

    lax.fori_loop(0, n_src, fw_sent, 0)


def write_kernel(src_in, tgt_in, src_res, tgt_res, sems):
    copies = [pltpu.make_async_copy(src_in, src_res, sems.at[0]),
              pltpu.make_async_copy(tgt_in, tgt_res, sems.at[1])]
    for c in copies:
        c.start()
    for c in copies:
        c.wait()


def write_out(src_read, tgt_read):
    return pl.pallas_call(
        write_kernel,
        out_shape=(jax.ShapeDtypeStruct(src_read.shape, src_read.dtype),
                   jax.ShapeDtypeStruct(tgt_read.shape, tgt_read.dtype)),
        in_specs=[pl.BlockSpec(memory_space=pltpu.VMEM)] * 2,
        out_specs=(pl.BlockSpec(memory_space=pl.ANY),) * 2,
        scratch_shapes=[pltpu.SemaphoreType.DMA((2,))],
    )(src_read, tgt_read)


def on_device(source, target, src_bucket, tgt_bucket, band, route):
    row_count, feature_count = source.shape
    src_count = lax.axis_size("src")
    tgt_count = lax.axis_size("tgt")
    per_peer = row_count // src_count
    scaling = 2.0 / math.sqrt(feature_count)

    width = feature_count + LABEL_LANES
    ints = [v.reshape(1, row_count) for v in (src_bucket, band, route, tgt_bucket)]

    block = jax.ShapeDtypeStruct((row_count, feature_count), jnp.float32)
    vmem = pl.BlockSpec(memory_space=pltpu.VMEM)
    reads = pl.pallas_call(
        functools.partial(kernel, feature_count, scaling),
        out_shape=(block, block),
        in_specs=[pl.BlockSpec(memory_space=pl.ANY)] * 6,
        out_specs=(vmem, vmem),
        scratch_shapes=[pltpu.VMEM((row_count, feature_count), jnp.bfloat16)] * 2
        + [pltpu.VMEM((1, row_count), jnp.int32)] * 4
        + [pltpu.VMEM((row_count, width), jnp.bfloat16)] * 7
        + [
            pltpu.SemaphoreType.DMA((src_count,)),
            pltpu.SemaphoreType.DMA((src_count,)),
            pltpu.SemaphoreType.DMA((2 * src_count,)),
            pltpu.SemaphoreType.DMA((2 * src_count,)),
            pltpu.SemaphoreType.DMA((2,)),
            pltpu.SemaphoreType.DMA((2,)),
            pltpu.SemaphoreType.DMA((7,)),
        ],
        compiler_params=pltpu.CompilerParams(collective_id=0, has_side_effects=True),
    )(source, target, *ints)
    return write_out(*reads)


def solution(mesh):
    placed = (
        P(("src", "tgt"), None),
        P(("src", "tgt"), None),
        P(("src", "tgt")),
        P(("src", "tgt")),
        P(("src", "tgt")),
        P(("src", "tgt")),
    )
    return jax.shard_map(
        on_device,
        mesh=mesh,
        in_specs=placed,
        out_specs=(P(("src", "tgt"), None), P(("src", "tgt"), None)),
        check_vma=False,
    )
```

```python
import functools
import math

import jax
import jax.numpy as jnp
from jax import lax
from jax.experimental import pallas as pl
from jax.experimental.pallas import tpu as pltpu
from jax.sharding import PartitionSpec as P

lowest = -1e30
MESH = pl.DeviceIdType.MESH
LABEL_LANES = 128
DIGIT = 64
SRC_HI, SRC_LO, SRC_BAND, TGT_HI, TGT_LO = 0, 1, 2, 4, 5


def masked_scores(main, main_bucket, band_col, blk, bucket_row, band_row, features, scaling):
    s = lax.dot_general(
        main, blk[:, :features], (((1,), (1,)), ((), ())),
        preferred_element_type=jnp.float32) * scaling
    band = band_col if band_row is None else band_row
    ok = (jnp.abs(main_bucket - bucket_row) <= band) & (
        (main_bucket >> 7) == (bucket_row >> 7))
    return jnp.where(ok, s, lowest), ok


def softmax_finish(scored, features):
    top = functools.reduce(jnp.maximum, [jnp.max(s, axis=1, keepdims=True) for s, _, _ in scored])
    total = jnp.zeros_like(top)
    read = jnp.zeros((top.shape[0], features), jnp.float32)
    for s, ok, blk in scored:
        w = jnp.where(ok, jnp.exp(s - top), 0.0)
        total = total + jnp.sum(w, axis=1, keepdims=True)
        read = read + jnp.dot(w.astype(jnp.bfloat16), blk[:, :features],
                              preferred_element_type=jnp.float32)
    return read / total


def label_rows(blk, features, hi, lo, band=None):
    slab = blk[:, features:].astype(jnp.float32).T.astype(jnp.int32)
    bucket = slab[hi:hi + 1, :] * DIGIT + slab[lo:lo + 1, :]
    return bucket, (slab[band:band + 1, :] if band is not None else None)


def shift_of(divisor):
    assert divisor & (divisor - 1) == 0
    return divisor.bit_length() - 1


def kernel(features, scaling, source_hbm, target_hbm, src_bucket_hbm, band_hbm, route_hbm,
           tgt_bucket_hbm, src_out, tgt_out,
           source, target, src_bucket, band, route, tgt_bucket, xsend, tsend, xs, xl, xr, tl, tr,
           a2a_send, a2a_recv, fw_send, fw_recv, nb_send, nb_recv, local_sem):
    g = lax.axis_index("src")
    t = lax.axis_index("tgt")
    n_src = lax.axis_size("src")
    n_tgt = lax.axis_size("tgt")
    rows = source.shape[0]
    span = rows // n_src
    n_z = n_src // 2
    z = g // 2
    core = g % 2
    partner = z * 2 + 1 - core
    left = lax.rem(t + n_tgt - 1, n_tgt)
    right = lax.rem(t + 1, n_tgt)

    def far_peer(j):
        kz = j // 2 + 1
        offset = ((kz + 1) // 2) * (2 * (kz % 2) - 1)
        return ((z + offset + n_z) % n_z) * 2 + j % 2

    pairs = ((source_hbm, source), (target_hbm, target), (src_bucket_hbm, src_bucket),
             (band_hbm, band), (route_hbm, route), (tgt_bucket_hbm, tgt_bucket))
    loads = [pltpu.make_async_copy(h, v, local_sem.at[1 + i]) for i, (h, v) in enumerate(pairs)]
    for c in loads:
        c.start()

    barrier = pltpu.get_barrier_semaphore()

    def greet(j, carry):
        pl.semaphore_signal(
            barrier, inc=1, device_id=(far_peer(n_src - 3 - j), t), device_id_type=MESH)
        return carry

    lax.fori_loop(0, n_src - 2, greet, 0)
    pl.semaphore_signal(barrier, inc=1, device_id=(g, left), device_id_type=MESH)
    pl.semaphore_signal(barrier, inc=1, device_id=(g, right), device_id_type=MESH)
    pl.semaphore_signal(barrier, inc=1, device_id=(partner, t), device_id_type=MESH)

    for c in loads:
        c.wait()

    where_to = route[...]
    dest = (where_to >> shift_of(rows * n_tgt)) * span + (where_to & ((1 << shift_of(span)) - 1))
    sb = src_bucket[...]
    tb = tgt_bucket[...]
    label_rows_of = {
        SRC_HI: sb >> shift_of(DIGIT), SRC_LO: sb & (DIGIT - 1), SRC_BAND: band[...],
        TGT_HI: tb >> shift_of(DIGIT), TGT_LO: tb & (DIGIT - 1),
    }
    slot = lax.broadcasted_iota(jnp.int32, (rows, rows), 0)
    lane = lax.broadcasted_iota(jnp.int32, (rows, LABEL_LANES), 1)
    onehot = (slot == dest).astype(jnp.float32)
    ident = (slot == lax.broadcasted_iota(jnp.int32, (rows, rows), 1)).astype(jnp.float32)

    def label_slab(select, kinds):
        slab = jnp.zeros((rows, LABEL_LANES), jnp.float32)
        for k in kinds:
            row = label_rows_of[k].astype(jnp.float32)
            column = jnp.sum(select * row, axis=1, keepdims=True)
            slab = jnp.where(lane == k, column, slab)
        return slab.astype(jnp.bfloat16)

    xsend[:, :features] = jnp.dot(
        onehot.astype(jnp.bfloat16), source[...],
        preferred_element_type=jnp.float32).astype(jnp.bfloat16)
    xsend[:, features:] = label_slab(onehot, (SRC_HI, SRC_LO, SRC_BAND))
    tsend[:, :features] = target[...]
    tsend[:, features:] = label_slab(ident, (TGT_HI, TGT_LO))

    pl.semaphore_wait(barrier, n_src + 1)

    t_to_right = pltpu.make_async_remote_copy(
        tsend, tl, nb_send.at[0], nb_recv.at[0], device_id=(g, right), device_id_type=MESH)
    t_to_left = pltpu.make_async_remote_copy(
        tsend, tr, nb_send.at[1], nb_recv.at[1], device_id=(g, left), device_id_type=MESH)

    def a2a_copy(peer, sender):
        return pltpu.make_async_remote_copy(
            xsend.at[pl.ds(peer * span, span)],
            xs.at[pl.ds(sender * span, span)],
            a2a_send.at[peer],
            a2a_recv.at[sender],
            device_id=(peer, t),
            device_id_type=MESH,
        )

    own = pltpu.make_async_copy(
        xsend.at[pl.ds(g * span, span)], xs.at[pl.ds(g * span, span)], local_sem.at[0])
    own.start()
    a2a_copy(partner, g).start()

    def a2a_start(j, carry):
        a2a_copy(far_peer(j), g).start()
        return carry

    lax.fori_loop(0, n_src - 2, a2a_start, 0)
    t_to_right.start()
    t_to_left.start()

    def forward(sender):
        rows_of = pl.ds(sender * span, span)
        return (
            pltpu.make_async_remote_copy(
                xs.at[rows_of], xl.at[rows_of], fw_send.at[sender], fw_recv.at[sender],
                device_id=(g, right), device_id_type=MESH),
            pltpu.make_async_remote_copy(
                xs.at[rows_of], xr.at[rows_of], fw_send.at[n_src + sender],
                fw_recv.at[n_src + sender], device_id=(g, left), device_id_type=MESH),
        )

    def arrive_and_forward(sender):
        rows_of = pl.ds(sender * span, span)
        pltpu.make_async_remote_copy(
            xsend.at[rows_of], xs.at[rows_of], a2a_send.at[sender], a2a_recv.at[sender],
            device_id=(sender, t), device_id_type=MESH).wait_recv()
        for c in forward(sender):
            c.start()

    own.wait()
    for c in forward(g):
        c.start()
    arrive_and_forward(partner)

    def a2a_arrive(j, carry):
        arrive_and_forward(far_peer(j))
        return carry

    lax.fori_loop(0, n_src - 2, a2a_arrive, 0)

    t_to_right.wait()
    t_to_left.wait()

    x_cols = xs[:, features:].astype(jnp.float32).astype(jnp.int32)
    x_bucket = x_cols[:, SRC_HI:SRC_HI + 1] * DIGIT + x_cols[:, SRC_LO:SRC_LO + 1]
    x_band = x_cols[:, SRC_BAND:SRC_BAND + 1]
    row_scored = []
    for blk in (tl, tsend, tr):
        bucket_row, _ = label_rows(blk[...], features, TGT_HI, TGT_LO)
        s, ok = masked_scores(xs[:, :features], x_bucket, x_band, blk, bucket_row, None,
                              features, scaling)
        row_scored.append((s, ok, blk))
    src_out[...] = softmax_finish(row_scored, features)

    y_cols = tsend[:, features:].astype(jnp.float32).astype(jnp.int32)
    y_bucket = y_cols[:, TGT_HI:TGT_HI + 1] * DIGIT + y_cols[:, TGT_LO:TGT_LO + 1]

    def col_scored(blk):
        bucket_row, band_row = label_rows(blk[...], features, SRC_HI, SRC_LO, SRC_BAND)
        s, ok = masked_scores(tsend[:, :features], y_bucket, None, blk, bucket_row, band_row,
                              features, scaling)
        return (s, ok, blk)

    own_scored = col_scored(xs)

    a2a_copy(partner, g).wait_send()

    def a2a_sent(j, carry):
        a2a_copy(far_peer(j), g).wait_send()
        return carry

    lax.fori_loop(0, n_src - 2, a2a_sent, 0)

    def left_arrived(s, carry):
        forward(s)[0].wait_recv()
        return carry

    def right_arrived(s, carry):
        forward(s)[1].wait_recv()
        return carry

    lax.fori_loop(0, n_src, left_arrived, 0)
    left_scored = col_scored(xl)
    lax.fori_loop(0, n_src, right_arrived, 0)
    right_scored = col_scored(xr)
    tgt_out[...] = softmax_finish([left_scored, own_scored, right_scored], features)

    def fw_sent(s, carry):
        for c in forward(s):
            c.wait_send()
        return carry

    lax.fori_loop(0, n_src, fw_sent, 0)


def write_kernel(src_in, tgt_in, src_res, tgt_res, sems):
    copies = [pltpu.make_async_copy(src_in, src_res, sems.at[0]),
              pltpu.make_async_copy(tgt_in, tgt_res, sems.at[1])]
    for c in copies:
        c.start()
    for c in copies:
        c.wait()


def write_out(src_read, tgt_read):
    return pl.pallas_call(
        write_kernel,
        out_shape=(jax.ShapeDtypeStruct(src_read.shape, src_read.dtype),
                   jax.ShapeDtypeStruct(tgt_read.shape, tgt_read.dtype)),
        in_specs=[pl.BlockSpec(memory_space=pltpu.VMEM)] * 2,
        out_specs=(pl.BlockSpec(memory_space=pl.ANY),) * 2,
        scratch_shapes=[pltpu.SemaphoreType.DMA((2,))],
    )(src_read, tgt_read)


def on_device(source, target, src_bucket, tgt_bucket, band, route):
    row_count, feature_count = source.shape
    src_count = lax.axis_size("src")
    tgt_count = lax.axis_size("tgt")
    per_peer = row_count // src_count
    scaling = 2.0 / math.sqrt(feature_count)

    width = feature_count + LABEL_LANES
    ints = [v.reshape(1, row_count) for v in (src_bucket, band, route, tgt_bucket)]

    block = jax.ShapeDtypeStruct((row_count, feature_count), jnp.float32)
    vmem = pl.BlockSpec(memory_space=pltpu.VMEM)
    reads = pl.pallas_call(
        functools.partial(kernel, feature_count, scaling),
        out_shape=(block, block),
        in_specs=[pl.BlockSpec(memory_space=pl.ANY)] * 6,
        out_specs=(vmem, vmem),
        scratch_shapes=[pltpu.VMEM((row_count, feature_count), jnp.bfloat16)] * 2
        + [pltpu.VMEM((1, row_count), jnp.int32)] * 4
        + [pltpu.VMEM((row_count, width), jnp.bfloat16)] * 7
        + [
            pltpu.SemaphoreType.DMA((src_count,)),
            pltpu.SemaphoreType.DMA((src_count,)),
            pltpu.SemaphoreType.DMA((2 * src_count,)),
            pltpu.SemaphoreType.DMA((2 * src_count,)),
            pltpu.SemaphoreType.DMA((2,)),
            pltpu.SemaphoreType.DMA((2,)),
            pltpu.SemaphoreType.DMA((7,)),
        ],
        compiler_params=pltpu.CompilerParams(collective_id=0, has_side_effects=True),
    )(source, target, *ints)
    return write_out(*reads)


def solution(mesh):
    placed = (
        P(("src", "tgt"), None),
        P(("src", "tgt"), None),
        P(("src", "tgt")),
        P(("src", "tgt")),
        P(("src", "tgt")),
        P(("src", "tgt")),
    )
    return jax.shard_map(
        on_device,
        mesh=mesh,
        in_specs=placed,
        out_specs=(P(("src", "tgt"), None), P(("src", "tgt"), None)),
        check_vma=False,
    )
```

```python
import functools
import math

import jax
import jax.numpy as jnp
from jax import lax
from jax.experimental import pallas as pl
from jax.experimental.pallas import tpu as pltpu
from jax.sharding import PartitionSpec as P

lowest = -1e30
MESH = pl.DeviceIdType.MESH
LABEL_LANES = 128
DIGIT = 64
SRC_HI, SRC_LO, SRC_BAND, TGT_HI, TGT_LO = 0, 1, 2, 4, 5


def softmax_read(main, main_bucket, band_col, others, features, scaling, band_of_rows):
    scores, masks = [], []
    for blk, bucket_row, band_row in others:
        s = lax.dot_general(
            main, blk[:, :features], (((1,), (1,)), ((), ())),
            preferred_element_type=jnp.float32) * scaling
        band = band_col if band_of_rows else band_row
        ok = (jnp.abs(main_bucket - bucket_row) <= band) & (
            (main_bucket >> 7) == (bucket_row >> 7))
        scores.append(jnp.where(ok, s, lowest))
        masks.append(ok)
    top = functools.reduce(jnp.maximum, [jnp.max(s, axis=1, keepdims=True) for s in scores])
    total = jnp.zeros_like(top)
    read = jnp.zeros((main.shape[0], features), jnp.float32)
    for s, ok, (blk, _, _) in zip(scores, masks, others):
        w = jnp.where(ok, jnp.exp(s - top), 0.0)
        total = total + jnp.sum(w, axis=1, keepdims=True)
        read = read + jnp.dot(w.astype(jnp.bfloat16), blk[:, :features],
                              preferred_element_type=jnp.float32)
    return read / total


def label_rows(blk, features, hi, lo, band=None):
    slab = blk[:, features:].astype(jnp.float32).T.astype(jnp.int32)
    bucket = slab[hi:hi + 1, :] * DIGIT + slab[lo:lo + 1, :]
    return bucket, (slab[band:band + 1, :] if band is not None else None)


def shift_of(divisor):
    assert divisor & (divisor - 1) == 0
    return divisor.bit_length() - 1


def kernel(features, scaling, source_hbm, target_hbm, src_bucket_hbm, band_hbm, route_hbm,
           tgt_bucket_hbm, src_out, tgt_out,
           source, target, src_bucket, band, route, tgt_bucket, xsend, tsend, xs, xl, xr, tl, tr,
           a2a_send, a2a_recv, fw_send, fw_recv, nb_send, nb_recv, local_sem):
    g = lax.axis_index("src")
    t = lax.axis_index("tgt")
    n_src = lax.axis_size("src")
    n_tgt = lax.axis_size("tgt")
    rows = source.shape[0]
    span = rows // n_src
    n_z = n_src // 2
    z = g // 2
    core = g % 2
    partner = z * 2 + 1 - core
    left = lax.rem(t + n_tgt - 1, n_tgt)
    right = lax.rem(t + 1, n_tgt)

    def far_peer(j):
        kz = j // 2 + 1
        offset = ((kz + 1) // 2) * (2 * (kz % 2) - 1)
        return ((z + offset + n_z) % n_z) * 2 + j % 2

    pairs = ((source_hbm, source), (target_hbm, target), (src_bucket_hbm, src_bucket),
             (band_hbm, band), (route_hbm, route), (tgt_bucket_hbm, tgt_bucket))
    barrier = pltpu.get_barrier_semaphore()

    def greet(j, carry):
        pl.semaphore_signal(
            barrier, inc=1, device_id=(far_peer(n_src - 3 - j), t), device_id_type=MESH)
        return carry

    lax.fori_loop(0, n_src - 2, greet, 0)
    pl.semaphore_signal(barrier, inc=1, device_id=(g, left), device_id_type=MESH)
    pl.semaphore_signal(barrier, inc=1, device_id=(g, right), device_id_type=MESH)
    pl.semaphore_signal(barrier, inc=1, device_id=(partner, t), device_id_type=MESH)

    loads = [pltpu.make_async_copy(h, v, local_sem.at[1 + i]) for i, (h, v) in enumerate(pairs)]
    for c in loads:
        c.start()
    for c in loads:
        c.wait()

    where_to = route[...]
    dest = (where_to >> shift_of(rows * n_tgt)) * span + (where_to & ((1 << shift_of(span)) - 1))
    sb = src_bucket[...]
    tb = tgt_bucket[...]
    label_rows_of = {
        SRC_HI: sb >> shift_of(DIGIT), SRC_LO: sb & (DIGIT - 1), SRC_BAND: band[...],
        TGT_HI: tb >> shift_of(DIGIT), TGT_LO: tb & (DIGIT - 1),
    }
    slot = lax.broadcasted_iota(jnp.int32, (rows, rows), 0)
    lane = lax.broadcasted_iota(jnp.int32, (rows, LABEL_LANES), 1)
    onehot = (slot == dest).astype(jnp.float32)
    ident = (slot == lax.broadcasted_iota(jnp.int32, (rows, rows), 1)).astype(jnp.float32)

    def label_slab(select, kinds):
        slab = jnp.zeros((rows, LABEL_LANES), jnp.float32)
        for k in kinds:
            row = label_rows_of[k].astype(jnp.float32)
            column = jnp.sum(select * row, axis=1, keepdims=True)
            slab = jnp.where(lane == k, column, slab)
        return slab.astype(jnp.bfloat16)

    xsend[:, :features] = jnp.dot(
        onehot.astype(jnp.bfloat16), source[...],
        preferred_element_type=jnp.float32).astype(jnp.bfloat16)
    xsend[:, features:] = label_slab(onehot, (SRC_HI, SRC_LO, SRC_BAND))
    tsend[:, :features] = target[...]
    tsend[:, features:] = label_slab(ident, (TGT_HI, TGT_LO))

    pl.semaphore_wait(barrier, n_src + 1)

    t_to_right = pltpu.make_async_remote_copy(
        tsend, tl, nb_send.at[0], nb_recv.at[0], device_id=(g, right), device_id_type=MESH)
    t_to_left = pltpu.make_async_remote_copy(
        tsend, tr, nb_send.at[1], nb_recv.at[1], device_id=(g, left), device_id_type=MESH)

    def a2a_copy(peer, sender):
        return pltpu.make_async_remote_copy(
            xsend.at[pl.ds(peer * span, span)],
            xs.at[pl.ds(sender * span, span)],
            a2a_send.at[peer],
            a2a_recv.at[sender],
            device_id=(peer, t),
            device_id_type=MESH,
        )

    own = pltpu.make_async_copy(
        xsend.at[pl.ds(g * span, span)], xs.at[pl.ds(g * span, span)], local_sem.at[0])
    own.start()
    a2a_copy(partner, g).start()

    def a2a_start(j, carry):
        a2a_copy(far_peer(j), g).start()
        return carry

    lax.fori_loop(0, n_src - 2, a2a_start, 0)
    t_to_right.start()
    t_to_left.start()

    def forward(sender):
        rows_of = pl.ds(sender * span, span)
        return (
            pltpu.make_async_remote_copy(
                xs.at[rows_of], xl.at[rows_of], fw_send.at[sender], fw_recv.at[sender],
                device_id=(g, right), device_id_type=MESH),
            pltpu.make_async_remote_copy(
                xs.at[rows_of], xr.at[rows_of], fw_send.at[n_src + sender],
                fw_recv.at[n_src + sender], device_id=(g, left), device_id_type=MESH),
        )

    def arrive_and_forward(sender):
        rows_of = pl.ds(sender * span, span)
        pltpu.make_async_remote_copy(
            xsend.at[rows_of], xs.at[rows_of], a2a_send.at[sender], a2a_recv.at[sender],
            device_id=(sender, t), device_id_type=MESH).wait_recv()
        for c in forward(sender):
            c.start()

    own.wait()
    for c in forward(g):
        c.start()
    arrive_and_forward(partner)

    def a2a_arrive(j, carry):
        arrive_and_forward(far_peer(j))
        return carry

    lax.fori_loop(0, n_src - 2, a2a_arrive, 0)

    t_to_right.wait()
    t_to_left.wait()

    x_cols = xs[:, features:].astype(jnp.float32).astype(jnp.int32)
    x_bucket = x_cols[:, SRC_HI:SRC_HI + 1] * DIGIT + x_cols[:, SRC_LO:SRC_LO + 1]
    x_band = x_cols[:, SRC_BAND:SRC_BAND + 1]
    tgt_blocks = []
    for blk in (tl, tsend, tr):
        bucket_row, _ = label_rows(blk[...], features, TGT_HI, TGT_LO)
        tgt_blocks.append((blk, bucket_row, None))
    src_out[...] = softmax_read(
        xs[:, :features], x_bucket, x_band, tgt_blocks, features, scaling, True)

    a2a_copy(partner, g).wait_send()

    def a2a_sent(j, carry):
        a2a_copy(far_peer(j), g).wait_send()
        return carry

    lax.fori_loop(0, n_src - 2, a2a_sent, 0)

    def fw_done(s, carry):
        for c in forward(s):
            c.wait_send()
            c.wait_recv()
        return carry

    lax.fori_loop(0, n_src, fw_done, 0)

    y_cols = tsend[:, features:].astype(jnp.float32).astype(jnp.int32)
    y_bucket = y_cols[:, TGT_HI:TGT_HI + 1] * DIGIT + y_cols[:, TGT_LO:TGT_LO + 1]
    src_blocks = []
    for blk in (xl, xs, xr):
        bucket_row, band_row = label_rows(blk[...], features, SRC_HI, SRC_LO, SRC_BAND)
        src_blocks.append((blk, bucket_row, band_row))
    tgt_out[...] = softmax_read(
        tsend[:, :features], y_bucket, None, src_blocks, features, scaling, False)


def write_kernel(src_in, tgt_in, src_res, tgt_res, sems):
    copies = [pltpu.make_async_copy(src_in, src_res, sems.at[0]),
              pltpu.make_async_copy(tgt_in, tgt_res, sems.at[1])]
    for c in copies:
        c.start()
    for c in copies:
        c.wait()


def write_out(src_read, tgt_read):
    return pl.pallas_call(
        write_kernel,
        out_shape=(jax.ShapeDtypeStruct(src_read.shape, src_read.dtype),
                   jax.ShapeDtypeStruct(tgt_read.shape, tgt_read.dtype)),
        in_specs=[pl.BlockSpec(memory_space=pltpu.VMEM)] * 2,
        out_specs=(pl.BlockSpec(memory_space=pl.ANY),) * 2,
        scratch_shapes=[pltpu.SemaphoreType.DMA((2,))],
    )(src_read, tgt_read)


def on_device(source, target, src_bucket, tgt_bucket, band, route):
    row_count, feature_count = source.shape
    src_count = lax.axis_size("src")
    tgt_count = lax.axis_size("tgt")
    per_peer = row_count // src_count
    scaling = 2.0 / math.sqrt(feature_count)

    width = feature_count + LABEL_LANES
    ints = [v.reshape(1, row_count) for v in (src_bucket, band, route, tgt_bucket)]

    block = jax.ShapeDtypeStruct((row_count, feature_count), jnp.float32)
    vmem = pl.BlockSpec(memory_space=pltpu.VMEM)
    reads = pl.pallas_call(
        functools.partial(kernel, feature_count, scaling),
        out_shape=(block, block),
        in_specs=[pl.BlockSpec(memory_space=pl.ANY)] * 6,
        out_specs=(vmem, vmem),
        scratch_shapes=[pltpu.VMEM((row_count, feature_count), jnp.bfloat16)] * 2
        + [pltpu.VMEM((1, row_count), jnp.int32)] * 4
        + [pltpu.VMEM((row_count, width), jnp.bfloat16)] * 7
        + [
            pltpu.SemaphoreType.DMA((src_count,)),
            pltpu.SemaphoreType.DMA((src_count,)),
            pltpu.SemaphoreType.DMA((2 * src_count,)),
            pltpu.SemaphoreType.DMA((2 * src_count,)),
            pltpu.SemaphoreType.DMA((2,)),
            pltpu.SemaphoreType.DMA((2,)),
            pltpu.SemaphoreType.DMA((7,)),
        ],
        compiler_params=pltpu.CompilerParams(collective_id=0, has_side_effects=True),
    )(source, target, *ints)
    return write_out(*reads)


def solution(mesh):
    placed = (
        P(("src", "tgt"), None),
        P(("src", "tgt"), None),
        P(("src", "tgt")),
        P(("src", "tgt")),
        P(("src", "tgt")),
        P(("src", "tgt")),
    )
    return jax.shard_map(
        on_device,
        mesh=mesh,
        in_specs=placed,
        out_specs=(P(("src", "tgt"), None), P(("src", "tgt"), None)),
        check_vma=False,
    )
```

```python
import functools
import math

import jax
import jax.numpy as jnp
from jax import lax
from jax.experimental import pallas as pl
from jax.experimental.pallas import tpu as pltpu
from jax.sharding import PartitionSpec as P

lowest = -1e30
MESH = pl.DeviceIdType.MESH
LABEL_LANES = 128
DIGIT = 64
SRC_HI, SRC_LO, SRC_BAND, TGT_HI, TGT_LO = 0, 1, 2, 4, 5


def softmax_read(main, main_bucket, band_col, others, features, scaling, band_of_rows):
    scores, masks = [], []
    for blk, bucket_row, band_row in others:
        s = lax.dot_general(
            main, blk[:, :features], (((1,), (1,)), ((), ())),
            preferred_element_type=jnp.float32) * scaling
        band = band_col if band_of_rows else band_row
        ok = (jnp.abs(main_bucket - bucket_row) <= band) & (
            (main_bucket >> 7) == (bucket_row >> 7))
        scores.append(jnp.where(ok, s, lowest))
        masks.append(ok)
    top = functools.reduce(jnp.maximum, [jnp.max(s, axis=1, keepdims=True) for s in scores])
    total = jnp.zeros_like(top)
    read = jnp.zeros((main.shape[0], features), jnp.float32)
    for s, ok, (blk, _, _) in zip(scores, masks, others):
        w = jnp.where(ok, jnp.exp(s - top), 0.0)
        total = total + jnp.sum(w, axis=1, keepdims=True)
        read = read + jnp.dot(w.astype(jnp.bfloat16), blk[:, :features],
                              preferred_element_type=jnp.float32)
    return read / total


def label_rows(blk, features, hi, lo, band=None):
    slab = blk[:, features:].astype(jnp.float32).T.astype(jnp.int32)
    bucket = slab[hi:hi + 1, :] * DIGIT + slab[lo:lo + 1, :]
    return bucket, (slab[band:band + 1, :] if band is not None else None)


def shift_of(divisor):
    assert divisor & (divisor - 1) == 0
    return divisor.bit_length() - 1


def kernel(features, scaling, source_hbm, target_hbm, src_bucket_hbm, band_hbm, route_hbm,
           tgt_bucket_hbm, src_out, tgt_out,
           source, target, src_bucket, band, route, tgt_bucket, xsend, tsend, xs, xl, xr, tl, tr,
           a2a_send, a2a_recv, fw_send, fw_recv, nb_send, nb_recv, local_sem):
    g = lax.axis_index("src")
    t = lax.axis_index("tgt")
    n_src = lax.axis_size("src")
    n_tgt = lax.axis_size("tgt")
    rows = source.shape[0]
    span = rows // n_src
    n_z = n_src // 2
    z = g // 2
    core = g % 2
    partner = z * 2 + 1 - core
    left = lax.rem(t + n_tgt - 1, n_tgt)
    right = lax.rem(t + 1, n_tgt)

    def far_peer(j):
        kz = j // 2 + 1
        offset = ((kz + 1) // 2) * (2 * (kz % 2) - 1)
        return ((z + offset + n_z) & (n_z - 1)) * 2 + j % 2

    shift_of(n_z)

    pairs = ((source_hbm, source), (target_hbm, target), (src_bucket_hbm, src_bucket),
             (band_hbm, band), (route_hbm, route), (tgt_bucket_hbm, tgt_bucket))
    barrier = pltpu.get_barrier_semaphore()

    for j in range(n_src - 3, -1, -1):
        pl.semaphore_signal(barrier, inc=1, device_id=(far_peer(j), t), device_id_type=MESH)
    pl.semaphore_signal(barrier, inc=1, device_id=(g, left), device_id_type=MESH)
    pl.semaphore_signal(barrier, inc=1, device_id=(g, right), device_id_type=MESH)
    pl.semaphore_signal(barrier, inc=1, device_id=(partner, t), device_id_type=MESH)

    loads = [pltpu.make_async_copy(h, v, local_sem.at[1 + i]) for i, (h, v) in enumerate(pairs)]
    for c in loads:
        c.start()
    for c in loads:
        c.wait()

    where_to = route[...]
    dest = (where_to >> shift_of(rows * n_tgt)) * span + (where_to & ((1 << shift_of(span)) - 1))
    sb = src_bucket[...]
    tb = tgt_bucket[...]
    label_rows_of = {
        SRC_HI: sb >> shift_of(DIGIT), SRC_LO: sb & (DIGIT - 1), SRC_BAND: band[...],
        TGT_HI: tb >> shift_of(DIGIT), TGT_LO: tb & (DIGIT - 1),
    }
    slot = lax.broadcasted_iota(jnp.int32, (rows, rows), 0)
    lane = lax.broadcasted_iota(jnp.int32, (rows, LABEL_LANES), 1)
    onehot = (slot == dest).astype(jnp.float32)
    ident = (slot == lax.broadcasted_iota(jnp.int32, (rows, rows), 1)).astype(jnp.float32)

    def label_slab(select, kinds):
        slab = jnp.zeros((rows, LABEL_LANES), jnp.float32)
        for k in kinds:
            row = label_rows_of[k].astype(jnp.float32)
            column = jnp.sum(select * row, axis=1, keepdims=True)
            slab = jnp.where(lane == k, column, slab)
        return slab.astype(jnp.bfloat16)

    xsend[:, :features] = jnp.dot(
        onehot.astype(jnp.bfloat16), source[...],
        preferred_element_type=jnp.float32).astype(jnp.bfloat16)
    xsend[:, features:] = label_slab(onehot, (SRC_HI, SRC_LO, SRC_BAND))
    tsend[:, :features] = target[...]
    tsend[:, features:] = label_slab(ident, (TGT_HI, TGT_LO))

    pl.semaphore_wait(barrier, n_src + 1)

    t_to_right = pltpu.make_async_remote_copy(
        tsend, tl, nb_send.at[0], nb_recv.at[0], device_id=(g, right), device_id_type=MESH)
    t_to_left = pltpu.make_async_remote_copy(
        tsend, tr, nb_send.at[1], nb_recv.at[1], device_id=(g, left), device_id_type=MESH)

    def a2a_copy(peer, sender):
        return pltpu.make_async_remote_copy(
            xsend.at[pl.ds(peer * span, span)],
            xs.at[pl.ds(sender * span, span)],
            a2a_send.at[peer],
            a2a_recv.at[sender],
            device_id=(peer, t),
            device_id_type=MESH,
        )

    own = pltpu.make_async_copy(
        xsend.at[pl.ds(g * span, span)], xs.at[pl.ds(g * span, span)], local_sem.at[0])
    own.start()
    a2a_copy(partner, g).start()

    for j in range(n_src - 2):
        a2a_copy(far_peer(j), g).start()
    t_to_right.start()
    t_to_left.start()

    def forward(sender):
        rows_of = pl.ds(sender * span, span)
        return (
            pltpu.make_async_remote_copy(
                xs.at[rows_of], xl.at[rows_of], fw_send.at[sender], fw_recv.at[sender],
                device_id=(g, right), device_id_type=MESH),
            pltpu.make_async_remote_copy(
                xs.at[rows_of], xr.at[rows_of], fw_send.at[n_src + sender],
                fw_recv.at[n_src + sender], device_id=(g, left), device_id_type=MESH),
        )

    def arrive_and_forward(sender):
        rows_of = pl.ds(sender * span, span)
        pltpu.make_async_remote_copy(
            xsend.at[rows_of], xs.at[rows_of], a2a_send.at[sender], a2a_recv.at[sender],
            device_id=(sender, t), device_id_type=MESH).wait_recv()
        for c in forward(sender):
            c.start()

    own.wait()
    for c in forward(g):
        c.start()
    arrive_and_forward(partner)

    for j in range(n_src - 2):
        arrive_and_forward(far_peer(j))

    t_to_right.wait()
    t_to_left.wait()

    x_cols = xs[:, features:].astype(jnp.float32).astype(jnp.int32)
    x_bucket = x_cols[:, SRC_HI:SRC_HI + 1] * DIGIT + x_cols[:, SRC_LO:SRC_LO + 1]
    x_band = x_cols[:, SRC_BAND:SRC_BAND + 1]
    tgt_blocks = []
    for blk in (tl, tsend, tr):
        bucket_row, _ = label_rows(blk[...], features, TGT_HI, TGT_LO)
        tgt_blocks.append((blk, bucket_row, None))
    src_out[...] = softmax_read(
        xs[:, :features], x_bucket, x_band, tgt_blocks, features, scaling, True)

    a2a_copy(partner, g).wait_send()

    def a2a_sent(j, carry):
        a2a_copy(far_peer(j), g).wait_send()
        return carry

    lax.fori_loop(0, n_src - 2, a2a_sent, 0)

    def fw_done(s, carry):
        for c in forward(s):
            c.wait_send()
            c.wait_recv()
        return carry

    lax.fori_loop(0, n_src, fw_done, 0)

    y_cols = tsend[:, features:].astype(jnp.float32).astype(jnp.int32)
    y_bucket = y_cols[:, TGT_HI:TGT_HI + 1] * DIGIT + y_cols[:, TGT_LO:TGT_LO + 1]
    src_blocks = []
    for blk in (xl, xs, xr):
        bucket_row, band_row = label_rows(blk[...], features, SRC_HI, SRC_LO, SRC_BAND)
        src_blocks.append((blk, bucket_row, band_row))
    tgt_out[...] = softmax_read(
        tsend[:, :features], y_bucket, None, src_blocks, features, scaling, False)


def write_kernel(src_in, tgt_in, src_res, tgt_res, sems):
    copies = [pltpu.make_async_copy(src_in, src_res, sems.at[0]),
              pltpu.make_async_copy(tgt_in, tgt_res, sems.at[1])]
    for c in copies:
        c.start()
    for c in copies:
        c.wait()


def write_out(src_read, tgt_read):
    return pl.pallas_call(
        write_kernel,
        out_shape=(jax.ShapeDtypeStruct(src_read.shape, src_read.dtype),
                   jax.ShapeDtypeStruct(tgt_read.shape, tgt_read.dtype)),
        in_specs=[pl.BlockSpec(memory_space=pltpu.VMEM)] * 2,
        out_specs=(pl.BlockSpec(memory_space=pl.ANY),) * 2,
        scratch_shapes=[pltpu.SemaphoreType.DMA((2,))],
    )(src_read, tgt_read)


def on_device(source, target, src_bucket, tgt_bucket, band, route):
    row_count, feature_count = source.shape
    src_count = lax.axis_size("src")
    tgt_count = lax.axis_size("tgt")
    per_peer = row_count // src_count
    scaling = 2.0 / math.sqrt(feature_count)

    width = feature_count + LABEL_LANES
    ints = [v.reshape(1, row_count) for v in (src_bucket, band, route, tgt_bucket)]

    block = jax.ShapeDtypeStruct((row_count, feature_count), jnp.float32)
    vmem = pl.BlockSpec(memory_space=pltpu.VMEM)
    reads = pl.pallas_call(
        functools.partial(kernel, feature_count, scaling),
        out_shape=(block, block),
        in_specs=[pl.BlockSpec(memory_space=pl.ANY)] * 6,
        out_specs=(vmem, vmem),
        scratch_shapes=[pltpu.VMEM((row_count, feature_count), jnp.bfloat16)] * 2
        + [pltpu.VMEM((1, row_count), jnp.int32)] * 4
        + [pltpu.VMEM((row_count, width), jnp.bfloat16)] * 7
        + [
            pltpu.SemaphoreType.DMA((src_count,)),
            pltpu.SemaphoreType.DMA((src_count,)),
            pltpu.SemaphoreType.DMA((2 * src_count,)),
            pltpu.SemaphoreType.DMA((2 * src_count,)),
            pltpu.SemaphoreType.DMA((2,)),
            pltpu.SemaphoreType.DMA((2,)),
            pltpu.SemaphoreType.DMA((7,)),
        ],
        compiler_params=pltpu.CompilerParams(collective_id=0, has_side_effects=True),
    )(source, target, *ints)
    return write_out(*reads)


def solution(mesh):
    placed = (
        P(("src", "tgt"), None),
        P(("src", "tgt"), None),
        P(("src", "tgt")),
        P(("src", "tgt")),
        P(("src", "tgt")),
        P(("src", "tgt")),
    )
    return jax.shard_map(
        on_device,
        mesh=mesh,
        in_specs=placed,
        out_specs=(P(("src", "tgt"), None), P(("src", "tgt"), None)),
        check_vma=False,
    )
```

```python
import functools
import math

import jax
import jax.numpy as jnp
from jax import lax
from jax.experimental import pallas as pl
from jax.experimental.pallas import tpu as pltpu
from jax.sharding import PartitionSpec as P

lowest = -1e30
MESH = pl.DeviceIdType.MESH
LABEL_LANES = 128
DIGIT = 64
SRC_HI, SRC_LO, SRC_BAND, TGT_HI, TGT_LO = 0, 1, 2, 4, 5


def softmax_read(main, main_bucket, band_col, others, features, scaling, band_of_rows):
    scores, masks = [], []
    for blk, bucket_row, band_row in others:
        s = lax.dot_general(
            main, blk[:, :features], (((1,), (1,)), ((), ())),
            preferred_element_type=jnp.float32) * scaling
        band = band_col if band_of_rows else band_row
        ok = (jnp.abs(main_bucket - bucket_row) <= band) & (
            (main_bucket >> 7) == (bucket_row >> 7))
        scores.append(jnp.where(ok, s, lowest))
        masks.append(ok)
    top = functools.reduce(jnp.maximum, [jnp.max(s, axis=1, keepdims=True) for s in scores])
    total = jnp.zeros_like(top)
    read = jnp.zeros((main.shape[0], features), jnp.float32)
    for s, ok, (blk, _, _) in zip(scores, masks, others):
        w = jnp.where(ok, jnp.exp(s - top), 0.0)
        total = total + jnp.sum(w, axis=1, keepdims=True)
        read = read + jnp.dot(w.astype(jnp.bfloat16), blk[:, :features],
                              preferred_element_type=jnp.float32)
    return read / total


def label_rows(blk, features, hi, lo, band=None):
    slab = blk[:, features:].astype(jnp.float32).T.astype(jnp.int32)
    bucket = slab[hi:hi + 1, :] * DIGIT + slab[lo:lo + 1, :]
    return bucket, (slab[band:band + 1, :] if band is not None else None)


def shift_of(divisor):
    assert divisor & (divisor - 1) == 0
    return divisor.bit_length() - 1


def kernel(features, scaling, source_hbm, target_hbm, src_bucket_hbm, band_hbm, route_hbm,
           tgt_bucket_hbm, src_out, tgt_out,
           source, target, src_bucket, band, route, tgt_bucket, xsend, tsend, xs, xl, xr, tl, tr,
           a2a_send, a2a_recv, fw_send, fw_recv, nb_send, nb_recv, local_sem):
    g = lax.axis_index("src")
    t = lax.axis_index("tgt")
    n_src = lax.axis_size("src")
    n_tgt = lax.axis_size("tgt")
    rows = source.shape[0]
    span = rows // n_src
    n_z = n_src // 2
    z = g // 2
    core = g % 2
    partner = z * 2 + 1 - core
    left = lax.rem(t + n_tgt - 1, n_tgt)
    right = lax.rem(t + 1, n_tgt)

    def far_peer(j):
        kz = j // 2 + 1
        offset = ((kz + 1) // 2) * (2 * (kz % 2) - 1)
        return ((z + offset + n_z) & (n_z - 1)) * 2 + j % 2

    shift_of(n_z)

    pairs = ((source_hbm, source), (target_hbm, target), (src_bucket_hbm, src_bucket),
             (band_hbm, band), (route_hbm, route), (tgt_bucket_hbm, tgt_bucket))
    barrier = pltpu.get_barrier_semaphore()

    for j in range(n_src - 3, -1, -1):
        pl.semaphore_signal(barrier, inc=1, device_id=(far_peer(j), t), device_id_type=MESH)
    pl.semaphore_signal(barrier, inc=1, device_id=(g, left), device_id_type=MESH)
    pl.semaphore_signal(barrier, inc=1, device_id=(g, right), device_id_type=MESH)
    pl.semaphore_signal(barrier, inc=1, device_id=(partner, t), device_id_type=MESH)

    loads = [pltpu.make_async_copy(h, v, local_sem.at[1 + i]) for i, (h, v) in enumerate(pairs)]
    for c in loads:
        c.start()
    for c in loads:
        c.wait()

    where_to = route[...]
    dest = (where_to >> shift_of(rows * n_tgt)) * span + (where_to & ((1 << shift_of(span)) - 1))
    sb = src_bucket[...]
    tb = tgt_bucket[...]
    label_rows_of = {
        SRC_HI: sb >> shift_of(DIGIT), SRC_LO: sb & (DIGIT - 1), SRC_BAND: band[...],
        TGT_HI: tb >> shift_of(DIGIT), TGT_LO: tb & (DIGIT - 1),
    }
    slot = lax.broadcasted_iota(jnp.int32, (rows, rows), 0)
    lane = lax.broadcasted_iota(jnp.int32, (rows, LABEL_LANES), 1)
    onehot = (slot == dest).astype(jnp.float32)
    ident = (slot == lax.broadcasted_iota(jnp.int32, (rows, rows), 1)).astype(jnp.float32)

    def label_slab(select, kinds):
        slab = jnp.zeros((rows, LABEL_LANES), jnp.float32)
        for k in kinds:
            row = label_rows_of[k].astype(jnp.float32)
            column = jnp.sum(select * row, axis=1, keepdims=True)
            slab = jnp.where(lane == k, column, slab)
        return slab.astype(jnp.bfloat16)

    xsend[:, :features] = jnp.dot(
        onehot.astype(jnp.bfloat16), source[...],
        preferred_element_type=jnp.float32).astype(jnp.bfloat16)
    xsend[:, features:] = label_slab(onehot, (SRC_HI, SRC_LO, SRC_BAND))
    tsend[:, :features] = target[...]
    tsend[:, features:] = label_slab(ident, (TGT_HI, TGT_LO))

    pl.semaphore_wait(barrier, n_src + 1)

    t_to_right = pltpu.make_async_remote_copy(
        tsend, tl, nb_send.at[0], nb_recv.at[0], device_id=(g, right), device_id_type=MESH)
    t_to_left = pltpu.make_async_remote_copy(
        tsend, tr, nb_send.at[1], nb_recv.at[1], device_id=(g, left), device_id_type=MESH)

    def a2a_copy(peer, sender):
        return pltpu.make_async_remote_copy(
            xsend.at[pl.ds(peer * span, span)],
            xs.at[pl.ds(sender * span, span)],
            a2a_send.at[peer],
            a2a_recv.at[sender],
            device_id=(peer, t),
            device_id_type=MESH,
        )

    own = pltpu.make_async_copy(
        xsend.at[pl.ds(g * span, span)], xs.at[pl.ds(g * span, span)], local_sem.at[0])
    own.start()
    a2a_copy(partner, g).start()

    for j in range(n_src - 2):
        a2a_copy(far_peer(j), g).start()
    t_to_right.start()
    t_to_left.start()

    def forward(sender):
        rows_of = pl.ds(sender * span, span)
        return (
            pltpu.make_async_remote_copy(
                xs.at[rows_of], xl.at[rows_of], fw_send.at[sender], fw_recv.at[sender],
                device_id=(g, right), device_id_type=MESH),
            pltpu.make_async_remote_copy(
                xs.at[rows_of], xr.at[rows_of], fw_send.at[n_src + sender],
                fw_recv.at[n_src + sender], device_id=(g, left), device_id_type=MESH),
        )

    def arrive_and_forward(sender):
        rows_of = pl.ds(sender * span, span)
        pltpu.make_async_remote_copy(
            xsend.at[rows_of], xs.at[rows_of], a2a_send.at[sender], a2a_recv.at[sender],
            device_id=(sender, t), device_id_type=MESH).wait_recv()
        for c in forward(sender):
            c.start()

    own.wait()
    for c in forward(g):
        c.start()
    arrive_and_forward(partner)

    for j in range(n_src - 2):
        arrive_and_forward(far_peer(j))

    t_to_right.wait()
    t_to_left.wait()

    x_cols = xs[:, features:].astype(jnp.float32).astype(jnp.int32)
    x_bucket = x_cols[:, SRC_HI:SRC_HI + 1] * DIGIT + x_cols[:, SRC_LO:SRC_LO + 1]
    x_band = x_cols[:, SRC_BAND:SRC_BAND + 1]
    tgt_blocks = []
    for blk in (tl, tsend, tr):
        bucket_row, _ = label_rows(blk[...], features, TGT_HI, TGT_LO)
        tgt_blocks.append((blk, bucket_row, None))
    src_out[...] = softmax_read(
        xs[:, :features], x_bucket, x_band, tgt_blocks, features, scaling, True)

    def fw_arrived(s, carry):
        for c in forward(s):
            c.wait_recv()
        return carry

    lax.fori_loop(0, n_src, fw_arrived, 0)

    y_cols = tsend[:, features:].astype(jnp.float32).astype(jnp.int32)
    y_bucket = y_cols[:, TGT_HI:TGT_HI + 1] * DIGIT + y_cols[:, TGT_LO:TGT_LO + 1]
    src_blocks = []
    for blk in (xl, xs, xr):
        bucket_row, band_row = label_rows(blk[...], features, SRC_HI, SRC_LO, SRC_BAND)
        src_blocks.append((blk, bucket_row, band_row))
    tgt_out[...] = softmax_read(
        tsend[:, :features], y_bucket, None, src_blocks, features, scaling, False)

    a2a_copy(partner, g).wait_send()

    def a2a_sent(j, carry):
        a2a_copy(far_peer(j), g).wait_send()
        return carry

    lax.fori_loop(0, n_src - 2, a2a_sent, 0)

    def fw_sent(s, carry):
        for c in forward(s):
            c.wait_send()
        return carry

    lax.fori_loop(0, n_src, fw_sent, 0)


def write_kernel(src_in, tgt_in, src_res, tgt_res, sems):
    copies = [pltpu.make_async_copy(src_in, src_res, sems.at[0]),
              pltpu.make_async_copy(tgt_in, tgt_res, sems.at[1])]
    for c in copies:
        c.start()
    for c in copies:
        c.wait()


def write_out(src_read, tgt_read):
    return pl.pallas_call(
        write_kernel,
        out_shape=(jax.ShapeDtypeStruct(src_read.shape, src_read.dtype),
                   jax.ShapeDtypeStruct(tgt_read.shape, tgt_read.dtype)),
        in_specs=[pl.BlockSpec(memory_space=pltpu.VMEM)] * 2,
        out_specs=(pl.BlockSpec(memory_space=pl.ANY),) * 2,
        scratch_shapes=[pltpu.SemaphoreType.DMA((2,))],
    )(src_read, tgt_read)


def on_device(source, target, src_bucket, tgt_bucket, band, route):
    row_count, feature_count = source.shape
    src_count = lax.axis_size("src")
    tgt_count = lax.axis_size("tgt")
    per_peer = row_count // src_count
    scaling = 2.0 / math.sqrt(feature_count)

    width = feature_count + LABEL_LANES
    ints = [v.reshape(1, row_count) for v in (src_bucket, band, route, tgt_bucket)]

    block = jax.ShapeDtypeStruct((row_count, feature_count), jnp.float32)
    vmem = pl.BlockSpec(memory_space=pltpu.VMEM)
    reads = pl.pallas_call(
        functools.partial(kernel, feature_count, scaling),
        out_shape=(block, block),
        in_specs=[pl.BlockSpec(memory_space=pl.ANY)] * 6,
        out_specs=(vmem, vmem),
        scratch_shapes=[pltpu.VMEM((row_count, feature_count), jnp.bfloat16)] * 2
        + [pltpu.VMEM((1, row_count), jnp.int32)] * 4
        + [pltpu.VMEM((row_count, width), jnp.bfloat16)] * 7
        + [
            pltpu.SemaphoreType.DMA((src_count,)),
            pltpu.SemaphoreType.DMA((src_count,)),
            pltpu.SemaphoreType.DMA((2 * src_count,)),
            pltpu.SemaphoreType.DMA((2 * src_count,)),
            pltpu.SemaphoreType.DMA((2,)),
            pltpu.SemaphoreType.DMA((2,)),
            pltpu.SemaphoreType.DMA((7,)),
        ],
        compiler_params=pltpu.CompilerParams(collective_id=0, has_side_effects=True),
    )(source, target, *ints)
    return write_out(*reads)


def solution(mesh):
    placed = (
        P(("src", "tgt"), None),
        P(("src", "tgt"), None),
        P(("src", "tgt")),
        P(("src", "tgt")),
        P(("src", "tgt")),
        P(("src", "tgt")),
    )
    return jax.shard_map(
        on_device,
        mesh=mesh,
        in_specs=placed,
        out_specs=(P(("src", "tgt"), None), P(("src", "tgt"), None)),
        check_vma=False,
    )
```

```python
import functools
import math

import jax
import jax.numpy as jnp
from jax import lax
from jax.experimental import pallas as pl
from jax.experimental.pallas import tpu as pltpu
from jax.sharding import PartitionSpec as P

lowest = -1e30
MESH = pl.DeviceIdType.MESH
LABEL_LANES = 128
DIGIT = 64
SRC_HI, SRC_LO, SRC_BAND, TGT_HI, TGT_LO = 0, 1, 2, 4, 5


def softmax_read(main, main_bucket, band_col, others, features, scaling, band_of_rows):
    scores, masks = [], []
    for blk, bucket_row, band_row in others:
        s = lax.dot_general(
            main, blk[:, :features], (((1,), (1,)), ((), ())),
            preferred_element_type=jnp.float32) * scaling
        band = band_col if band_of_rows else band_row
        ok = (jnp.abs(main_bucket - bucket_row) <= band) & (
            (main_bucket >> 7) == (bucket_row >> 7))
        scores.append(jnp.where(ok, s, lowest))
        masks.append(ok)
    top = functools.reduce(jnp.maximum, [jnp.max(s, axis=1, keepdims=True) for s in scores])
    total = jnp.zeros_like(top)
    read = jnp.zeros((main.shape[0], features), jnp.float32)
    for s, ok, (blk, _, _) in zip(scores, masks, others):
        w = jnp.where(ok, jnp.exp(s - top), 0.0)
        total = total + jnp.sum(w, axis=1, keepdims=True)
        read = read + jnp.dot(w.astype(jnp.bfloat16), blk[:, :features],
                              preferred_element_type=jnp.float32)
    return read / total


def label_rows(blk, features, hi, lo, band=None):
    slab = blk[:, features:].astype(jnp.float32).T.astype(jnp.int32)
    bucket = slab[hi:hi + 1, :] * DIGIT + slab[lo:lo + 1, :]
    return bucket, (slab[band:band + 1, :] if band is not None else None)


def shift_of(divisor):
    assert divisor & (divisor - 1) == 0
    return divisor.bit_length() - 1


def kernel(features, scaling, source_hbm, target_hbm, src_bucket_hbm, band_hbm, route_hbm,
           tgt_bucket_hbm, src_out, tgt_out,
           source, target, src_bucket, band, route, tgt_bucket, xsend, tsend, xs, xl, xr, tl, tr,
           a2a_send, a2a_recv, fw_send, fw_recv, nb_send, nb_recv, local_sem):
    g = lax.axis_index("src")
    t = lax.axis_index("tgt")
    n_src = lax.axis_size("src")
    n_tgt = lax.axis_size("tgt")
    rows = source.shape[0]
    span = rows // n_src
    n_z = n_src // 2
    z = g // 2
    core = g % 2
    partner = z * 2 + 1 - core
    left = lax.rem(t + n_tgt - 1, n_tgt)
    right = lax.rem(t + 1, n_tgt)

    def far_peer(j):
        kz = j // 2 + 1
        offset = ((kz + 1) // 2) * (2 * (kz % 2) - 1)
        return ((z + offset + n_z) & (n_z - 1)) * 2 + j % 2

    shift_of(n_z)

    pairs = ((source_hbm, source), (target_hbm, target), (src_bucket_hbm, src_bucket),
             (band_hbm, band), (route_hbm, route), (tgt_bucket_hbm, tgt_bucket))
    barrier = pltpu.get_barrier_semaphore()

    for j in range(n_src - 3, -1, -1):
        pl.semaphore_signal(barrier, inc=1, device_id=(far_peer(j), t), device_id_type=MESH)
    pl.semaphore_signal(barrier, inc=1, device_id=(g, left), device_id_type=MESH)
    pl.semaphore_signal(barrier, inc=1, device_id=(g, right), device_id_type=MESH)
    pl.semaphore_signal(barrier, inc=1, device_id=(partner, t), device_id_type=MESH)

    loads = [pltpu.make_async_copy(h, v, local_sem.at[1 + i]) for i, (h, v) in enumerate(pairs)]
    for c in loads:
        c.start()
    for c in loads:
        c.wait()

    where_to = route[...]
    dest = (where_to >> shift_of(rows * n_tgt)) * span + (where_to & ((1 << shift_of(span)) - 1))
    sb = src_bucket[...]
    tb = tgt_bucket[...]
    label_rows_of = {
        SRC_HI: sb >> shift_of(DIGIT), SRC_LO: sb & (DIGIT - 1), SRC_BAND: band[...],
        TGT_HI: tb >> shift_of(DIGIT), TGT_LO: tb & (DIGIT - 1),
    }
    slot = lax.broadcasted_iota(jnp.int32, (rows, rows), 0)
    lane = lax.broadcasted_iota(jnp.int32, (rows, LABEL_LANES), 1)
    onehot = (slot == dest).astype(jnp.float32)
    ident = (slot == lax.broadcasted_iota(jnp.int32, (rows, rows), 1)).astype(jnp.float32)

    def label_slab(select, kinds):
        slab = jnp.zeros((rows, LABEL_LANES), jnp.float32)
        for k in kinds:
            row = label_rows_of[k].astype(jnp.float32)
            column = jnp.sum(select * row, axis=1, keepdims=True)
            slab = jnp.where(lane == k, column, slab)
        return slab.astype(jnp.bfloat16)

    xsend[:, :features] = jnp.dot(
        onehot.astype(jnp.bfloat16), source[...],
        preferred_element_type=jnp.float32).astype(jnp.bfloat16)
    xsend[:, features:] = label_slab(onehot, (SRC_HI, SRC_LO, SRC_BAND))
    tsend[:, :features] = target[...]
    tsend[:, features:] = label_slab(ident, (TGT_HI, TGT_LO))

    pl.semaphore_wait(barrier, n_src + 1)

    t_to_right = pltpu.make_async_remote_copy(
        tsend, tl, nb_send.at[0], nb_recv.at[0], device_id=(g, right), device_id_type=MESH)
    t_to_left = pltpu.make_async_remote_copy(
        tsend, tr, nb_send.at[1], nb_recv.at[1], device_id=(g, left), device_id_type=MESH)

    def a2a_copy(peer, sender):
        return pltpu.make_async_remote_copy(
            xsend.at[pl.ds(peer * span, span)],
            xs.at[pl.ds(sender * span, span)],
            a2a_send.at[peer],
            a2a_recv.at[sender],
            device_id=(peer, t),
            device_id_type=MESH,
        )

    own = pltpu.make_async_copy(
        xsend.at[pl.ds(g * span, span)], xs.at[pl.ds(g * span, span)], local_sem.at[0])
    own.start()
    a2a_copy(partner, g).start()

    for j in range(n_src - 2):
        a2a_copy(far_peer(j), g).start()
    t_to_right.start()
    t_to_left.start()

    def forward(sender):
        rows_of = pl.ds(sender * span, span)
        return (
            pltpu.make_async_remote_copy(
                xs.at[rows_of], xl.at[rows_of], fw_send.at[sender], fw_recv.at[sender],
                device_id=(g, right), device_id_type=MESH),
            pltpu.make_async_remote_copy(
                xs.at[rows_of], xr.at[rows_of], fw_send.at[n_src + sender],
                fw_recv.at[n_src + sender], device_id=(g, left), device_id_type=MESH),
        )

    def arrive_and_forward(sender):
        rows_of = pl.ds(sender * span, span)
        pltpu.make_async_remote_copy(
            xsend.at[rows_of], xs.at[rows_of], a2a_send.at[sender], a2a_recv.at[sender],
            device_id=(sender, t), device_id_type=MESH).wait_recv()
        for c in forward(sender):
            c.start()

    own.wait()
    for c in forward(g):
        c.start()
    arrive_and_forward(partner)

    for j in range(n_src - 2):
        arrive_and_forward(far_peer(j))

    t_to_right.wait()
    t_to_left.wait()

    x_cols = xs[:, features:].astype(jnp.float32).astype(jnp.int32)
    x_bucket = x_cols[:, SRC_HI:SRC_HI + 1] * DIGIT + x_cols[:, SRC_LO:SRC_LO + 1]
    x_band = x_cols[:, SRC_BAND:SRC_BAND + 1]
    tgt_blocks = []
    for blk in (tl, tsend, tr):
        bucket_row, _ = label_rows(blk[...], features, TGT_HI, TGT_LO)
        tgt_blocks.append((blk, bucket_row, None))
    src_out[...] = softmax_read(
        xs[:, :features], x_bucket, x_band, tgt_blocks, features, scaling, True)

    a2a_copy(partner, g).wait_send()

    for j in range(n_src - 2):
        a2a_copy(far_peer(j), g).wait_send()

    def fw_done(s, carry):
        for c in forward(s):
            c.wait_send()
            c.wait_recv()
        return carry

    lax.fori_loop(0, n_src, fw_done, 0)

    y_cols = tsend[:, features:].astype(jnp.float32).astype(jnp.int32)
    y_bucket = y_cols[:, TGT_HI:TGT_HI + 1] * DIGIT + y_cols[:, TGT_LO:TGT_LO + 1]
    src_blocks = []
    for blk in (xl, xs, xr):
        bucket_row, band_row = label_rows(blk[...], features, SRC_HI, SRC_LO, SRC_BAND)
        src_blocks.append((blk, bucket_row, band_row))
    tgt_out[...] = softmax_read(
        tsend[:, :features], y_bucket, None, src_blocks, features, scaling, False)


def write_kernel(src_in, tgt_in, src_res, tgt_res, sems):
    copies = [pltpu.make_async_copy(src_in, src_res, sems.at[0]),
              pltpu.make_async_copy(tgt_in, tgt_res, sems.at[1])]
    for c in copies:
        c.start()
    for c in copies:
        c.wait()


def write_out(src_read, tgt_read):
    return pl.pallas_call(
        write_kernel,
        out_shape=(jax.ShapeDtypeStruct(src_read.shape, src_read.dtype),
                   jax.ShapeDtypeStruct(tgt_read.shape, tgt_read.dtype)),
        in_specs=[pl.BlockSpec(memory_space=pltpu.VMEM)] * 2,
        out_specs=(pl.BlockSpec(memory_space=pl.ANY),) * 2,
        scratch_shapes=[pltpu.SemaphoreType.DMA((2,))],
    )(src_read, tgt_read)


def on_device(source, target, src_bucket, tgt_bucket, band, route):
    row_count, feature_count = source.shape
    src_count = lax.axis_size("src")
    tgt_count = lax.axis_size("tgt")
    per_peer = row_count // src_count
    scaling = 2.0 / math.sqrt(feature_count)

    width = feature_count + LABEL_LANES
    ints = [v.reshape(1, row_count) for v in (src_bucket, band, route, tgt_bucket)]

    block = jax.ShapeDtypeStruct((row_count, feature_count), jnp.float32)
    vmem = pl.BlockSpec(memory_space=pltpu.VMEM)
    reads = pl.pallas_call(
        functools.partial(kernel, feature_count, scaling),
        out_shape=(block, block),
        in_specs=[pl.BlockSpec(memory_space=pl.ANY)] * 6,
        out_specs=(vmem, vmem),
        scratch_shapes=[pltpu.VMEM((row_count, feature_count), jnp.bfloat16)] * 2
        + [pltpu.VMEM((1, row_count), jnp.int32)] * 4
        + [pltpu.VMEM((row_count, width), jnp.bfloat16)] * 7
        + [
            pltpu.SemaphoreType.DMA((src_count,)),
            pltpu.SemaphoreType.DMA((src_count,)),
            pltpu.SemaphoreType.DMA((2 * src_count,)),
            pltpu.SemaphoreType.DMA((2 * src_count,)),
            pltpu.SemaphoreType.DMA((2,)),
            pltpu.SemaphoreType.DMA((2,)),
            pltpu.SemaphoreType.DMA((7,)),
        ],
        compiler_params=pltpu.CompilerParams(collective_id=0, has_side_effects=True),
    )(source, target, *ints)
    return write_out(*reads)


def solution(mesh):
    placed = (
        P(("src", "tgt"), None),
        P(("src", "tgt"), None),
        P(("src", "tgt")),
        P(("src", "tgt")),
        P(("src", "tgt")),
        P(("src", "tgt")),
    )
    return jax.shard_map(
        on_device,
        mesh=mesh,
        in_specs=placed,
        out_specs=(P(("src", "tgt"), None), P(("src", "tgt"), None)),
        check_vma=False,
    )
```

```python
import functools
import math

import jax
import jax.numpy as jnp
from jax import lax
from jax.experimental import pallas as pl
from jax.experimental.pallas import tpu as pltpu
from jax.sharding import PartitionSpec as P

lowest = -1e30
MESH = pl.DeviceIdType.MESH
LABEL_LANES = 128
DIGIT = 64
SRC_HI, SRC_LO, SRC_BAND, TGT_HI, TGT_LO = 0, 1, 2, 4, 5


def softmax_read(main, main_bucket, band_col, others, features, scaling, band_of_rows):
    scores, masks = [], []
    for blk, bucket_row, band_row in others:
        s = lax.dot_general(
            main, blk[:, :features], (((1,), (1,)), ((), ())),
            preferred_element_type=jnp.float32) * scaling
        band = band_col if band_of_rows else band_row
        ok = (jnp.abs(main_bucket - bucket_row) <= band) & (
            (main_bucket >> 7) == (bucket_row >> 7))
        scores.append(jnp.where(ok, s, lowest))
        masks.append(ok)
    top = functools.reduce(jnp.maximum, [jnp.max(s, axis=1, keepdims=True) for s in scores])
    total = jnp.zeros_like(top)
    read = jnp.zeros((main.shape[0], features), jnp.float32)
    for s, ok, (blk, _, _) in zip(scores, masks, others):
        w = jnp.where(ok, jnp.exp(s - top), 0.0)
        total = total + jnp.sum(w, axis=1, keepdims=True)
        read = read + jnp.dot(w.astype(jnp.bfloat16), blk[:, :features],
                              preferred_element_type=jnp.float32)
    return read / total


def label_rows(blk, features, hi, lo, band=None):
    slab = blk[:, features:].astype(jnp.float32).T.astype(jnp.int32)
    bucket = slab[hi:hi + 1, :] * DIGIT + slab[lo:lo + 1, :]
    return bucket, (slab[band:band + 1, :] if band is not None else None)


def shift_of(divisor):
    assert divisor & (divisor - 1) == 0
    return divisor.bit_length() - 1


def kernel(features, scaling, source_hbm, target_hbm, src_bucket_hbm, band_hbm, route_hbm,
           tgt_bucket_hbm, src_out, tgt_out,
           source, target, src_bucket, band, route, tgt_bucket, xsend, tsend, xs, xl, xr, tl, tr,
           a2a_send, a2a_recv, fw_send, fw_recv, nb_send, nb_recv, local_sem):
    g = lax.axis_index("src")
    t = lax.axis_index("tgt")
    n_src = lax.axis_size("src")
    n_tgt = lax.axis_size("tgt")
    rows = source.shape[0]
    span = rows // n_src
    n_z = n_src // 2
    z = g // 2
    core = g % 2
    partner = z * 2 + 1 - core
    left = lax.rem(t + n_tgt - 1, n_tgt)
    right = lax.rem(t + 1, n_tgt)

    def far_peer(j):
        kz = j // 2 + 1
        offset = ((kz + 1) // 2) * (2 * (kz % 2) - 1)
        return ((z + offset + n_z) & (n_z - 1)) * 2 + j % 2

    shift_of(n_z)

    pairs = ((source_hbm, source), (target_hbm, target), (src_bucket_hbm, src_bucket),
             (band_hbm, band), (route_hbm, route), (tgt_bucket_hbm, tgt_bucket))
    barrier = pltpu.get_barrier_semaphore()

    for j in range(n_src - 3, -1, -1):
        pl.semaphore_signal(barrier, inc=1, device_id=(far_peer(j), t), device_id_type=MESH)
    pl.semaphore_signal(barrier, inc=1, device_id=(g, left), device_id_type=MESH)
    pl.semaphore_signal(barrier, inc=1, device_id=(g, right), device_id_type=MESH)
    pl.semaphore_signal(barrier, inc=1, device_id=(partner, t), device_id_type=MESH)

    loads = [pltpu.make_async_copy(h, v, local_sem.at[1 + i]) for i, (h, v) in enumerate(pairs)]
    for c in loads:
        c.start()
    for c in loads:
        c.wait()

    where_to = route[...]
    dest = (where_to >> shift_of(rows * n_tgt)) * span + (where_to & ((1 << shift_of(span)) - 1))
    sb = src_bucket[...]
    tb = tgt_bucket[...]
    label_rows_of = {
        SRC_HI: sb >> shift_of(DIGIT), SRC_LO: sb & (DIGIT - 1), SRC_BAND: band[...],
        TGT_HI: tb >> shift_of(DIGIT), TGT_LO: tb & (DIGIT - 1),
    }
    slot = lax.broadcasted_iota(jnp.int32, (rows, rows), 0)
    lane = lax.broadcasted_iota(jnp.int32, (rows, LABEL_LANES), 1)
    onehot = (slot == dest).astype(jnp.float32)
    ident = (slot == lax.broadcasted_iota(jnp.int32, (rows, rows), 1)).astype(jnp.float32)

    def label_slab(select, kinds):
        slab = jnp.zeros((rows, LABEL_LANES), jnp.float32)
        for k in kinds:
            row = label_rows_of[k].astype(jnp.float32)
            column = jnp.sum(select * row, axis=1, keepdims=True)
            slab = jnp.where(lane == k, column, slab)
        return slab.astype(jnp.bfloat16)

    xsend[:, :features] = jnp.dot(
        onehot.astype(jnp.bfloat16), source[...],
        preferred_element_type=jnp.float32).astype(jnp.bfloat16)
    xsend[:, features:] = label_slab(onehot, (SRC_HI, SRC_LO, SRC_BAND))
    tsend[:, :features] = target[...]
    tsend[:, features:] = label_slab(ident, (TGT_HI, TGT_LO))

    pl.semaphore_wait(barrier, n_src + 1)

    t_to_right = pltpu.make_async_remote_copy(
        tsend, tl, nb_send.at[0], nb_recv.at[0], device_id=(g, right), device_id_type=MESH)
    t_to_left = pltpu.make_async_remote_copy(
        tsend, tr, nb_send.at[1], nb_recv.at[1], device_id=(g, left), device_id_type=MESH)

    def a2a_copy(peer, sender):
        return pltpu.make_async_remote_copy(
            xsend.at[pl.ds(peer * span, span)],
            xs.at[pl.ds(sender * span, span)],
            a2a_send.at[peer],
            a2a_recv.at[sender],
            device_id=(peer, t),
            device_id_type=MESH,
        )

    own = pltpu.make_async_copy(
        xsend.at[pl.ds(g * span, span)], xs.at[pl.ds(g * span, span)], local_sem.at[0])
    own.start()
    a2a_copy(partner, g).start()

    def mirrored_peer(j):
        kz = j // 2 + 1
        offset = ((kz + 1) // 2) * (2 * (kz % 2) - 1)
        return ((z + offset * (1 - 2 * core) + n_z) & (n_z - 1)) * 2 + j % 2

    for j in range(n_src - 2):
        a2a_copy(mirrored_peer(j), g).start()
    t_to_right.start()
    t_to_left.start()

    def forward(sender):
        rows_of = pl.ds(sender * span, span)
        return (
            pltpu.make_async_remote_copy(
                xs.at[rows_of], xl.at[rows_of], fw_send.at[sender], fw_recv.at[sender],
                device_id=(g, right), device_id_type=MESH),
            pltpu.make_async_remote_copy(
                xs.at[rows_of], xr.at[rows_of], fw_send.at[n_src + sender],
                fw_recv.at[n_src + sender], device_id=(g, left), device_id_type=MESH),
        )

    def arrive_and_forward(sender):
        rows_of = pl.ds(sender * span, span)
        pltpu.make_async_remote_copy(
            xsend.at[rows_of], xs.at[rows_of], a2a_send.at[sender], a2a_recv.at[sender],
            device_id=(sender, t), device_id_type=MESH).wait_recv()
        for c in forward(sender):
            c.start()

    own.wait()
    for c in forward(g):
        c.start()
    arrive_and_forward(partner)

    for j in range(n_src - 2):
        arrive_and_forward(far_peer(j))

    t_to_right.wait()
    t_to_left.wait()

    x_cols = xs[:, features:].astype(jnp.float32).astype(jnp.int32)
    x_bucket = x_cols[:, SRC_HI:SRC_HI + 1] * DIGIT + x_cols[:, SRC_LO:SRC_LO + 1]
    x_band = x_cols[:, SRC_BAND:SRC_BAND + 1]
    tgt_blocks = []
    for blk in (tl, tsend, tr):
        bucket_row, _ = label_rows(blk[...], features, TGT_HI, TGT_LO)
        tgt_blocks.append((blk, bucket_row, None))
    src_out[...] = softmax_read(
        xs[:, :features], x_bucket, x_band, tgt_blocks, features, scaling, True)

    a2a_copy(partner, g).wait_send()

    def a2a_sent(j, carry):
        a2a_copy(far_peer(j), g).wait_send()
        return carry

    lax.fori_loop(0, n_src - 2, a2a_sent, 0)

    def fw_done(s, carry):
        for c in forward(s):
            c.wait_send()
            c.wait_recv()
        return carry

    lax.fori_loop(0, n_src, fw_done, 0)

    y_cols = tsend[:, features:].astype(jnp.float32).astype(jnp.int32)
    y_bucket = y_cols[:, TGT_HI:TGT_HI + 1] * DIGIT + y_cols[:, TGT_LO:TGT_LO + 1]
    src_blocks = []
    for blk in (xl, xs, xr):
        bucket_row, band_row = label_rows(blk[...], features, SRC_HI, SRC_LO, SRC_BAND)
        src_blocks.append((blk, bucket_row, band_row))
    tgt_out[...] = softmax_read(
        tsend[:, :features], y_bucket, None, src_blocks, features, scaling, False)


def write_kernel(src_in, tgt_in, src_res, tgt_res, sems):
    copies = [pltpu.make_async_copy(src_in, src_res, sems.at[0]),
              pltpu.make_async_copy(tgt_in, tgt_res, sems.at[1])]
    for c in copies:
        c.start()
    for c in copies:
        c.wait()


def write_out(src_read, tgt_read):
    return pl.pallas_call(
        write_kernel,
        out_shape=(jax.ShapeDtypeStruct(src_read.shape, src_read.dtype),
                   jax.ShapeDtypeStruct(tgt_read.shape, tgt_read.dtype)),
        in_specs=[pl.BlockSpec(memory_space=pltpu.VMEM)] * 2,
        out_specs=(pl.BlockSpec(memory_space=pl.ANY),) * 2,
        scratch_shapes=[pltpu.SemaphoreType.DMA((2,))],
    )(src_read, tgt_read)


def on_device(source, target, src_bucket, tgt_bucket, band, route):
    row_count, feature_count = source.shape
    src_count = lax.axis_size("src")
    tgt_count = lax.axis_size("tgt")
    per_peer = row_count // src_count
    scaling = 2.0 / math.sqrt(feature_count)

    width = feature_count + LABEL_LANES
    ints = [v.reshape(1, row_count) for v in (src_bucket, band, route, tgt_bucket)]

    block = jax.ShapeDtypeStruct((row_count, feature_count), jnp.float32)
    vmem = pl.BlockSpec(memory_space=pltpu.VMEM)
    reads = pl.pallas_call(
        functools.partial(kernel, feature_count, scaling),
        out_shape=(block, block),
        in_specs=[pl.BlockSpec(memory_space=pl.ANY)] * 6,
        out_specs=(vmem, vmem),
        scratch_shapes=[pltpu.VMEM((row_count, feature_count), jnp.bfloat16)] * 2
        + [pltpu.VMEM((1, row_count), jnp.int32)] * 4
        + [pltpu.VMEM((row_count, width), jnp.bfloat16)] * 7
        + [
            pltpu.SemaphoreType.DMA((src_count,)),
            pltpu.SemaphoreType.DMA((src_count,)),
            pltpu.SemaphoreType.DMA((2 * src_count,)),
            pltpu.SemaphoreType.DMA((2 * src_count,)),
            pltpu.SemaphoreType.DMA((2,)),
            pltpu.SemaphoreType.DMA((2,)),
            pltpu.SemaphoreType.DMA((7,)),
        ],
        compiler_params=pltpu.CompilerParams(collective_id=0, has_side_effects=True),
    )(source, target, *ints)
    return write_out(*reads)


def solution(mesh):
    placed = (
        P(("src", "tgt"), None),
        P(("src", "tgt"), None),
        P(("src", "tgt")),
        P(("src", "tgt")),
        P(("src", "tgt")),
        P(("src", "tgt")),
    )
    return jax.shard_map(
        on_device,
        mesh=mesh,
        in_specs=placed,
        out_specs=(P(("src", "tgt"), None), P(("src", "tgt"), None)),
        check_vma=False,
    )
```

```python
import functools
import math

import jax
import jax.numpy as jnp
from jax import lax
from jax.experimental import pallas as pl
from jax.experimental.pallas import tpu as pltpu
from jax.sharding import PartitionSpec as P

lowest = -1e30
MESH = pl.DeviceIdType.MESH
LABEL_LANES = 128
DIGIT = 64
SRC_HI, SRC_LO, SRC_BAND, TGT_HI, TGT_LO = 0, 1, 2, 4, 5


def softmax_read(main, main_bucket, band_col, others, features, scaling, band_of_rows):
    scores, masks = [], []
    for blk, bucket_row, band_row in others:
        s = lax.dot_general(
            main, blk[:, :features], (((1,), (1,)), ((), ())),
            preferred_element_type=jnp.float32) * scaling
        band = band_col if band_of_rows else band_row
        ok = (jnp.abs(main_bucket - bucket_row) <= band) & (
            (main_bucket >> 7) == (bucket_row >> 7))
        scores.append(jnp.where(ok, s, lowest))
        masks.append(ok)
    top = functools.reduce(jnp.maximum, [jnp.max(s, axis=1, keepdims=True) for s in scores])
    total = jnp.zeros_like(top)
    read = jnp.zeros((main.shape[0], features), jnp.float32)
    for s, ok, (blk, _, _) in zip(scores, masks, others):
        w = jnp.where(ok, jnp.exp(s - top), 0.0)
        total = total + jnp.sum(w, axis=1, keepdims=True)
        read = read + jnp.dot(w.astype(jnp.bfloat16), blk[:, :features],
                              preferred_element_type=jnp.float32)
    return read / total


def label_rows(blk, features, hi, lo, band=None):
    slab = blk[:, features:].astype(jnp.float32).T.astype(jnp.int32)
    bucket = slab[hi:hi + 1, :] * DIGIT + slab[lo:lo + 1, :]
    return bucket, (slab[band:band + 1, :] if band is not None else None)


def shift_of(divisor):
    assert divisor & (divisor - 1) == 0
    return divisor.bit_length() - 1


def kernel(features, scaling, source_hbm, target_hbm, src_bucket_hbm, band_hbm, route_hbm,
           tgt_bucket_hbm, src_out, tgt_out,
           source, target, src_bucket, band, route, tgt_bucket, xsend, tsend, xs, xl, xr, tl, tr,
           a2a_send, a2a_recv, fw_send, fw_recv, nb_send, nb_recv, local_sem):
    g = lax.axis_index("src")
    t = lax.axis_index("tgt")
    n_src = lax.axis_size("src")
    n_tgt = lax.axis_size("tgt")
    rows = source.shape[0]
    span = rows // n_src
    n_z = n_src // 2
    z = g // 2
    core = g % 2
    partner = z * 2 + 1 - core
    left = lax.rem(t + n_tgt - 1, n_tgt)
    right = lax.rem(t + 1, n_tgt)

    def far_peer(j):
        kz = j // 2 + 1
        offset = ((kz + 1) // 2) * (2 * (kz % 2) - 1)
        return ((z + offset + n_z) & (n_z - 1)) * 2 + j % 2

    shift_of(n_z)

    pairs = ((source_hbm, source), (target_hbm, target), (src_bucket_hbm, src_bucket),
             (band_hbm, band), (route_hbm, route), (tgt_bucket_hbm, tgt_bucket))
    barrier = pltpu.get_barrier_semaphore()

    for j in range(n_src - 3, -1, -1):
        pl.semaphore_signal(barrier, inc=1, device_id=(far_peer(j), t), device_id_type=MESH)
    pl.semaphore_signal(barrier, inc=1, device_id=(g, left), device_id_type=MESH)
    pl.semaphore_signal(barrier, inc=1, device_id=(g, right), device_id_type=MESH)
    pl.semaphore_signal(barrier, inc=1, device_id=(partner, t), device_id_type=MESH)

    loads = [pltpu.make_async_copy(h, v, local_sem.at[1 + i]) for i, (h, v) in enumerate(pairs)]
    for c in loads:
        c.start()
    for c in loads:
        c.wait()

    where_to = route[...]
    dest = (where_to >> shift_of(rows * n_tgt)) * span + (where_to & ((1 << shift_of(span)) - 1))
    sb = src_bucket[...]
    tb = tgt_bucket[...]
    label_rows_of = {
        SRC_HI: sb >> shift_of(DIGIT), SRC_LO: sb & (DIGIT - 1), SRC_BAND: band[...],
        TGT_HI: tb >> shift_of(DIGIT), TGT_LO: tb & (DIGIT - 1),
    }
    slot = lax.broadcasted_iota(jnp.int32, (rows, rows), 0)
    lane = lax.broadcasted_iota(jnp.int32, (rows, LABEL_LANES), 1)
    onehot = (slot == dest).astype(jnp.float32)
    ident = (slot == lax.broadcasted_iota(jnp.int32, (rows, rows), 1)).astype(jnp.float32)

    def label_slab(select, kinds):
        slab = jnp.zeros((rows, LABEL_LANES), jnp.float32)
        for k in kinds:
            row = label_rows_of[k].astype(jnp.float32)
            column = jnp.sum(select * row, axis=1, keepdims=True)
            slab = jnp.where(lane == k, column, slab)
        return slab.astype(jnp.bfloat16)

    xsend[:, :features] = jnp.dot(
        onehot.astype(jnp.bfloat16), source[...],
        preferred_element_type=jnp.float32).astype(jnp.bfloat16)
    xsend[:, features:] = label_slab(onehot, (SRC_HI, SRC_LO, SRC_BAND))
    tsend[:, :features] = target[...]
    tsend[:, features:] = label_slab(ident, (TGT_HI, TGT_LO))

    pl.semaphore_wait(barrier, n_src + 1)

    t_to_right = pltpu.make_async_remote_copy(
        tsend, tl, nb_send.at[0], nb_recv.at[0], device_id=(g, right), device_id_type=MESH)
    t_to_left = pltpu.make_async_remote_copy(
        tsend, tr, nb_send.at[1], nb_recv.at[1], device_id=(g, left), device_id_type=MESH)

    def a2a_copy(peer, sender):
        return pltpu.make_async_remote_copy(
            xsend.at[pl.ds(peer * span, span)],
            xs.at[pl.ds(sender * span, span)],
            a2a_send.at[peer],
            a2a_recv.at[sender],
            device_id=(peer, t),
            device_id_type=MESH,
        )

    own = pltpu.make_async_copy(
        xsend.at[pl.ds(g * span, span)], xs.at[pl.ds(g * span, span)], local_sem.at[0])
    own.start()
    a2a_copy(partner, g).start()

    for j in range(n_src - 2):
        a2a_copy(far_peer(j), g).start()
    t_to_right.start()
    t_to_left.start()

    def forward(sender):
        rows_of = pl.ds(sender * span, span)
        return (
            pltpu.make_async_remote_copy(
                xs.at[rows_of], xl.at[rows_of], fw_send.at[sender], fw_recv.at[sender],
                device_id=(g, right), device_id_type=MESH),
            pltpu.make_async_remote_copy(
                xs.at[rows_of], xr.at[rows_of], fw_send.at[n_src + sender],
                fw_recv.at[n_src + sender], device_id=(g, left), device_id_type=MESH),
        )

    def arrive_and_forward(sender):
        rows_of = pl.ds(sender * span, span)
        pltpu.make_async_remote_copy(
            xsend.at[rows_of], xs.at[rows_of], a2a_send.at[sender], a2a_recv.at[sender],
            device_id=(sender, t), device_id_type=MESH).wait_recv()
        for c in forward(sender):
            c.start()

    own.wait()
    for c in forward(g):
        c.start()
    arrive_and_forward(partner)

    for j in range(n_src - 2):
        arrive_and_forward(far_peer(j))

    t_to_right.wait()
    t_to_left.wait()

    x_cols = xs[:, features:].astype(jnp.float32).astype(jnp.int32)
    x_bucket = x_cols[:, SRC_HI:SRC_HI + 1] * DIGIT + x_cols[:, SRC_LO:SRC_LO + 1]
    x_band = x_cols[:, SRC_BAND:SRC_BAND + 1]
    tgt_blocks = []
    for blk in (tl, tsend, tr):
        bucket_row, _ = label_rows(blk[...], features, TGT_HI, TGT_LO)
        tgt_blocks.append((blk, bucket_row, None))
    src_out[...] = softmax_read(
        xs[:, :features], x_bucket, x_band, tgt_blocks, features, scaling, True)

    a2a_copy(partner, g).wait_send()

    def a2a_sent(j, carry):
        a2a_copy(far_peer(j), g).wait_send()
        return carry

    lax.fori_loop(0, n_src - 2, a2a_sent, 0)

    def fw_done(s, carry):
        for c in forward(s):
            c.wait_send()
            c.wait_recv()
        return carry

    lax.fori_loop(0, n_src, fw_done, 0)

    y_cols = tsend[:, features:].astype(jnp.float32).astype(jnp.int32)
    y_bucket = y_cols[:, TGT_HI:TGT_HI + 1] * DIGIT + y_cols[:, TGT_LO:TGT_LO + 1]
    src_blocks = []
    for blk in (xl, xs, xr):
        bucket_row, band_row = label_rows(blk[...], features, SRC_HI, SRC_LO, SRC_BAND)
        src_blocks.append((blk, bucket_row, band_row))
    tgt_out[...] = softmax_read(
        tsend[:, :features], y_bucket, None, src_blocks, features, scaling, False)


def write_kernel(src_in, tgt_in, src_res, tgt_res):
    src_res[...] = src_in[...]
    tgt_res[...] = tgt_in[...]


def write_out(src_read, tgt_read, steps=4):
    rows, columns = src_read.shape
    spec = pl.BlockSpec((rows // steps, columns), lambda i: (i, 0))
    return pl.pallas_call(
        write_kernel,
        grid=(steps,),
        out_shape=(jax.ShapeDtypeStruct(src_read.shape, src_read.dtype),
                   jax.ShapeDtypeStruct(tgt_read.shape, tgt_read.dtype)),
        in_specs=[spec, spec],
        out_specs=(spec, spec),
    )(src_read, tgt_read)


def on_device(source, target, src_bucket, tgt_bucket, band, route):
    row_count, feature_count = source.shape
    src_count = lax.axis_size("src")
    tgt_count = lax.axis_size("tgt")
    per_peer = row_count // src_count
    scaling = 2.0 / math.sqrt(feature_count)

    width = feature_count + LABEL_LANES
    ints = [v.reshape(1, row_count) for v in (src_bucket, band, route, tgt_bucket)]

    block = jax.ShapeDtypeStruct((row_count, feature_count), jnp.float32)
    vmem = pl.BlockSpec(memory_space=pltpu.VMEM)
    reads = pl.pallas_call(
        functools.partial(kernel, feature_count, scaling),
        out_shape=(block, block),
        in_specs=[pl.BlockSpec(memory_space=pl.ANY)] * 6,
        out_specs=(vmem, vmem),
        scratch_shapes=[pltpu.VMEM((row_count, feature_count), jnp.bfloat16)] * 2
        + [pltpu.VMEM((1, row_count), jnp.int32)] * 4
        + [pltpu.VMEM((row_count, width), jnp.bfloat16)] * 7
        + [
            pltpu.SemaphoreType.DMA((src_count,)),
            pltpu.SemaphoreType.DMA((src_count,)),
            pltpu.SemaphoreType.DMA((2 * src_count,)),
            pltpu.SemaphoreType.DMA((2 * src_count,)),
            pltpu.SemaphoreType.DMA((2,)),
            pltpu.SemaphoreType.DMA((2,)),
            pltpu.SemaphoreType.DMA((7,)),
        ],
        compiler_params=pltpu.CompilerParams(collective_id=0, has_side_effects=True),
    )(source, target, *ints)
    return write_out(*reads)


def solution(mesh):
    placed = (
        P(("src", "tgt"), None),
        P(("src", "tgt"), None),
        P(("src", "tgt")),
        P(("src", "tgt")),
        P(("src", "tgt")),
        P(("src", "tgt")),
    )
    return jax.shard_map(
        on_device,
        mesh=mesh,
        in_specs=placed,
        out_specs=(P(("src", "tgt"), None), P(("src", "tgt"), None)),
        check_vma=False,
    )
```
